32 devices in a mesh: dp: 16 (over z, x, core), tp: 2 (over y).
Axes of the slice: x: 2, y: 2, z: 4, core: 2. Of those that a mesh axis runs over, the one named last changes fastest.
Arguments:
- layer_in: bfloat16 [16384, 768], P(('dp', 'tp')), may hold values from -6 to 6
- lengths: int32 [128, 17], P('dp'), may hold values from 0 to 77, as said below
- attn_gain: float32 [768], replicated, may hold values from 0.25 to 1.75
- attn_shift: float32 [768], replicated, may hold values from -2 to 2
- qkv_weight: bfloat16 [768, 3, 768], P(None, None, 'tp'), may hold values from -0.21875 to 0.21875
- qv_bias: float32 [2, 768], P(None, 'tp'), may hold values from -3 to 3
- out_weight: bfloat16 [768, 768], P('tp'), may hold values from -0.875 to 0.875
- out_bias: float32 [768], replicated, may hold values from -2 to 2
- mlp_gain: float32 [768], replicated, may hold values from 0.25 to 1.75
- mlp_shift: float32 [768], replicated, may hold values from -2 to 2
- up_weight: bfloat16 [768, 3072], P(None, 'tp'), may hold values from -0.21875 to 0.21875
- up_bias: float32 [3072], P('tp'), may hold values from -3 to 3
- down_weight: bfloat16 [3072, 768], P('tp'), may hold values from -0.15625 to 0.15625
- down_bias: float32 [768], replicated, may hold values from -2 to 2
- cotangent: bfloat16 [16384, 768], P(('dp', 'tp')), may hold values from -6 to 6
Outputs:
- layer_out: bfloat16 [16384, 768], P(('dp', 'tp'))
- in_grad: bfloat16 [16384, 768], P(('dp', 'tp'))
- attn_gain_grad: float32 [768], replicated
- attn_shift_grad: float32 [768], replicated
- qkv_weight_grad: float32 [768, 3, 768], P(None, None, 'tp')
- qv_bias_grad: float32 [2, 768], P(None, 'tp')
- out_weight_grad: float32 [768, 768], P('tp')
- out_bias_grad: float32 [768], replicated
- mlp_gain_grad: float32 [768], replicated
- mlp_shift_grad: float32 [768], replicated
- up_weight_grad: float32 [768, 3072], P(None, 'tp')
- up_bias_grad: float32 [3072], P('tp')
- down_weight_grad: float32 [3072, 768], P('tp')
- down_bias_grad: float32 [768], replicated
The draws below stay inside these ranges and needn't reach their ends.
Inputs may be any that keep to these rules, and one draw needn't show every extreme that they name: Row r's captions take lengths[r, 0], lengths[r, 1], ... tokens in order from slot 0; each entry is 0 or between 8 and 77; after a 0 all entries of the row are 0; a row's entries sum to at most 128, and its slots from that sum on are padding.
All inputs are finite; a program needn't handle non-finite values.
Results may differ from the reference program's by a relative error of at most 0.017.
Values may be sent and summed in bfloat16 or wider, within the bound.
No kernel may reach another device: no remote copies, remote signals or barrier semaphores. Data moves between devices by JAX's collectives and lax.ppermute only.
A program may use at most 128 MiB of HBM per device.

```python
import math
import jax
import jax.numpy as jnp
from jax import lax

D = 768
HEADS = 12
HEAD = 64
FF = 3072
SEQ = 128
SEG_MIN = 8
SEG_MAX = 77
MAXSEG = 17
ROWS = 128
TOKENS = 16384


def draw_lengths(key, part):
    raw_len = jax.random.randint(key, (ROWS, MAXSEG), SEG_MIN, SEG_MAX + 1, dtype=jnp.int32)
    raw_len = raw_len.at[0, 0].set(SEG_MAX)
    seg_ends = jnp.cumsum(raw_len, axis=1)
    return jnp.where(seg_ends <= SEQ, raw_len, 0).astype(jnp.int32)


def block_levels(key, extent, pieces, low, largest):
    level, own = 1.0, jax.random.fold_in(key, 6)
    for position, parts in pieces:
        steps = jnp.exp(jax.random.uniform(jax.random.fold_in(own, position), (parts,), jnp.float32, low / len(pieces), largest / len(pieces)))
        level = level * jnp.repeat(steps, extent[position] // parts).reshape([-1 if axis == position else 1 for axis in range(len(extent))])
    return level


def scatter_about(stream_key, shape, deviation, most, split=(), kind=jnp.bfloat16):
    result = jax.random.normal(stream_key, shape, jnp.float32) * deviation
    if len(split) > 0:
        result = block_levels(stream_key, shape, split, -0.22, 0.18) * result
    return jnp.clip(result, min=-most, max=most).astype(kind)


def setup_inputs(seed: int = 0) -> dict:
    arg_keys = jax.random.split(jax.random.key(seed), 16)
    return {
        "layer_in": scatter_about(arg_keys[0], (TOKENS, D), 1.0, 6.0, ((0, 32),)),
        "lengths": draw_lengths(jax.random.fold_in(arg_keys[15], 71), 0),
        "attn_gain": jnp.clip(1.0 + 0.15 * jax.random.normal(arg_keys[2], (D,), jnp.float32), 0.25, 1.75),
        "attn_shift": scatter_about(arg_keys[3], (D,), 0.3, 2.0, (), jnp.float32),
        "qkv_weight": scatter_about(arg_keys[4], (D, 3, D), D ** -0.5, 0.21875, ((2, 2),)),
        "qv_bias": scatter_about(arg_keys[5], (2, D), 0.5, 3.0, ((1, 2),), jnp.float32),
        "out_weight": scatter_about(arg_keys[6], (D, D), (D // 16) ** -0.5, 0.875, ((0, 2),)),
        "out_bias": scatter_about(arg_keys[7], (D,), 0.3, 2.0, (), jnp.float32),
        "mlp_gain": jnp.clip(1.0 + 0.15 * jax.random.normal(arg_keys[8], (D,), jnp.float32), 0.25, 1.75),
        "mlp_shift": scatter_about(arg_keys[9], (D,), 0.3, 2.0, (), jnp.float32),
        "up_weight": scatter_about(arg_keys[10], (D, FF), D ** -0.5, 0.21875, ((1, 2),)),
        "up_bias": scatter_about(arg_keys[11], (FF,), 0.5, 3.0, ((0, 2),), jnp.float32),
        "down_weight": scatter_about(arg_keys[12], (FF, D), (FF // 2) ** -0.5, 0.15625, ((0, 2),)),
        "down_bias": scatter_about(arg_keys[13], (D,), 0.3, 2.0, (), jnp.float32),
        "cotangent": scatter_about(arg_keys[14], (TOKENS, D), 1.0, 6.0, ((0, 32),)),
    }


HIGHEST = lax.Precision.HIGHEST
norm_epsilon = 1e-05

@jax.custom_vjp
def low(v):
    return lax.optimization_barrier(v.astype(jnp.bfloat16)).astype(jnp.float32)

@jax.custom_vjp
def low_back(v):
    return v

def low_keep(v):
    return (low(v), None)

def low_pass(kept, grad):
    return (grad,)

def back_keep(v):
    return (v, None)

def back_low(kept, grad):
    return (low(grad),)
low.defvjp(low_keep, low_pass)
low_back.defvjp(back_keep, back_low)

def layer_norm(values, gain, shift):
    center = values - lax.optimization_barrier(jnp.mean(values, axis=-1, keepdims=True))
    spread = lax.optimization_barrier(jnp.mean(center * center, axis=-1, keepdims=True))
    return center * lax.rsqrt(spread + norm_epsilon) * gain + shift

def segment_masks(lengths):
    seg_ends = jnp.cumsum(lengths.astype(jnp.int32), axis=1).astype(jnp.int32)
    places = jnp.arange(SEQ, dtype=jnp.int32)
    segment = lax.optimization_barrier(jnp.sum((seg_ends[:, None, :] <= places[None, :, None]).astype(jnp.int32), axis=2))
    tok_valid = places[None, :] < seg_ends[:, -1:]
    causal = places[None, :] <= places[:, None]
    self_pair = places[None, :] == places[:, None]
    same_seg = segment[:, :, None] == segment[:, None, :]
    allowed = same_seg & causal[None] & (tok_valid[:, None, :] | self_pair[None])
    return (allowed, tok_valid)

def layer(resid_in, attn_gain, attn_shift, qkv_weight, qv_bias, out_weight, out_bias, mlp_gain, mlp_shift, up_weight, up_bias, down_weight, down_bias, allowed, tok_valid):
    row_count = allowed.shape[0]
    tok_count = resid_in.shape[0]
    score_scale = 1.0 / math.sqrt(HEAD)
    normed_attn = low(layer_norm(resid_in, attn_gain, attn_shift))
    projected = jnp.einsum('td,dce->cte', normed_attn, qkv_weight, precision=HIGHEST)
    queries = low_back(low(projected[0] + qv_bias[0])).reshape(row_count, SEQ, HEADS, HEAD)
    key_rows = low_back(low(projected[1])).reshape(row_count, SEQ, HEADS, HEAD)
    value_rows = low_back(low(projected[2] + qv_bias[1])).reshape(row_count, SEQ, HEADS, HEAD)
    raw_scores = jnp.einsum('rqhd,rkhd->rhqk', queries, key_rows, precision=HIGHEST)
    scores = jnp.where(allowed[:, None], low_back(raw_scores * score_scale), -1e+30)
    attn_probs = jax.nn.softmax(scores, axis=-1)
    valid_col = tok_valid.astype(jnp.float32)[:, :, None, None]
    attended = jnp.einsum('rhqk,rkhd->rqhd', low(attn_probs), value_rows, precision=HIGHEST) * valid_col
    attended = low_back(low(attended.reshape(tok_count, D)))
    attn_sum = low_back(jnp.dot(attended, out_weight, precision=HIGHEST))
    resid_mid = resid_in + attn_sum + out_bias
    normed_mlp = low(layer_norm(resid_mid, mlp_gain, mlp_shift))
    pre_act = low_back(jnp.dot(normed_mlp, up_weight, precision=HIGHEST) + up_bias)
    activated = low(jax.nn.gelu(pre_act, approximate=False))
    mlp_sum = low_back(jnp.dot(activated, down_weight, precision=HIGHEST))
    return resid_mid + mlp_sum + down_bias

def reference(layer_in, lengths, attn_gain, attn_shift, qkv_weight, qv_bias, out_weight, out_bias, mlp_gain, mlp_shift, up_weight, up_bias, down_weight, down_bias, cotangent):
    block_rows = math.gcd(ROWS, 32)
    blocks = ROWS // block_rows
    inputs_f = layer_in.astype(jnp.float32).reshape(blocks, block_rows * SEQ, D)
    cot_f = cotangent.astype(jnp.float32).reshape(blocks, block_rows * SEQ, D)
    len_blocks = lengths.astype(jnp.int32).reshape(blocks, block_rows, MAXSEG)
    weights = (attn_gain.astype(jnp.float32), attn_shift.astype(jnp.float32), qkv_weight.astype(jnp.float32), qv_bias.astype(jnp.float32), out_weight.astype(jnp.float32), out_bias.astype(jnp.float32), mlp_gain.astype(jnp.float32), mlp_shift.astype(jnp.float32), up_weight.astype(jnp.float32), up_bias.astype(jnp.float32), down_weight.astype(jnp.float32), down_bias.astype(jnp.float32))

    def block_step(running, block_item):
        x_block, cot_block, len_block = block_item
        allowed, tok_valid = segment_masks(len_block)

        def forward(x_val, *params):
            return layer(x_val, *params, allowed, tok_valid)
        out_block, back_fn = jax.vjp(forward, x_block, *weights)
        block_grads = back_fn(cot_block)
        updated = tuple((left + right for left, right in zip(running, block_grads[1:])))
        return (updated, (out_block.astype(jnp.bfloat16), block_grads[0].astype(jnp.bfloat16)))
    zero_grads = tuple((jnp.zeros_like(weight_item) for weight_item in weights))
    total_grads, (out_blocks, grad_blocks) = lax.scan(block_step, zero_grads, (inputs_f, cot_f, len_blocks))
    return (out_blocks.reshape(TOKENS, D), grad_blocks.reshape(TOKENS, D), total_grads[0], total_grads[1], total_grads[2], total_grads[3], total_grads[4], total_grads[5], total_grads[6], total_grads[7], total_grads[8], total_grads[9], total_grads[10], total_grads[11])
```

```python
import math

import jax
import jax.numpy as jnp
from jax import lax
from jax.experimental import pallas as pl
from jax.experimental.pallas import tpu as pltpu
from jax.sharding import PartitionSpec as P

HEAD = 64
SEQ = 128
UNITS = 4
EPS = 1e-05
SCALE = 1.0 / math.sqrt(HEAD)
F32 = jnp.float32
BF16 = jnp.bfloat16

VM = pl.BlockSpec(memory_space=pltpu.VMEM)
SM = pl.BlockSpec(memory_space=pltpu.SMEM)
HB = pl.BlockSpec(memory_space=pl.ANY)

ORDER_A, ORDER_B = (0, 2, 1, 3), (0, 1, 2, 3)
TP_BIT, CORE_BIT, NEAR_BIT, FAR_BIT, FIRST_REST = 0, 1, 2, 3, 4


def nn(a, b):
    return lax.dot_general(a, b, (((1,), (0,)), ((), ())), preferred_element_type=F32)


def nt(a, b):
    return lax.dot_general(a, b, (((1,), (1,)), ((), ())), preferred_element_type=F32)


def tn(a, b):
    return lax.dot_general(a, b, (((0,), (0,)), ((), ())), preferred_element_type=F32)


def normalize(values):
    center = values - jnp.mean(values, axis=-1, keepdims=True)
    inv = lax.rsqrt(jnp.mean(center * center, axis=-1, keepdims=True) + EPS)
    return center * inv, inv


def norm_back(values, grad, gain):
    normed, inv = normalize(values)
    scaled = grad * gain
    mean_g = jnp.mean(scaled, axis=-1, keepdims=True)
    mean_gn = jnp.mean(scaled * normed, axis=-1, keepdims=True)
    part = inv * (scaled - mean_g - normed * mean_gn)
    gain_sum = jnp.sum(grad * normed, axis=0, keepdims=True)
    shift_sum = jnp.sum(grad, axis=0, keepdims=True)
    return part, gain_sum, shift_sum


def row_mask(lens, row):
    at_q = lax.broadcasted_iota(jnp.int32, (SEQ, 1), 0)
    at_k = lax.broadcasted_iota(jnp.int32, (1, SEQ), 1)
    total = jnp.int32(0)
    seg_q = jnp.zeros((SEQ, 1), jnp.int32)
    seg_k = jnp.zeros((1, SEQ), jnp.int32)
    for entry in range(lens.shape[1]):
        total = total + lens[row, entry]
        seg_q = seg_q + jnp.where(at_q >= total, 1, 0)
        seg_k = seg_k + jnp.where(at_k >= total, 1, 0)
    allowed = (seg_q == seg_k) & (at_k <= at_q) & ((at_k < total) | (at_k == at_q))
    valid = jnp.where(at_q < total, 1.0, 0.0).astype(F32)
    return allowed, valid


def low_lanes():
    return lax.broadcasted_iota(jnp.int32, (SEQ, 2 * HEAD), 1) < HEAD


def stack_pair(pair, low):
    zero = jnp.zeros_like(pair)
    return jnp.concatenate([jnp.where(low, pair, zero), jnp.where(low, zero, pair)], axis=0)


def pair_probs(q_stack, keys, allowed2):
    scores = jnp.where(allowed2, nt(q_stack, keys) * SCALE, -1e30)
    top = jnp.max(scores, axis=-1, keepdims=True)
    weights = jnp.exp(scores - top)
    return weights * (1.0 / jnp.sum(weights, axis=-1, keepdims=True))


def attend(lens, ids, nrm, w, bias, qkv, att):
    width = w.shape[2]
    rows = nrm.shape[0] // SEQ
    for part in range(3):
        value = nn(nrm[...], w[part])
        if part != 1:
            value = value + bias[pl.ds(part // 2, 1), :]
        qkv[:, part * width : (part + 1) * width] = value.astype(BF16)
    low = low_lanes()

    @pl.loop(0, rows)
    def _(row):
        allowed, valid = row_mask(lens, ids[0] * rows + row)
        allowed2 = jnp.concatenate([allowed, allowed], axis=0)
        at = pl.ds(pl.multiple_of(row * SEQ, SEQ), SEQ)
        for first in range(0, width, 2 * HEAD):
            q = qkv[at, first : first + 2 * HEAD]
            k = qkv[at, width + first : width + first + 2 * HEAD]
            v = qkv[at, 2 * width + first : 2 * width + first + 2 * HEAD]
            probs = pair_probs(stack_pair(q, low), k, allowed2)
            both = nn(probs.astype(BF16), v)
            out = jnp.where(low, both[:SEQ], both[SEQ:]) * valid
            att[at, first : first + 2 * HEAD] = out.astype(BF16)


def own_fwd_kernel(lens, ids, x, gain, shift, w, bias, nrm, qkv, att):
    @pl.loop(0, x.shape[0] // SEQ)
    def _(row):
        at = pl.ds(pl.multiple_of(row * SEQ, SEQ), SEQ)
        normed, _ = normalize(x[at, :].astype(F32))
        nrm[at, :] = (normed * gain[...] + shift[...]).astype(BF16)

    attend(lens, ids, nrm, w, bias, qkv, att)


def other_fwd_kernel(
    lens, ids, x, nrm, bias, att_own, wo_own, out_bias, gain, shift,
    m0, mx, mz, mda, mdb, s0, sx, sz, sda, sdb,
    w, wo, qkv, att, mid, nm, sems,
):
    core, mine = ids[1], ids[2]
    width = w.shape[2]
    part_rows = m0.shape[0] // 4
    copies = []

    def fetch(src, dst):
        copy = pltpu.make_async_copy(src, dst, sems.at[len(copies)])
        copy.start()
        copies.append(copy)

    for side, (u0, ux, uz, da, db) in ((core, (m0, mx, mz, mda, mdb)), (1 - core, (s0, sx, sz, sda, sdb))):
        def rows_of(step):
            unit = jnp.bitwise_xor(mine, step)
            at_w = pl.ds(pl.multiple_of((side * UNITS + unit) * part_rows, part_rows), part_rows)
            at_o = pl.ds(pl.multiple_of(unit * part_rows, part_rows), part_rows)
            cols = pl.ds(pl.multiple_of(side * width, width), width)
            return at_w, at_o, cols

        for step, unit_ref in ((0, u0), (1, ux), (2, uz)):
            at_w, at_o, cols = rows_of(step)
            for part in range(3):
                fetch(unit_ref.at[pl.ds(part * part_rows, part_rows)], w.at[part, at_w, :])
            fetch(unit_ref.at[pl.ds(3 * part_rows, part_rows)], wo.at[at_o, cols])
        at_w, at_o, cols = rows_of(3)
        fetch(da.at[pl.ds(0, part_rows)], w.at[0, at_w, :])
        fetch(da.at[pl.ds(part_rows, part_rows)], w.at[1, at_w, :])
        fetch(db.at[pl.ds(0, part_rows)], w.at[2, at_w, :])
        fetch(db.at[pl.ds(part_rows, part_rows)], wo.at[at_o, cols])
    for copy in copies:
        copy.wait()

    attend(lens, ids, nrm, w, bias, qkv, att)
    mid[...] = nn(att_own[...], wo_own[...]) + nn(att[...], wo[...])

    @pl.loop(0, x.shape[0] // SEQ)
    def _(row):
        at = pl.ds(pl.multiple_of(row * SEQ, SEQ), SEQ)
        value = x[at, :].astype(F32) + mid[at, :] + out_bias[...]
        mid[at, :] = value
        normed, _ = normalize(value)
        nm[at, :] = (normed * gain[...] + shift[...]).astype(BF16)


def gelu_parts(pre):
    bell = jnp.exp(-0.5 * pre * pre)
    t = 1.0 / (1.0 + (0.3275911 * math.sqrt(0.5)) * jnp.abs(pre))
    poly = 1.061405429 * t - 1.453152027
    poly = poly * t + 1.421413741
    poly = poly * t - 0.284496736
    poly = poly * t + 0.254829592
    tail = 0.5 * (poly * t) * bell
    cdf = jnp.where(pre >= 0, 1.0 - tail, tail)
    return pre * cdf, cdf + pre * bell * (1.0 / math.sqrt(2.0 * math.pi))


def mlp_kernel(own, *refs):
    ids, nm_a, nm_b, ct_a, ct_b, bias = refs[:6]
    if own:
        up_hbm, down_hbm = refs[6:8]
        out, dnm, grads_a, grads_b, bias_g = refs[8:13]
        scratch = refs[13:]
    else:
        m0, mx, mz, mda, mdb, out_prev, dnm_prev = refs[6:13]
        out_own, out_sib, dnm_own, dnm_sib, grads_a, grads_b, bias_g = refs[13:20]
        scratch = refs[20:]
    up, down, nm, ct, acc_out, acc_dnm, pre, dact, act, pg, gu, gd = scratch[:12]
    core, mine = ids[1], ids[2]
    hidden = up.shape[1]
    tokens = nm_a.shape[0]
    unit_rows = up.shape[0] // UNITS
    copies = []

    def fetch(src, dst, sem):
        copy = pltpu.make_async_copy(src, dst, sem)
        copy.start()
        copies.append(copy)

    sems = scratch[12]
    if own:
        at = pl.ds(pl.multiple_of(core * hidden, hidden), hidden)
        fetch(up_hbm.at[:, at], up, sems.at[0])
        fetch(down_hbm.at[at, :], down, sems.at[1])
    else:
        prev_out, prev_dnm = scratch[13:15]
        for step, unit in ((0, m0), (1, mx), (2, mz)):
            at = pl.ds(pl.multiple_of(jnp.bitwise_xor(mine, step) * unit_rows, unit_rows), unit_rows)
            fetch(unit.at[pl.ds(0, unit_rows)], up.at[at, :], sems.at[2 * step])
            fetch(unit.at[pl.ds(unit_rows, unit_rows)], down.at[at, :], sems.at[2 * step + 1])
        at = pl.ds(pl.multiple_of(jnp.bitwise_xor(mine, 3) * unit_rows, unit_rows), unit_rows)
        fetch(mda, up.at[at, :], sems.at[6])
        fetch(mdb, down.at[at, :], sems.at[7])
        late_out = pltpu.make_async_copy(out_prev, prev_out, sems.at[8])
        late_dnm = pltpu.make_async_copy(dnm_prev, prev_dnm, sems.at[9])
        late_out.start()
        late_dnm.start()
    nm[:tokens, :] = nm_a[...]
    nm[tokens:, :] = nm_b[...]
    ct[:tokens, :] = ct_a[...]
    ct[tokens:, :] = ct_b[...]
    for copy in copies:
        copy.wait()

    block = pre.shape[1]
    for first in range(0, hidden, block):
        cols = slice(first, first + block)
        pre[...] = nn(nm[...], up[:, cols])
        dact[...] = nt(ct[...], down[cols, :])
        piece = 32

        def elementwise(step, total):
            at = pl.ds(pl.multiple_of(step * piece, piece), piece)
            value, slope = gelu_parts(pre[at, :] + bias[:, cols])
            act[at, :] = value.astype(BF16)
            back = (dact[at, :] * slope).astype(BF16)
            pg[at, :] = back
            return total + jnp.sum(back.astype(F32), axis=0, keepdims=True)

        bias_g[:, cols] = lax.fori_loop(
            0, 2 * tokens // piece, elementwise, jnp.zeros((1, block), F32), unroll=4
        )
        gd[cols, :] = tn(act[...], ct[...]).astype(BF16)
        gu[:, cols] = tn(nm[...], pg[...]).astype(BF16)
        if first == 0:
            acc_out[...] = nn(act[...], down[cols, :])
            acc_dnm[...] = nt(pg[...], up[:, cols])
        else:
            acc_out[...] += nn(act[...], down[cols, :])
            acc_dnm[...] += nt(pg[...], up[:, cols])
    for place in range(UNITS):
        to = slice(place * unit_rows, (place + 1) * unit_rows)
        for source, target, order in ((gu, grads_a, ORDER_A), (gd, grads_b, ORDER_B)):
            unit = jnp.bitwise_xor(mine, order[place])
            target[to, :] = source[pl.ds(pl.multiple_of(unit * unit_rows, unit_rows), unit_rows), :]
    if own:
        out[...] = acc_out[...].astype(BF16)
        dnm[...] = acc_dnm[...].astype(BF16)
    else:
        late_out.wait()
        late_dnm.wait()
        out_own[...] = acc_out[:tokens, :] + prev_out[:tokens, :].astype(F32)
        out_sib[...] = (acc_out[tokens:, :] + prev_out[tokens:, :].astype(F32)).astype(BF16)
        dnm_own[...] = acc_dnm[:tokens, :] + prev_dnm[:tokens, :].astype(F32)
        dnm_sib[...] = (acc_dnm[tokens:, :] + prev_dnm[tokens:, :].astype(F32)).astype(BF16)


def attend_back(lens, ids, ml, nrm, w, wo, qkv, att, datt, dqkv, dw, dwo, send_a, send_b, keep_a, keep_b, qvb):
    core, mine = ids[1], ids[2]
    width = w.shape[2]
    rows = nrm.shape[0] // SEQ
    datt[...] = nt(ml[...], wo[...]).astype(BF16)
    dwo[...] = tn(att[...], ml[...]).astype(BF16)
    low = low_lanes()

    @pl.loop(0, rows)
    def _(row):
        allowed, valid = row_mask(lens, ids[0] * rows + row)
        allowed2 = jnp.concatenate([allowed, allowed], axis=0)
        at = pl.ds(pl.multiple_of(row * SEQ, SEQ), SEQ)
        for first in range(0, width, 2 * HEAD):
            q_cols = slice(first, first + 2 * HEAD)
            k_cols = slice(width + first, width + first + 2 * HEAD)
            v_cols = slice(2 * width + first, 2 * width + first + 2 * HEAD)
            k = qkv[at, k_cols]
            q_stack = stack_pair(qkv[at, q_cols], low)
            grad = (datt[at, q_cols].astype(F32) * valid).astype(BF16)
            g_stack = stack_pair(grad, low)
            probs = pair_probs(q_stack, k, allowed2)
            dqkv[at, v_cols] = tn(probs.astype(BF16), g_stack).astype(BF16)
            prob_grad = nt(g_stack, qkv[at, v_cols])
            inner = jnp.sum(probs * prob_grad, axis=-1, keepdims=True)
            score_grad = (probs * (prob_grad - inner)).astype(BF16)
            both = nn(score_grad, k)
            dqkv[at, q_cols] = (jnp.where(low, both[:SEQ], both[SEQ:]) * SCALE).astype(BF16)
            dqkv[at, k_cols] = (tn(score_grad, q_stack) * SCALE).astype(BF16)

    qvb[0:1, :] = jnp.sum(dqkv[:, :width].astype(F32), axis=0, keepdims=True)
    qvb[1:2, :] = jnp.sum(dqkv[:, 2 * width :].astype(F32), axis=0, keepdims=True)
    for part in range(3):
        dw[part] = tn(nrm[...], dqkv[:, part * width : (part + 1) * width]).astype(BF16)
    part_rows = keep_a.shape[0] // (2 * UNITS)
    for place in range(UNITS):
        for side, target_a, target_b in ((core, keep_a, keep_b), (1 - core, send_a, send_b)):
            def rows_of(order):
                unit = jnp.bitwise_xor(mine, order[place])
                at_w = pl.ds(pl.multiple_of((side * UNITS + unit) * part_rows, part_rows), part_rows)
                return at_w, pl.ds(pl.multiple_of(unit * part_rows, part_rows), part_rows)

            first = 2 * place * part_rows
            one, two = slice(first, first + part_rows), slice(first + part_rows, first + 2 * part_rows)
            at_w, _ = rows_of(ORDER_A)
            target_a[one, :] = dw[0, at_w, :]
            target_a[two, :] = dw[1, at_w, :]
            at_w, at_o = rows_of(ORDER_B)
            target_b[one, :] = dw[2, at_w, :]
            target_b[two, :] = dwo[at_o, pl.ds(pl.multiple_of(side * width, width), width)]


def normed_grad(dqkv, w):
    width = w.shape[2]
    total = nt(dqkv[:, :width], w[0])
    for part in range(1, 3):
        total = total + nt(dqkv[:, part * width : (part + 1) * width], w[part])
    return total


def other_back_kernel(
    lens, ids, dnm_own, dnm_sib, ct, mid, gain, w, wo, qkv, att, nrm,
    mg, dn, send_a, send_b, keep_a, keep_b, sums, qvb,
    ml, datt, dqkv, dw, dwo,
):
    sums[...] = jnp.zeros_like(sums)

    @pl.loop(0, mid.shape[0] // SEQ)
    def _(row):
        at = pl.ds(pl.multiple_of(row * SEQ, SEQ), SEQ)
        grad = dnm_own[at, :] + dnm_sib[at, :].astype(F32)
        part, gain_sum, shift_sum = norm_back(mid[at, :], grad, gain[...])
        out_grad = ct[at, :].astype(F32)
        value = out_grad + part
        mg[at, :] = value
        ml[at, :] = value.astype(BF16)
        sums[0:1, :] += gain_sum
        sums[1:2, :] += shift_sum
        sums[2:3, :] += jnp.sum(value, axis=0, keepdims=True)
        sums[3:4, :] += jnp.sum(out_grad, axis=0, keepdims=True)

    attend_back(lens, ids, ml, nrm, w, wo, qkv, att, datt, dqkv, dw, dwo, send_a, send_b, keep_a, keep_b, qvb)
    dn[...] = normed_grad(dqkv, w)


def own_back_kernel(
    lens, ids, mg, dn, x, gain, w, wo, qkv, att, nrm,
    in_grad, send_a, send_b, keep_a, keep_b, sums, qvb,
    ml, datt, dqkv, dw, dwo, dn2,
):
    ml[...] = mg[...].astype(BF16)
    attend_back(lens, ids, ml, nrm, w, wo, qkv, att, datt, dqkv, dw, dwo, send_a, send_b, keep_a, keep_b, qvb)
    dn2[...] = normed_grad(dqkv, w)
    sums[...] = jnp.zeros_like(sums)

    @pl.loop(0, x.shape[0] // SEQ)
    def _(row):
        at = pl.ds(pl.multiple_of(row * SEQ, SEQ), SEQ)
        grad = dn[at, :] + dn2[at, :]
        part, gain_sum, shift_sum = norm_back(x[at, :].astype(F32), grad, gain[...])
        in_grad[at, :] = (mg[at, :] + part).astype(BF16)
        sums[0:1, :] += gain_sum
        sums[1:2, :] += shift_sum


def place_mlp_kernel(ids, *refs):
    core, mine = ids[1], ids[2]
    up, down = refs[10:]
    for side, pieces in ((core, refs[:5]), (1 - core, refs[5:10])):
        rows, width = pieces[3].shape
        base = pl.multiple_of(side * width, width)
        for step in range(UNITS):
            first = pl.multiple_of(jnp.bitwise_xor(mine, step) * rows, rows)
            left = pieces[step][:rows, :] if step < 3 else pieces[3][...]
            right = pieces[step][rows:, :] if step < 3 else pieces[4][...]
            up[pl.ds(first, rows), pl.ds(base, width)] = left.astype(F32)
            down[pl.ds(pl.multiple_of(base + first, rows), rows), :] = right.astype(F32)


def place_attn_kernel(ids, *refs):
    core, mine = ids[1], ids[2]
    w, wo = refs[10:]
    for side, pieces in ((core, refs[:5]), (1 - core, refs[5:10])):
        rows, width = pieces[3].shape
        rows = rows // 2
        for step in range(UNITS):
            unit = jnp.bitwise_xor(mine, step)
            at_w = pl.ds(pl.multiple_of((side * UNITS + unit) * rows, rows), rows)
            at_o = pl.ds(pl.multiple_of(unit * rows, rows), rows)
            cols = pl.ds(pl.multiple_of(side * width, width), width)
            for part in range(4):
                if step < 3:
                    value = pieces[step][part * rows : (part + 1) * rows, :]
                else:
                    value = pieces[3 + part // 2][(part % 2) * rows : (part % 2 + 1) * rows, :]
                if part < 3:
                    w[part, at_w, :] = value.astype(F32)
                else:
                    wo[at_o, cols] = value.astype(F32)


def call(kernel, outs, in_specs, name, scratch=()):
    return pl.pallas_call(
        kernel,
        out_shape=tuple(jax.ShapeDtypeStruct(shape, dtype) for shape, dtype in outs),
        in_specs=in_specs,
        out_specs=tuple(VM for _ in outs),
        scratch_shapes=list(scratch),
        name=name,
        compiler_params=pltpu.CompilerParams(vmem_limit_bytes=60 * 1024 * 1024),
    )


def build(mesh):
    devices = mesh.shape["dp"] * mesh.shape["tp"]
    bits = devices.bit_length() - 1

    def swap(value, bit):
        pairs = [(i, i ^ (1 << bit)) for i in range(devices)]
        return lax.ppermute(value, ("dp", "tp"), pairs)

    def share(unit):
        rows = unit.shape[0] // 2
        near = swap(unit, NEAR_BIT)
        far = swap(unit, FAR_BIT)
        corner_a = swap(far[:rows], NEAR_BIT)
        corner_b = swap(near[rows:], FAR_BIT)
        return unit, near, far, corner_a, corner_b

    def reduce_colour(terms, bit_one, bit_two):
        rows = terms[0].shape[0] // UNITS

        def add(first, last, *more):
            total = terms[0][first * rows : last * rows].astype(F32)
            for term in terms[1:]:
                total = total + term[first * rows : last * rows].astype(F32)
            for term in more:
                total = total + term.astype(F32)
            return total

        one = swap(add(2, 4).astype(BF16), bit_one)
        two = swap(add(1, 2, one[rows:]).astype(BF16), bit_two)
        return add(0, 1, one[:rows], two)

    def finish(unit_a, unit_b):
        mine = jnp.concatenate([unit_a, unit_b]).astype(BF16)
        for bit in range(FIRST_REST, bits):
            mine = (mine.astype(F32) + swap(mine, bit).astype(F32)).astype(BF16)
        parts = share(mine)
        return parts, [swap(part, CORE_BIT) for part in parts]

    def on_device(
        layer_in, lengths, attn_gain, attn_shift, qkv_weight, qv_bias, out_weight, out_bias,
        mlp_gain, mlp_shift, up_weight, up_bias, down_weight, down_bias, cotangent,
    ):
        tokens, wide = layer_in.shape
        width = qkv_weight.shape[2]
        hidden = up_weight.shape[1] // 2
        flat = lax.axis_index("dp") * 2 + lax.axis_index("tp")
        half = lax.axis_index("tp")
        core = (flat >> CORE_BIT) & 1
        mine = ((flat >> FAR_BIT) & 1) * 2 + ((flat >> NEAR_BIT) & 1)
        ids = jnp.stack([half, core, mine]).astype(jnp.int32)
        row = lambda v: v.reshape(1, -1)
        w_own = jnp.transpose(qkv_weight, (1, 0, 2))

        part_rows = wide // (2 * UNITS)
        attn_unit = jnp.concatenate(
            [
                lax.dynamic_slice(
                    w_own, (0, (core * UNITS + mine) * part_rows, 0), (3, part_rows, width)
                ).reshape(3 * part_rows, width),
                lax.dynamic_slice(out_weight, (mine * part_rows, core * width), (part_rows, width)),
            ]
        )
        small = jnp.concatenate([qv_bias.reshape(-1), up_bias])
        small_other = swap(small.reshape(-1, 128), TP_BIT).reshape(-1)
        attn_parts = share(swap(attn_unit, TP_BIT))
        attn_sib = [swap(part, CORE_BIT) for part in attn_parts]
        unit_rows = hidden // UNITS
        mlp_unit = jnp.concatenate(
            [
                lax.dynamic_slice(up_weight, (mine * unit_rows, core * hidden), (unit_rows, hidden)),
                lax.dynamic_slice(down_weight, (core * hidden + mine * unit_rows, 0), (unit_rows, wide)),
            ]
        )
        mlp_parts = share(swap(mlp_unit, TP_BIT))
        ct_sib = swap(cotangent, CORE_BIT)
        bias_other = small_other[: 2 * width].reshape(2, width)
        up_bias_own = lax.dynamic_slice(up_bias, (core * hidden,), (hidden,))
        up_bias_other = lax.dynamic_slice(small_other, (2 * width + core * hidden,), (hidden,))

        acts = (tokens, 3 * width)
        nrm, qkv_own, att_own = call(
            own_fwd_kernel,
            [((tokens, wide), BF16), (acts, BF16), ((tokens, width), BF16)],
            [SM, SM] + [VM] * 5,
            "attn_own_fwd",
        )(lengths, ids, layer_in, row(attn_gain), row(attn_shift), w_own, qv_bias)
        w_other, wo_other, qkv_other, att_other, mid, nm = call(
            other_fwd_kernel,
            [
                ((3, wide, width), BF16), ((width, wide), BF16), (acts, BF16),
                ((tokens, width), BF16), ((tokens, wide), F32), ((tokens, wide), BF16),
            ],
            [SM, SM] + [VM] * 8 + [HB] * 10,
            "attn_other_fwd",
            [pltpu.SemaphoreType.DMA((32,))],
        )(
            lengths, ids, layer_in, nrm, bias_other, att_own, out_weight, row(out_bias),
            row(mlp_gain), row(mlp_shift), *attn_parts, *attn_sib,
        )

        nm_sib = swap(nm, CORE_BIT)
        block = 256
        scratch = [
            pltpu.VMEM((wide, hidden), BF16), pltpu.VMEM((hidden, wide), BF16),
            pltpu.VMEM((2 * tokens, wide), BF16), pltpu.VMEM((2 * tokens, wide), BF16),
            pltpu.VMEM((2 * tokens, wide), F32), pltpu.VMEM((2 * tokens, wide), F32),
            pltpu.VMEM((2 * tokens, block), F32), pltpu.VMEM((2 * tokens, block), F32),
            pltpu.VMEM((2 * tokens, block), BF16), pltpu.VMEM((2 * tokens, block), BF16),
            pltpu.VMEM((wide, hidden), BF16), pltpu.VMEM((hidden, wide), BF16),
            pltpu.SemaphoreType.DMA((10,)),
        ]
        both = (2 * tokens, wide)
        units = (UNITS * unit_rows, hidden)
        out_a, dnm_a, g_own_a, g_own_b, ub_own = call(
            lambda *r: mlp_kernel(True, *r),
            [(both, BF16), (both, BF16), (units, BF16), (units, BF16), ((1, hidden), F32)],
            [SM] + [VM] * 5 + [HB] * 2,
            "mlp_own",
            scratch,
        )(ids, nm, nm_sib, cotangent, ct_sib, row(up_bias_own), up_weight, down_weight)
        one = (tokens, wide)
        out_own, out_sib, dnm_own, dnm_sib, g_other_a, g_other_b, ub_other = call(
            lambda *r: mlp_kernel(False, *r),
            [
                (one, F32), (one, BF16), (one, F32), (one, BF16), (units, BF16), (units, BF16), ((1, hidden), F32),
            ],
            [SM] + [VM] * 5 + [HB] * 7,
            "mlp_other",
            scratch + [pltpu.VMEM(both, BF16), pltpu.VMEM(both, BF16)],
        )(ids, nm, nm_sib, cotangent, ct_sib, row(up_bias_other), *mlp_parts, out_a, dnm_a)
        dnm_got = swap(dnm_sib, CORE_BIT)
        out_got = swap(out_sib, CORE_BIT)
        layer_out = (mid + out_own + out_got.astype(F32) + down_bias).astype(BF16)

        grad_units = (UNITS * 2 * part_rows, width)
        back_scratch = [
            pltpu.VMEM((tokens, wide), BF16), pltpu.VMEM((tokens, width), BF16), pltpu.VMEM(acts, BF16),
            pltpu.VMEM((3, wide, width), BF16), pltpu.VMEM((width, wide), BF16),
        ]
        mg, dn, send_other_a, send_other_b, keep_other_a, keep_other_b, sums_mid, qvb_other = call(
            other_back_kernel,
            [
                (one, F32), (one, F32), *[(grad_units, BF16)] * 4, ((8, wide), F32), ((2, width), F32),
            ],
            [SM, SM] + [VM] * 10,
            "attn_other_back",
            back_scratch,
        )(
            lengths, ids, dnm_own, dnm_got, cotangent, mid, row(mlp_gain), w_other, wo_other,
            qkv_other, att_other, nrm,
        )
        in_grad, send_own_a, send_own_b, keep_own_a, keep_own_b, sums_in, qvb_own = call(
            own_back_kernel,
            [(one, BF16), *[(grad_units, BF16)] * 4, ((8, wide), F32), ((2, width), F32)],
            [SM, SM] + [VM] * 9,
            "attn_own_back",
            back_scratch + [pltpu.VMEM(one, F32)],
        )(lengths, ids, mg, dn, layer_in, row(attn_gain), w_own, out_weight, qkv_own, att_own, nrm)

        g_mlp, g_mlp_sib = finish(
            reduce_colour([g_own_a, swap(g_other_a, TP_BIT)], NEAR_BIT, FAR_BIT),
            reduce_colour([g_own_b, swap(g_other_b, TP_BIT)], FAR_BIT, NEAR_BIT),
        )
        up_grad, down_grad = call(
            place_mlp_kernel,
            [((wide, 2 * hidden), F32), ((2 * hidden, wide), F32)],
            [SM] + [VM] * 10,
            "place_mlp",
        )(ids, *g_mlp, *g_mlp_sib)

        def attn_terms(keep_own, send_own, keep_other, send_other):
            to_other = (keep_other.astype(F32) + swap(send_other, CORE_BIT).astype(F32)).astype(BF16)
            return [keep_own, swap(send_own, CORE_BIT), swap(to_other, TP_BIT)]

        g_attn, g_attn_sib = finish(
            reduce_colour(attn_terms(keep_own_a, send_own_a, keep_other_a, send_other_a), NEAR_BIT, FAR_BIT),
            reduce_colour(attn_terms(keep_own_b, send_own_b, keep_other_b, send_other_b), FAR_BIT, NEAR_BIT),
        )
        qkv_grad, out_grad = call(
            place_attn_kernel,
            [((3, wide, width), F32), ((width, wide), F32)],
            [SM] + [VM] * 10,
            "place_attn",
        )(ids, *g_attn, *g_attn_sib)

        halves = lambda own, other: jnp.stack(
            [jnp.where(half == 0, own, other), jnp.where(half == 0, other, own)]
        )
        qvb = jnp.transpose(halves(qvb_own, qvb_other), (1, 0, 2))
        ub = halves(ub_own, ub_other)
        ub = jnp.where((jnp.arange(2) == core)[None, :, None], ub, 0.0)
        vec = jnp.concatenate([sums_in[:2].reshape(-1), sums_mid[:4].reshape(-1), qvb.reshape(-1), ub.reshape(-1)])
        vec = vec.reshape(-1, 128)
        for bit in range(bits):
            vec = vec + swap(vec, bit)
        vec = vec.reshape(-1)
        one_of = lambda i: vec[i * wide : (i + 1) * wide]
        qvb = lax.dynamic_slice(vec[6 * wide : 8 * wide].reshape(2, 2, width), (0, half, 0), (2, 1, width))
        ub = lax.dynamic_slice(vec[8 * wide :], (half * 2 * hidden,), (2 * hidden,))
        return (
            layer_out, in_grad, one_of(0), one_of(1), jnp.transpose(qkv_grad, (1, 0, 2)), qvb.reshape(2, width),
            out_grad, one_of(4), one_of(2), one_of(3), up_grad, ub, down_grad, one_of(5),
        )

    return on_device


def solution(mesh):
    tokens, vector = P(("dp", "tp"), None), P()
    in_specs = (
        tokens, P("dp", None), vector, vector, P(None, None, "tp"), P(None, "tp"), P("tp", None), vector,
        vector, vector, P(None, "tp"), P("tp"), P("tp", None), vector, tokens,
    )
    out_specs = (
        tokens, tokens, vector, vector, P(None, None, "tp"), P(None, "tp"), P("tp", None), vector,
        vector, vector, P(None, "tp"), P("tp"), P("tp", None), vector,
    )
    return jax.shard_map(build(mesh), mesh=mesh, in_specs=in_specs, out_specs=out_specs, check_vma=False)
```

```python
import math

import jax
import jax.numpy as jnp
from jax import lax
from jax.experimental import pallas as pl
from jax.experimental.pallas import tpu as pltpu
from jax.sharding import PartitionSpec as P

HEAD = 64
SEQ = 128
UNITS = 4
EPS = 1e-05
SCALE = 1.0 / math.sqrt(HEAD)
F32 = jnp.float32
BF16 = jnp.bfloat16

VM = pl.BlockSpec(memory_space=pltpu.VMEM)
SM = pl.BlockSpec(memory_space=pltpu.SMEM)
HB = pl.BlockSpec(memory_space=pl.ANY)

NEAR_FIRST, FAR_FIRST = (0, 2, 1, 3), (0, 1, 2, 3)
TP_BIT, CORE_BIT, NEAR_BIT, FAR_BIT, FIRST_REST = 0, 1, 2, 3, 4
TP, CORE, NEAR, FAR = (1 << bit for bit in (TP_BIT, CORE_BIT, NEAR_BIT, FAR_BIT))


def nn(a, b):
    return lax.dot_general(a, b, (((1,), (0,)), ((), ())), preferred_element_type=F32)


def nt(a, b):
    return lax.dot_general(a, b, (((1,), (1,)), ((), ())), preferred_element_type=F32)


def tn(a, b):
    return lax.dot_general(a, b, (((0,), (0,)), ((), ())), preferred_element_type=F32)


def normalize(values):
    center = values - jnp.mean(values, axis=-1, keepdims=True)
    inv = lax.rsqrt(jnp.mean(center * center, axis=-1, keepdims=True) + EPS)
    return center * inv, inv


def norm_back(values, grad, gain):
    normed, inv = normalize(values)
    scaled = grad * gain
    mean_g = jnp.mean(scaled, axis=-1, keepdims=True)
    mean_gn = jnp.mean(scaled * normed, axis=-1, keepdims=True)
    part = inv * (scaled - mean_g - normed * mean_gn)
    gain_sum = jnp.sum(grad * normed, axis=0, keepdims=True)
    shift_sum = jnp.sum(grad, axis=0, keepdims=True)
    return part, gain_sum, shift_sum


def row_mask(lens, row):
    at_k = lax.broadcasted_iota(jnp.int32, (SEQ, 1), 0)
    at_q = lax.broadcasted_iota(jnp.int32, (1, SEQ), 1)
    total = jnp.int32(0)
    seg_q = jnp.zeros((1, SEQ), jnp.int32)
    seg_k = jnp.zeros((SEQ, 1), jnp.int32)
    for entry in range(lens.shape[1]):
        total = total + lens[row, entry]
        seg_q = seg_q + jnp.where(at_q >= total, 1, 0)
        seg_k = seg_k + jnp.where(at_k >= total, 1, 0)
    allowed = (seg_q == seg_k) & (at_k <= at_q) & ((at_k < total) | (at_k == at_q))
    valid = jnp.where(at_k < total, 1.0, 0.0).astype(F32)
    return jnp.concatenate([allowed, allowed], axis=1), valid


def low_lanes():
    return lax.broadcasted_iota(jnp.int32, (SEQ, 2 * HEAD), 1) < HEAD


def stack_pair(pair, low):
    zero = jnp.zeros_like(pair)
    return jnp.concatenate([jnp.where(low, pair, zero), jnp.where(low, zero, pair)], axis=0)


def pair_probs(q_stack, keys, allowed2):
    scores = jnp.where(allowed2, nt(keys, q_stack) * SCALE, -1e30)
    weights = jnp.exp(scores - jnp.max(scores, axis=0, keepdims=True))
    return weights * (1.0 / jnp.sum(weights, axis=0, keepdims=True))


class Copies:
    def __init__(self, sems):
        self.sems = sems
        self.count = 0

    def start(self, src, dst):
        made = pltpu.make_async_copy(src, dst, self.sems.at[self.count])
        self.count += 1
        made.start()
        return made


def wait(*copies):
    for made in copies:
        made.wait()


def blocks(count, size=SEQ):
    return [slice(i * size, (i + 1) * size) for i in range(count)]


def project(nrm, w, bias, qkv):
    width = w.shape[2]
    for part in range(3):
        value = nn(nrm[...], w[part])
        if part != 1:
            value = value + bias[pl.ds(part // 2, 1), :]
        qkv[:, part * width : (part + 1) * width] = value.astype(BF16)


def attend(lens, ids, qkv, att):
    width = att.shape[1]
    rows = att.shape[0] // SEQ
    low = low_lanes()
    for row, at in enumerate(blocks(rows)):
        allowed2, valid = row_mask(lens, ids[0] * rows + row)
        for first in range(0, width, 2 * HEAD):
            q = qkv[at, first : first + 2 * HEAD]
            k = qkv[at, width + first : width + first + 2 * HEAD]
            v = qkv[at, 2 * width + first : 2 * width + first + 2 * HEAD]
            probs = pair_probs(stack_pair(q, low), k, allowed2)
            both = tn(probs.astype(BF16), v)
            out = jnp.where(low, both[:SEQ], both[SEQ:]) * valid
            att[at, first : first + 2 * HEAD] = out.astype(BF16)


def own_fwd_kernel(lens, ids, x_hbm, vecs, w_hbm, bias, nrm_hbm, qkv_hbm, att, x, w, nrm, qkv, sems):
    copies = Copies(sems)
    x_in = copies.start(x_hbm, x)
    w_in = copies.start(w_hbm, w)
    wait(x_in)
    for at in blocks(x.shape[0] // SEQ):
        normed, _ = normalize(x[at, :].astype(F32))
        nrm[at, :] = (normed * vecs[0:1, :] + vecs[1:2, :]).astype(BF16)
    nrm_out = copies.start(nrm, nrm_hbm)
    wait(w_in)
    project(nrm, w, bias, qkv)
    qkv_out = copies.start(qkv, qkv_hbm)
    attend(lens, ids, qkv, att)
    wait(nrm_out, qkv_out)


def unit_block(part, rows, width, first=0):
    return pl.ds(first + (part // 2) * rows, rows), pl.ds((part % 2) * width, width)


def fetch_weights(copies, ids, mine_parts, sib_parts, w, wo):
    core, mine = ids[1], ids[2]
    width = w.shape[2]
    part_rows = w.shape[1] // (2 * UNITS)
    to_w, to_wo = [], []
    for side, parts in ((core, mine_parts), (1 - core, sib_parts)):
        for step, unit_ref in enumerate(parts):
            unit = jnp.bitwise_xor(mine, step)
            at_w = pl.ds(pl.multiple_of((side * UNITS + unit) * part_rows, part_rows), part_rows)
            at_o = pl.ds(pl.multiple_of(unit * part_rows, part_rows), part_rows)
            cols = pl.ds(pl.multiple_of(side * width, width), width)
            for part in range(3):
                to_w.append(copies.start(unit_ref.at[unit_block(part, part_rows, width)], w.at[part, at_w, :]))
            if wo is not None:
                to_wo.append(copies.start(unit_ref.at[unit_block(3, part_rows, width)], wo.at[at_o, cols]))
    return to_w, to_wo


def fetch_output_weight(copies, ids, mine_parts, sib_parts, wo):
    core, mine = ids[1], ids[2]
    width = wo.shape[0]
    part_rows = width // UNITS
    made = []
    for side, parts in ((core, mine_parts), (1 - core, sib_parts)):
        for step, unit_ref in enumerate(parts):
            at_o = pl.ds(pl.multiple_of(jnp.bitwise_xor(mine, step) * part_rows, part_rows), part_rows)
            cols = pl.ds(pl.multiple_of(side * width, width), width)
            made.append(copies.start(unit_ref.at[unit_block(3, part_rows, width)], wo.at[at_o, cols]))
    return made


def other_fwd_kernel(lens, ids, x_hbm, nrm_hbm, bias, att_own_hbm, wo_own_hbm, vecs, *refs):
    mine_parts, sib_parts = refs[:4], refs[4:8]
    qkv_hbm, att_hbm, mid_hbm, nm = refs[8:12]
    x, nrm, att_own, wo_own, w, wo, qkv, att, mid, sems = refs[12:]
    copies = Copies(sems)
    nrm_in = copies.start(nrm_hbm, nrm)
    to_w, to_wo = fetch_weights(copies, ids, mine_parts, sib_parts, w, wo)
    late = [copies.start(x_hbm, x), copies.start(att_own_hbm, att_own), copies.start(wo_own_hbm, wo_own)]
    wait(nrm_in, *to_w)
    project(nrm, w, bias, qkv)
    qkv_out = copies.start(qkv, qkv_hbm)
    attend(lens, ids, qkv, att)
    att_out = copies.start(att, att_hbm)
    wait(*to_wo, *late)
    mid[...] = nn(att_own[...], wo_own[...]) + nn(att[...], wo[...])
    for at in blocks(x.shape[0] // SEQ):
        value = x[at, :].astype(F32) + mid[at, :] + vecs[2:3, :]
        mid[at, :] = value
        normed, _ = normalize(value)
        nm[at, :] = (normed * vecs[3:4, :] + vecs[4:5, :]).astype(BF16)
    mid_out = copies.start(mid, mid_hbm)
    wait(qkv_out, att_out, mid_out)


def gelu_parts(pre):
    bell = jnp.exp(-0.5 * pre * pre)
    t = 1.0 / (1.0 + (0.3275911 * math.sqrt(0.5)) * jnp.abs(pre))
    poly = 1.061405429 * t - 1.453152027
    poly = poly * t + 1.421413741
    poly = poly * t - 0.284496736
    poly = poly * t + 0.254829592
    tail = 0.5 * (poly * t) * bell
    cdf = jnp.where(pre >= 0, 1.0 - tail, tail)
    return pre * cdf, cdf + pre * bell * (1.0 / math.sqrt(2.0 * math.pi))


def mlp_kernel(own, *refs):
    ids, nm_a, nm_b, ct_a, ct_b, bias = refs[:6]
    if own:
        up_hbm, down_hbm = refs[6:8]
        out, dnm, keep_a, send_a, keep_b, send_b, bias_g = refs[8:15]
        scratch = refs[15:]
    else:
        units, (out_prev, dnm_prev) = refs[6:10], refs[10:12]
        out_own, out_sib, dnm_own, dnm_sib, keep_a, send_a, keep_b, send_b, bias_g = refs[12:21]
        scratch = refs[21:]
    up, down, nm, ct, pre, dact, act, pg, gu, gd, sems = scratch[:11]
    core, mine = ids[1], ids[2]
    hidden = up.shape[1]
    tokens = nm_a.shape[0]
    unit_rows = up.shape[0] // UNITS
    copies = Copies(sems)
    copy = copies.start

    def unit_at(step):
        start = jnp.bitwise_xor(mine, step) * unit_rows
        return pl.ds(pl.multiple_of(start, unit_rows), unit_rows)

    if own:
        at = pl.ds(pl.multiple_of(core * hidden, hidden), hidden)
        ups = [copy(up_hbm.at[:, at], up)]
    else:
        ups = [copy(unit.at[pl.ds(0, unit_rows)], up.at[unit_at(i), :]) for i, unit in enumerate(units)]
    ups += [copy(nm_a, nm.at[pl.ds(0, tokens)]), copy(nm_b, nm.at[pl.ds(tokens, tokens)])]
    if own:
        downs = [copy(down_hbm.at[at, :], down)]
    else:
        downs = [
            copy(unit.at[pl.ds(unit_rows, unit_rows)], down.at[unit_at(i), :])
            for i, unit in enumerate(units)
        ]
    downs += [copy(ct_a, ct.at[pl.ds(0, tokens)]), copy(ct_b, ct.at[pl.ds(tokens, tokens)])]
    if not own:
        prev_out, prev_dnm = scratch[11:13]
        lates = [copy(out_prev, prev_out), copy(dnm_prev, prev_dnm)]

    block = pre.shape[1]
    piece = 32
    wait(*ups)
    for first in range(0, hidden, block):
        cols = slice(first, first + block)
        pre[...] = nn(nm[...], up[:, cols])
        if first == 0:
            wait(*downs)
        dact[...] = nt(ct[...], down[cols, :])

        def elementwise(step, total):
            at = pl.ds(pl.multiple_of(step * piece, piece), piece)
            value, slope = gelu_parts(pre[at, :] + bias[:, cols])
            act[at, cols] = value.astype(BF16)
            back = (dact[at, :] * slope).astype(BF16)
            pg[at, cols] = back
            return total + jnp.sum(back.astype(F32), axis=0, keepdims=True)

        bias_g[:, cols] = lax.fori_loop(
            0, 2 * tokens // piece, elementwise, jnp.zeros((1, block), F32), unroll=4
        )
    writes = []
    for source, grad, order, targets in (
        (gd, lambda: tn(act[...], ct[...]), FAR_FIRST, (keep_b, send_b)),
        (gu, lambda: tn(nm[...], pg[...]), NEAR_FIRST, (keep_a, send_a)),
    ):
        source[...] = grad().astype(BF16)
        for place, step in enumerate(order):
            to = targets[place // 2].at[pl.ds((place % 2) * unit_rows, unit_rows)]
            writes.append(copy(source.at[unit_at(step), :], to))
    if own:
        dnm[...] = nt(pg[...], up[...]).astype(BF16)
        out[...] = nn(act[...], down[...]).astype(BF16)
    else:
        wait(*lates)
        total = nt(pg[...], up[...])
        dnm_own[...] = total[:tokens] + prev_dnm[:tokens, :].astype(F32)
        dnm_sib[...] = (total[tokens:] + prev_dnm[tokens:, :].astype(F32)).astype(BF16)
        total = nn(act[...], down[...])
        out_own[...] = total[:tokens] + prev_out[:tokens, :].astype(F32)
        out_sib[...] = (total[tokens:] + prev_out[tokens:, :].astype(F32)).astype(BF16)
    wait(*writes)


def attend_back(lens, ids, qkv, datt, dqkv):
    width = datt.shape[1]
    rows = datt.shape[0] // SEQ
    low = low_lanes()

    @pl.loop(0, rows, unroll=2)
    def _(row):
        allowed2, valid = row_mask(lens, ids[0] * rows + row)
        at = pl.ds(pl.multiple_of(row * SEQ, SEQ), SEQ)
        for first in range(0, width, 2 * HEAD):
            q_cols = slice(first, first + 2 * HEAD)
            k_cols = slice(width + first, width + first + 2 * HEAD)
            v_cols = slice(2 * width + first, 2 * width + first + 2 * HEAD)
            k = qkv[at, k_cols]
            q_stack = stack_pair(qkv[at, q_cols], low)
            grad = (datt[at, q_cols].astype(F32) * valid).astype(BF16)
            g_stack = stack_pair(grad, low)
            probs = pair_probs(q_stack, k, allowed2)
            dqkv[at, v_cols] = nn(probs.astype(BF16), g_stack).astype(BF16)
            prob_grad = nt(qkv[at, v_cols], g_stack)
            inner = jnp.sum(probs * prob_grad, axis=0, keepdims=True)
            score_grad = (probs * (prob_grad - inner)).astype(BF16)
            both = tn(score_grad, k)
            dqkv[at, q_cols] = (jnp.where(low, both[:SEQ], both[SEQ:]) * SCALE).astype(BF16)
            dqkv[at, k_cols] = (nn(score_grad, q_stack) * SCALE).astype(BF16)


def weight_grads(copies, ids, nrm, dqkv, dw, dwo, order, keep, send):
    core, mine = ids[1], ids[2]
    width = dw.shape[2]
    part_rows = dw.shape[1] // (2 * UNITS)
    made = []
    for part in (3, 2, 1, 0):
        if part < 3:
            dw[part] = tn(nrm[...], dqkv[:, part * width : (part + 1) * width]).astype(BF16)
        for place in range(UNITS):
            unit = jnp.bitwise_xor(mine, order[place])
            for side, target in ((1 - core, send), (core, keep)):
                at_w = pl.ds(pl.multiple_of((side * UNITS + unit) * part_rows, part_rows), part_rows)
                at_o = pl.ds(pl.multiple_of(unit * part_rows, part_rows), part_rows)
                cols = pl.ds(pl.multiple_of(side * width, width), width)
                source = dw.at[part, at_w, :] if part < 3 else dwo.at[at_o, cols]
                made.append(copies.start(source, target.at[unit_block(part, part_rows, width, 2 * place * part_rows)]))
    return made


def bias_sums(dqkv):
    width = dqkv.shape[1] // 3
    return [
        jnp.sum(dqkv[:, first : first + width].astype(F32), axis=0, keepdims=True) for first in (0, 2 * width)
    ]


def normed_grad(dqkv, w):
    width = w.shape[2]
    total = nt(dqkv[:, :width], w[0])
    for part in range(1, 3):
        total = total + nt(dqkv[:, part * width : (part + 1) * width], w[part])
    return total


def other_back_kernel(lens, ids, dnm_own_hbm, dnm_sib_hbm, ct_hbm, mid_hbm, vecs, qkv_hbm, att_hbm, nrm_hbm, *refs):
    mine_parts, sib_parts = refs[:4], refs[4:8]
    mg_hbm, dqkv_hbm, keep, send, sums = refs[8:13]
    dnm_own, dnm_sib, ct, mid, qkv, att, nrm, wo, mg, ml, datt, dqkv, dw, dwo, sems = refs[13:]
    copies = Copies(sems)
    first_in = [
        copies.start(dnm_own_hbm, dnm_own), copies.start(dnm_sib_hbm, dnm_sib),
        copies.start(ct_hbm, ct), copies.start(mid_hbm, mid),
    ]
    to_wo = fetch_output_weight(copies, ids, mine_parts, sib_parts, wo)
    qkv_in, att_in, nrm_in = copies.start(qkv_hbm, qkv), copies.start(att_hbm, att), copies.start(nrm_hbm, nrm)
    wait(*first_in)
    totals = [jnp.zeros((1, mid.shape[1]), F32)] * 4
    for at in blocks(mid.shape[0] // SEQ):
        grad = dnm_own[at, :] + dnm_sib[at, :].astype(F32)
        part, gain_sum, shift_sum = norm_back(mid[at, :], grad, vecs[3:4, :])
        out_grad = ct[at, :].astype(F32)
        value = out_grad + part
        mg[at, :] = value
        ml[at, :] = value.astype(BF16)
        adds = (gain_sum, shift_sum, jnp.sum(value, axis=0, keepdims=True), jnp.sum(out_grad, axis=0, keepdims=True))
        totals = [total + add for total, add in zip(totals, adds)]
    sums[...] = jnp.concatenate(totals + [jnp.zeros((4, mid.shape[1]), F32)])
    mg_out = copies.start(mg, mg_hbm)
    wait(*to_wo, qkv_in, att_in)
    datt[...] = nt(ml[...], wo[...]).astype(BF16)
    dwo[...] = tn(att[...], ml[...]).astype(BF16)
    attend_back(lens, ids, qkv, datt, dqkv)
    wait(nrm_in)
    dqkv_out = copies.start(dqkv, dqkv_hbm)
    outs = weight_grads(copies, ids, nrm, dqkv, dw, dwo, NEAR_FIRST, keep, send)
    wait(mg_out, dqkv_out, *outs)


def own_back_kernel(
    lens, ids, mg_hbm, wo_hbm, qkv_hbm, att_hbm, nrm_hbm, dqkv_hbm, keep, send,
    mg, wo, qkv, att, nrm, ml, datt, dqkv, dw, dwo, sems,
):
    copies = Copies(sems)
    mg_in, wo_in = copies.start(mg_hbm, mg), copies.start(wo_hbm, wo)
    att_in, qkv_in, nrm_in = copies.start(att_hbm, att), copies.start(qkv_hbm, qkv), copies.start(nrm_hbm, nrm)
    wait(mg_in)
    ml[...] = mg[...].astype(BF16)
    wait(wo_in, att_in, qkv_in)
    datt[...] = nt(ml[...], wo[...]).astype(BF16)
    dwo[...] = tn(att[...], ml[...]).astype(BF16)
    attend_back(lens, ids, qkv, datt, dqkv)
    dqkv_out = copies.start(dqkv, dqkv_hbm)
    wait(nrm_in)
    outs = weight_grads(copies, ids, nrm, dqkv, dw, dwo, NEAR_FIRST, keep, send)
    wait(dqkv_out, *outs)


def input_grad_kernel(ids, dqkv_a_hbm, dqkv_b_hbm, mg_hbm, x_hbm, vecs, w_hbm, sums, ub_own, ub_other, *refs):
    mine_parts, sib_parts = refs[:4], refs[4:8]
    in_grad, vec = refs[8:10]
    dqkv_a, dqkv_b, mg, x, w_own, w_other, dn, sems = refs[10:]
    half, core = ids[0], ids[1]
    copies = Copies(sems)
    own_in = [copies.start(dqkv_a_hbm, dqkv_a), copies.start(w_hbm, w_own)]
    other_in, _ = fetch_weights(copies, ids, mine_parts, sib_parts, w_other, None)
    other_in.append(copies.start(dqkv_b_hbm, dqkv_b))
    late = [copies.start(mg_hbm, mg), copies.start(x_hbm, x)]
    width = w_own.shape[2]
    wait(*own_in)
    dn[...] = normed_grad(dqkv_a, w_own)
    wait(*other_in)
    dn[...] += normed_grad(dqkv_b, w_other)
    wait(*late)
    totals = [jnp.zeros((1, x.shape[1]), F32)] * 2
    for at in blocks(x.shape[0] // SEQ):
        part, gain_sum, shift_sum = norm_back(x[at, :].astype(F32), dn[at, :], vecs[0:1, :])
        in_grad[at, :] = (mg[at, :] + part).astype(BF16)
        totals = [totals[0] + gain_sum, totals[1] + shift_sum]
    vec[...] = jnp.zeros_like(vec)
    for i in range(2):
        vec[i : i + 1, :] = totals[i]
    vec[2:6, :] = sums[0:4, :]
    for dqkv, side in ((dqkv_a, half), (dqkv_b, 1 - half)):
        for i, value in enumerate(bias_sums(dqkv)):
            vec[6 + i : 7 + i, pl.ds(pl.multiple_of(side * width, width), width)] = value
    vec[pl.ds(8 + 2 * half + core, 1), :] = ub_own[...]
    vec[pl.ds(8 + 2 * (1 - half) + core, 1), :] = ub_other[...]


def placed_units(ids, refs):
    core, mine = ids[1], ids[2]
    for side, three, corner in ((core, refs[0], refs[1]), (1 - core, refs[2], refs[3])):
        rows = corner.shape[0]
        for step in range(UNITS):
            source, first = (three, step * rows) if step < 3 else (corner, 0)
            yield side, jnp.bitwise_xor(mine, step), source, first


def place_mlp_kernel(down_first, ids, *refs):
    out = refs[4]
    rows, width = refs[1].shape
    for side, unit, source, first in placed_units(ids, refs[:4]):
        base, start = pl.multiple_of(side * width, width), pl.multiple_of(unit * rows, rows)
        value = source[first : first + rows, :].astype(F32)
        if down_first:
            out[pl.ds(pl.multiple_of(base + start, rows), rows), :] = value
        else:
            out[pl.ds(start, rows), pl.ds(base, width)] = value


def place_attn_kernel(ids, *refs):
    w, wo = refs[4:]
    width = w.shape[2]
    rows = w.shape[1] // (2 * UNITS)
    for side, unit, source, first in placed_units(ids, refs[:4]):
        at_w = pl.ds(pl.multiple_of((side * UNITS + unit) * rows, rows), rows)
        at_o = pl.ds(pl.multiple_of(unit * rows, rows), rows)
        cols = pl.ds(pl.multiple_of(side * width, width), width)
        for part in range(4):
            value = source[unit_block(part, rows, width, first)].astype(F32)
            if part < 3:
                w[part, at_w, :] = value
            else:
                wo[at_o, cols] = value


def vmem(*buffers, sems):
    return [pltpu.VMEM(shape, dtype) for shape, dtype in buffers] + [pltpu.SemaphoreType.DMA((sems,))]


def call(kernel, outs, in_specs, name, scratch=(), out_specs=None, limit=60, gflop=1.0):
    return pl.pallas_call(
        kernel,
        out_shape=tuple(jax.ShapeDtypeStruct(shape, dtype) for shape, dtype in outs),
        in_specs=in_specs,
        out_specs=tuple(VM for _ in outs) if out_specs is None else tuple(out_specs),
        scratch_shapes=list(scratch),
        name=name,
        cost_estimate=pl.CostEstimate(flops=int(gflop * 1e9), bytes_accessed=8 << 20, transcendentals=0),
        compiler_params=pltpu.CompilerParams(vmem_limit_bytes=limit * 1024 * 1024),
    )


def build(mesh):
    devices = mesh.shape["dp"] * mesh.shape["tp"]
    bits = devices.bit_length() - 1

    def swap(value, mask):
        return lax.ppermute(value, ("dp", "tp"), [(i, i ^ mask) for i in range(devices)])

    def after(value, *deps):
        return lax.optimization_barrier((value, deps))[0]

    def share(unit):
        return [unit] + [swap(unit, mask) for mask in (NEAR, FAR, NEAR | FAR)]

    def add(*terms):
        total = terms[0].astype(F32)
        for term in terms[1:]:
            total = total + term.astype(F32)
        return total

    last = []

    def turn(*values):
        return lax.optimization_barrier((values, last[-1]))[0]

    def note(value):
        last.append(value)
        return value

    def total(parts, *terms):
        cut = lambda v, part: v if part is None else v[v.shape[0] * part[0] // 4 : v.shape[0] * part[1] // 4]
        return note(add(*[cut(term, part) for term, part in zip(turn(*terms), parts)]).astype(BF16))

    def on_device(
        layer_in, lengths, attn_gain, attn_shift, qkv_weight, qv_bias, out_weight, out_bias,
        mlp_gain, mlp_shift, up_weight, up_bias, down_weight, down_bias, cotangent,
    ):
        tokens, wide = layer_in.shape
        width = qkv_weight.shape[2]
        hidden = up_weight.shape[1] // 2
        flat = lax.axis_index("dp") * 2 + lax.axis_index("tp")
        half = lax.axis_index("tp")
        core = (flat >> CORE_BIT) & 1
        mine = ((flat >> FAR_BIT) & 1) * 2 + ((flat >> NEAR_BIT) & 1)
        ids = jnp.stack([half, core, mine]).astype(jnp.int32)
        row = lambda v: v.reshape(1, -1)
        none = jnp.zeros_like(out_bias)
        vecs = jnp.stack([attn_gain, attn_shift, out_bias, mlp_gain, mlp_shift, none, none, none])
        w_own = jnp.transpose(qkv_weight, (1, 0, 2))

        part_rows = wide // (2 * UNITS)
        unit_w = lax.dynamic_slice(w_own, (0, (core * UNITS + mine) * part_rows, 0), (3, part_rows, width))
        unit_o = lax.dynamic_slice(out_weight, (mine * part_rows, core * width), (part_rows, width))
        attn_unit = jnp.concatenate(
            [jnp.concatenate([unit_w[0], unit_w[1]], axis=1), jnp.concatenate([unit_w[2], unit_o], axis=1)]
        )
        attn_unit = swap(attn_unit, TP)

        acts = (tokens, 3 * width)
        one = (tokens, wide)
        head = (tokens, width)
        w_shape, wo_shape = (3, wide, width), (width, wide)
        nrm, qkv_own, att_own = call(
            own_fwd_kernel,
            [(one, BF16), (acts, BF16), (head, BF16)],
            [SM, SM, HB, VM, HB, VM],
            "attn_own_fwd",
            gflop=0.5,
            scratch=vmem((one, BF16), (w_shape, BF16), (one, BF16), (acts, BF16), sems=4),
            out_specs=[HB, HB, VM],
        )(lengths, ids, layer_in, vecs, w_own, qv_bias)
        attn_parts = share(after(attn_unit, att_own))
        unit_rows = hidden // UNITS
        up_late, down_late, bias_late, up_bias_late = after((up_weight, down_weight, qv_bias, up_bias), att_own)
        mlp_unit = jnp.concatenate(
            [
                lax.dynamic_slice(up_late, (mine * unit_rows, core * hidden), (unit_rows, hidden)),
                lax.dynamic_slice(down_late, (core * hidden + mine * unit_rows, 0), (unit_rows, wide)),
            ]
        )
        mlp_unit = swap(mlp_unit, TP)
        small = jnp.concatenate([bias_late.reshape(-1), up_bias_late])
        small_other = swap(small.reshape(-1, 128), TP).reshape(-1)
        ct_sib = swap(cotangent, CORE)
        bias_other = small_other[: 2 * width].reshape(2, width)
        up_bias_own = lax.dynamic_slice(up_bias, (core * hidden,), (hidden,))
        up_bias_other = lax.dynamic_slice(small_other, (2 * width + core * hidden,), (hidden,))
        attn_sib = [swap(part, CORE) for part in attn_parts]
        qkv_other, att_other, mid, nm = call(
            other_fwd_kernel,
            [(acts, BF16), (head, BF16), (one, F32), (one, BF16)],
            [SM, SM, HB, HB, VM, HB, HB, VM] + [HB] * 8,
            "attn_other_fwd",
            gflop=6,
            scratch=vmem(
                (one, BF16), (one, BF16), (head, BF16), (wo_shape, BF16), (w_shape, BF16), (wo_shape, BF16),
                (acts, BF16), (head, BF16), (one, F32), sems=40,
            ),
            out_specs=[HB, HB, HB, VM],
        )(
            lengths, ids, layer_in, after(nrm, mlp_unit), bias_other, att_own, out_weight, vecs,
            *attn_parts, *attn_sib,
        )
        mlp_near, mlp_far = swap(mlp_unit, NEAR), swap(mlp_unit, FAR)

        mlp_near, mlp_far, nm = after((mlp_near, mlp_far, nm))
        mlp_parts = [mlp_unit, mlp_near, mlp_far, swap(mlp_unit, NEAR | FAR)]
        nm_sib = swap(nm, CORE)
        block = 256
        tall = (2 * tokens, wide)
        scratch = [
            pltpu.VMEM((wide, hidden), BF16), pltpu.VMEM((hidden, wide), BF16),
            pltpu.VMEM(tall, BF16), pltpu.VMEM(tall, BF16),
            pltpu.VMEM((2 * tokens, block), F32), pltpu.VMEM((2 * tokens, block), F32),
            pltpu.VMEM((2 * tokens, hidden), BF16), pltpu.VMEM((2 * tokens, hidden), BF16),
            pltpu.VMEM((wide, hidden), BF16), pltpu.VMEM((hidden, wide), BF16),
            pltpu.SemaphoreType.DMA((24,)),
        ]
        both = (2 * tokens, wide)
        pair = (2 * unit_rows, hidden)
        out_a, dnm_a, keep_own, send_own, b_own_lo, b_own_hi, ub_own = call(
            lambda *r: mlp_kernel(True, *r),
            [(both, BF16), (both, BF16), *[(pair, BF16)] * 4, ((1, hidden), F32)],
            [SM] + [HB] * 4 + [VM] + [HB] * 2,
            "mlp_own",
            gflop=1,
            scratch=scratch,
            out_specs=[VM, VM, HB, HB, HB, HB, VM],
        )(ids, nm, nm_sib, cotangent, ct_sib, row(up_bias_own), up_weight, down_weight)
        out_own, out_sib, dnm_own, dnm_sib, keep_other, send_other, b_other_lo, b_other_hi, ub_other = call(
            lambda *r: mlp_kernel(False, *r),
            [
                (one, F32), (one, BF16), (one, F32), (one, BF16), *[(pair, BF16)] * 4,
                ((1, hidden), F32),
            ],
            [SM] + [HB] * 4 + [VM] + [HB] * 6,
            "mlp_other",
            gflop=12,
            scratch=scratch + [pltpu.VMEM(both, BF16), pltpu.VMEM(both, BF16)],
            out_specs=[VM, VM, VM, VM, HB, HB, HB, HB, VM],
        )(ids, nm, nm_sib, cotangent, ct_sib, row(up_bias_other), *mlp_parts, out_a, dnm_a)
        grad_units = (2 * UNITS * part_rows, 2 * width)
        whole, low_half, high_half, first, second = None, (0, 2), (2, 4), (0, 1), (1, 2)
        a_own = swap(send_own, NEAR)
        note(ub_other)
        a_own, dnm_sib, out_sib, send_other, b_other_hi, b_other_lo = turn(
            a_own, dnm_sib, out_sib, send_other, b_other_hi, b_other_lo
        )
        dnm_got = swap(dnm_sib, CORE)
        a_own2 = swap(total((high_half, high_half), keep_own, a_own), FAR)
        a_other = swap(send_other, NEAR)
        b_hi = swap(b_other_hi, TP)
        mg, dqkv_other, keep_o, send_o, sums_mid = call(
            other_back_kernel,
            [(one, F32), (acts, BF16), (grad_units, BF16), (grad_units, BF16), ((8, wide), F32)],
            [SM, SM, HB, HB, HB, HB, VM, HB, HB, HB] + [HB] * 8,
            "attn_other_back",
            gflop=10,
            scratch=vmem(
                (one, F32), (one, BF16), (one, BF16), (one, F32), (acts, BF16), (head, BF16), (one, BF16),
                (wo_shape, BF16), (one, F32), (one, BF16), (head, BF16), (acts, BF16),
                (w_shape, BF16), (wo_shape, BF16), sems=60,
            ),
            out_specs=[HB] * 4 + [VM],
        )(
            lengths, ids, dnm_own, dnm_got, cotangent, mid, vecs, qkv_other, att_other, nrm,
            *attn_parts, *attn_sib,
        )
        note(sums_mid)
        a_other, a_own2, b_hi, send_o = turn(a_other, a_own2, b_hi, send_o)
        o_sib = swap(send_o, CORE)
        a_other2 = swap(total((high_half, high_half), keep_other, a_other), FAR)
        b1 = swap(total((whole, whole), b_own_hi, b_hi), FAR)
        o1 = swap(total((high_half, high_half), keep_o, o_sib), NEAR)
        b_lo = swap(b_other_lo, TP)
        mg_now, = turn(mg)
        dqkv_own, keep_s, send_s = call(
            own_back_kernel,
            [(acts, BF16), (grad_units, BF16), (grad_units, BF16)],
            [SM, SM] + [HB] * 5,
            "attn_own_back",
            gflop=10,
            scratch=vmem(
                (one, F32), (wo_shape, BF16), (acts, BF16), (head, BF16), (one, BF16),
                (one, BF16), (head, BF16), (acts, BF16), (w_shape, BF16), (wo_shape, BF16), sems=48,
            ),
            out_specs=[HB] * 3,
        )(lengths, ids, mg_now, out_weight, qkv_own, att_own, nrm)
        note(dqkv_own)
        a_other2, o1, b_lo, send_s = turn(a_other2, o1, b_lo, send_s)
        s_sib = swap(send_s, CORE)
        a_back = swap(total((low_half, low_half, whole), keep_other, a_other, a_other2), TP)
        o2 = swap(total((second, second, high_half), keep_o, o_sib, o1), FAR)
        s1 = swap(total((high_half, high_half), keep_s, s_sib), NEAR)
        in_grad, vec = call(
            input_grad_kernel,
            [(one, BF16), ((16, wide), F32)],
            [SM, HB, HB, HB, HB, VM, HB, VM, VM, VM] + [HB] * 8,
            "input_grad",
            gflop=4,
            scratch=vmem(
                (acts, BF16), (acts, BF16), (one, F32), (one, BF16), (w_shape, BF16), (w_shape, BF16), (one, F32),
                sems=32,
            ),
        )(
            ids, dqkv_own, dqkv_other, *turn(mg), layer_in, vecs, w_own, sums_mid, ub_own, ub_other,
            *attn_parts, *attn_sib,
        )
        note(vec)

        def step(value, bit):
            mine, got = turn(value, swap(value, 1 << bit))
            return note(mine + got)

        def rest(unit, got):
            unit = total((whole, whole), unit, got)
            for bit in range(FIRST_REST + 1, bits):
                unit = total((whole, whole), unit, swap(unit, 1 << bit))
            return unit

        a_back, o2, b1, vec = turn(a_back, o2, b1, vec)
        a_unit = total((low_half, low_half, whole, whole), keep_own, a_own, a_own2, a_back)
        a_more = swap(a_unit, 1 << FIRST_REST)
        o_back = swap(total((first, first, low_half, whole), keep_o, o_sib, o1, o2), TP)
        b2 = swap(total((high_half, high_half, high_half), b_own_lo, b_lo, b1), NEAR)
        s2 = swap(total((second, second, high_half), keep_s, s_sib, s1), FAR)
        vec = step(vec, CORE_BIT)
        a_unit = rest(a_unit, a_more)
        a_near, a_far = swap(a_unit, NEAR), swap(a_unit, FAR)
        s_unit = total((first, first, low_half, whole, whole), keep_s, s_sib, s1, s2, o_back)
        s_more = swap(s_unit, 1 << FIRST_REST)
        vec = step(vec, TP_BIT)
        b_unit = total((low_half, low_half, low_half, whole), b_own_lo, b_lo, b1, b2)
        b_more = swap(b_unit, 1 << FIRST_REST)

        def join(*parts):
            return note(jnp.concatenate(turn(*parts)))

        a_three = join(a_unit, a_near, a_far)
        a_corner = swap(a_far, NEAR)
        a_sib = swap(a_three, CORE)
        vec = step(vec, NEAR_BIT)
        s_unit = rest(s_unit, s_more)
        s_near, s_far = swap(s_unit, NEAR), swap(s_unit, FAR)
        vec = step(vec, FAR_BIT)
        a_corner, = turn(a_corner)
        a_corner_sib = swap(a_corner, CORE)
        out_got = swap(turn(out_sib)[0], CORE)
        layer_out = note((mid + out_own + turn(out_got)[0].astype(F32) + down_bias).astype(BF16))
        b_unit = rest(b_unit, b_more)
        b_near, b_far = swap(b_unit, NEAR), swap(b_unit, FAR)
        s_three = join(s_unit, s_near, s_far)
        s_corner = swap(s_far, NEAR)
        s_sib = swap(s_three, CORE)
        for bit in range(FIRST_REST, bits):
            vec = step(vec, bit)
        up_grad, = call(
            lambda *r: place_mlp_kernel(False, *r),
            [((wide, 2 * hidden), F32)],
            [SM] + [VM] * 4,
            "place_up",
        )(ids, *turn(a_three, a_corner, a_sib, a_corner_sib))
        note(up_grad)
        b_three = join(b_unit, b_near, b_far)
        b_corner = swap(b_near, FAR)
        b_sib = swap(b_three, CORE)
        s_corner, = turn(s_corner)
        s_corner_sib = swap(s_corner, CORE)
        qkv_grad, out_grad = call(
            place_attn_kernel,
            [((3, wide, width), F32), ((width, wide), F32)],
            [SM] + [VM] * 4,
            "place_attn",
        )(ids, *turn(s_three, s_corner, s_sib, s_corner_sib))
        note(out_grad)
        b_corner, = turn(b_corner)
        down_grad, = call(
            lambda *r: place_mlp_kernel(True, *r),
            [((2 * hidden, wide), F32)],
            [SM] + [VM] * 4,
            "place_down",
        )(ids, b_three, b_corner, b_sib, swap(b_corner, CORE))
        one_of = lambda i: vec[i]
        qvb = lax.dynamic_slice(vec, (6, half * width), (2, width))
        ub = lax.dynamic_slice(vec, (8 + 2 * half, 0), (2, hidden)).reshape(2 * hidden)
        return (
            layer_out, in_grad, one_of(0), one_of(1), jnp.transpose(qkv_grad, (1, 0, 2)), qvb,
            out_grad, one_of(4), one_of(2), one_of(3), up_grad, ub, down_grad, one_of(5),
        )

    return on_device


def solution(mesh):
    tokens, vector = P(("dp", "tp"), None), P()
    in_specs = (
        tokens, P("dp", None), vector, vector, P(None, None, "tp"), P(None, "tp"), P("tp", None), vector,
        vector, vector, P(None, "tp"), P("tp"), P("tp", None), vector, tokens,
    )
    out_specs = (
        tokens, tokens, vector, vector, P(None, None, "tp"), P(None, "tp"), P("tp", None), vector,
        vector, vector, P(None, "tp"), P("tp"), P("tp", None), vector,
    )
    return jax.shard_map(build(mesh), mesh=mesh, in_specs=in_specs, out_specs=out_specs, check_vma=False)
```

```python
import math

import jax
import jax.numpy as jnp
from jax import lax
from jax.experimental import pallas as pl
from jax.experimental.pallas import tpu as pltpu
from jax.sharding import PartitionSpec as P

HEAD = 64
SEQ = 128
UNITS = 4
EPS = 1e-05
SCALE = 1.0 / math.sqrt(HEAD)
F32 = jnp.float32
BF16 = jnp.bfloat16

VM = pl.BlockSpec(memory_space=pltpu.VMEM)
SM = pl.BlockSpec(memory_space=pltpu.SMEM)
HB = pl.BlockSpec(memory_space=pl.ANY)

NEAR_FIRST, FAR_FIRST = (0, 2, 1, 3), (0, 1, 2, 3)
TP_BIT, CORE_BIT, NEAR_BIT, FAR_BIT, FIRST_REST = 0, 1, 2, 3, 4
TP, CORE, NEAR, FAR = (1 << bit for bit in (TP_BIT, CORE_BIT, NEAR_BIT, FAR_BIT))


def nn(a, b):
    return lax.dot_general(a, b, (((1,), (0,)), ((), ())), preferred_element_type=F32)


def nt(a, b):
    return lax.dot_general(a, b, (((1,), (1,)), ((), ())), preferred_element_type=F32)


def tn(a, b):
    return lax.dot_general(a, b, (((0,), (0,)), ((), ())), preferred_element_type=F32)


def normalize(values):
    center = values - jnp.mean(values, axis=-1, keepdims=True)
    inv = lax.rsqrt(jnp.mean(center * center, axis=-1, keepdims=True) + EPS)
    return center * inv, inv


def norm_back(values, grad, gain):
    normed, inv = normalize(values)
    scaled = grad * gain
    mean_g = jnp.mean(scaled, axis=-1, keepdims=True)
    mean_gn = jnp.mean(scaled * normed, axis=-1, keepdims=True)
    part = inv * (scaled - mean_g - normed * mean_gn)
    gain_sum = jnp.sum(grad * normed, axis=0, keepdims=True)
    shift_sum = jnp.sum(grad, axis=0, keepdims=True)
    return part, gain_sum, shift_sum


def row_mask(lens, row):
    at_k = lax.broadcasted_iota(jnp.int32, (SEQ, 1), 0)
    at_q = lax.broadcasted_iota(jnp.int32, (1, SEQ), 1)
    total = jnp.int32(0)
    seg_q = jnp.zeros((1, SEQ), jnp.int32)
    seg_k = jnp.zeros((SEQ, 1), jnp.int32)
    for entry in range(lens.shape[1]):
        total = total + lens[row, entry]
        seg_q = seg_q + jnp.where(at_q >= total, 1, 0)
        seg_k = seg_k + jnp.where(at_k >= total, 1, 0)
    allowed = (seg_q == seg_k) & (at_k <= at_q) & ((at_k < total) | (at_k == at_q))
    valid = jnp.where(at_k < total, 1.0, 0.0).astype(F32)
    return jnp.concatenate([allowed, allowed], axis=1), valid


def low_lanes():
    return lax.broadcasted_iota(jnp.int32, (SEQ, 2 * HEAD), 1) < HEAD


def stack_pair(pair, low):
    zero = jnp.zeros_like(pair)
    return jnp.concatenate([jnp.where(low, pair, zero), jnp.where(low, zero, pair)], axis=0)


def pair_probs(q_stack, keys, allowed2):
    scores = jnp.where(allowed2, nt(keys, q_stack) * SCALE, -1e30)
    weights = jnp.exp(scores - jnp.max(scores, axis=0, keepdims=True))
    return weights * (1.0 / jnp.sum(weights, axis=0, keepdims=True))


class Copies:
    def __init__(self, sems):
        self.sems = sems
        self.count = 0

    def start(self, src, dst):
        made = pltpu.make_async_copy(src, dst, self.sems.at[self.count])
        self.count += 1
        made.start()
        return made


def wait(*copies):
    for made in copies:
        made.wait()


def blocks(count, size=SEQ):
    return [slice(i * size, (i + 1) * size) for i in range(count)]


def over_rows(tokens, body, start):
    at = lambda i: pl.ds(pl.multiple_of(i * SEQ, SEQ), SEQ)
    return lax.fori_loop(0, tokens // SEQ, lambda i, carry: body(at(i), carry), start)


def project(nrm, w, bias, qkv):
    width = w.shape[2]
    for part in range(3):
        value = nn(nrm[...], w[part])
        if part != 1:
            value = value + bias[pl.ds(part // 2, 1), :]
        qkv[:, part * width : (part + 1) * width] = value.astype(BF16)


def attend(lens, ids, qkv, att):
    width = att.shape[1]
    rows = att.shape[0] // SEQ
    low = low_lanes()
    @pl.loop(0, rows, unroll=2)
    def _(row):
        at = pl.ds(pl.multiple_of(row * SEQ, SEQ), SEQ)
        allowed2, valid = row_mask(lens, ids[0] * rows + row)
        for first in range(0, width, 2 * HEAD):
            q = qkv[at, first : first + 2 * HEAD]
            k = qkv[at, width + first : width + first + 2 * HEAD]
            v = qkv[at, 2 * width + first : 2 * width + first + 2 * HEAD]
            probs = pair_probs(stack_pair(q, low), k, allowed2)
            both = tn(probs.astype(BF16), v)
            out = jnp.where(low, both[:SEQ], both[SEQ:]) * valid
            att[at, first : first + 2 * HEAD] = out.astype(BF16)


def own_fwd_kernel(lens, ids, x_hbm, vecs, w_hbm, bias, nrm_hbm, qkv_hbm, att, x, w, nrm, qkv, sems):
    copies = Copies(sems)
    x_in = copies.start(x_hbm, x)
    w_in = copies.start(w_hbm, w)
    wait(x_in)

    def norm_rows(at, carry):
        normed, _ = normalize(x[at, :].astype(F32))
        nrm[at, :] = (normed * vecs[0:1, :] + vecs[1:2, :]).astype(BF16)
        return carry

    over_rows(x.shape[0], norm_rows, 0)
    nrm_out = copies.start(nrm, nrm_hbm)
    wait(w_in)
    project(nrm, w, bias, qkv)
    qkv_out = copies.start(qkv, qkv_hbm)
    attend(lens, ids, qkv, att)
    wait(nrm_out, qkv_out)


def unit_block(part, rows, width, first=0):
    return pl.ds(first + (part // 2) * rows, rows), pl.ds((part % 2) * width, width)


def fetch_weights(copies, ids, mine_parts, sib_parts, w, wo):
    core, mine = ids[1], ids[2]
    width = w.shape[2]
    part_rows = w.shape[1] // (2 * UNITS)
    to_w, to_wo = [], []
    for side, parts in ((core, mine_parts), (1 - core, sib_parts)):
        for step, unit_ref in enumerate(parts):
            unit = jnp.bitwise_xor(mine, step)
            at_w = pl.ds(pl.multiple_of((side * UNITS + unit) * part_rows, part_rows), part_rows)
            at_o = pl.ds(pl.multiple_of(unit * part_rows, part_rows), part_rows)
            cols = pl.ds(pl.multiple_of(side * width, width), width)
            for part in range(3):
                to_w.append(copies.start(unit_ref.at[unit_block(part, part_rows, width)], w.at[part, at_w, :]))
            if wo is not None:
                to_wo.append(copies.start(unit_ref.at[unit_block(3, part_rows, width)], wo.at[at_o, cols]))
    return to_w, to_wo


def fetch_output_weight(copies, ids, mine_parts, sib_parts, wo):
    core, mine = ids[1], ids[2]
    width = wo.shape[0]
    part_rows = width // UNITS
    made = []
    for side, parts in ((core, mine_parts), (1 - core, sib_parts)):
        for step, unit_ref in enumerate(parts):
            at_o = pl.ds(pl.multiple_of(jnp.bitwise_xor(mine, step) * part_rows, part_rows), part_rows)
            cols = pl.ds(pl.multiple_of(side * width, width), width)
            made.append(copies.start(unit_ref.at[unit_block(3, part_rows, width)], wo.at[at_o, cols]))
    return made


def other_fwd_kernel(lens, ids, x_hbm, nrm_hbm, bias, att_own_hbm, wo_own_hbm, vecs, *refs):
    mine_parts, sib_parts = refs[:4], refs[4:8]
    qkv_hbm, att_hbm, mid_hbm, nm = refs[8:12]
    x, nrm, att_own, wo_own, w, wo, qkv, att, mid, sems = refs[12:]
    copies = Copies(sems)
    nrm_in = copies.start(nrm_hbm, nrm)
    to_w, to_wo = fetch_weights(copies, ids, mine_parts, sib_parts, w, wo)
    late = [copies.start(x_hbm, x), copies.start(att_own_hbm, att_own), copies.start(wo_own_hbm, wo_own)]
    wait(nrm_in, *to_w)
    project(nrm, w, bias, qkv)
    qkv_out = copies.start(qkv, qkv_hbm)
    attend(lens, ids, qkv, att)
    att_out = copies.start(att, att_hbm)
    wait(*to_wo, *late)
    mid[...] = nn(att_own[...], wo_own[...]) + nn(att[...], wo[...])

    def norm_rows(at, carry):
        value = x[at, :].astype(F32) + mid[at, :] + vecs[2:3, :]
        mid[at, :] = value
        normed, _ = normalize(value)
        nm[at, :] = (normed * vecs[3:4, :] + vecs[4:5, :]).astype(BF16)
        return carry

    over_rows(x.shape[0], norm_rows, 0)
    mid_out = copies.start(mid, mid_hbm)
    wait(qkv_out, att_out, mid_out)


def gelu_parts(pre):
    bell = jnp.exp(-0.5 * pre * pre)
    t = 1.0 / (1.0 + (0.3275911 * math.sqrt(0.5)) * jnp.abs(pre))
    poly = 1.061405429 * t - 1.453152027
    poly = poly * t + 1.421413741
    poly = poly * t - 0.284496736
    poly = poly * t + 0.254829592
    tail = 0.5 * (poly * t) * bell
    cdf = jnp.where(pre >= 0, 1.0 - tail, tail)
    return pre * cdf, cdf + pre * bell * (1.0 / math.sqrt(2.0 * math.pi))


def mlp_kernel(own, *refs):
    ids, nm_a, nm_b, ct_a, ct_b, bias = refs[:6]
    if own:
        up_hbm, down_hbm = refs[6:8]
        out_hbm, dnm_hbm, keep_a, send_a, keep_b, send_b, bias_g = refs[8:15]
        scratch = refs[15:]
    else:
        units, (out_prev, dnm_prev) = refs[6:10], refs[10:12]
        out_own_hbm, out_sib_hbm, dnm_own_hbm, dnm_sib_hbm, keep_a, send_a, keep_b, send_b, bias_g = refs[12:21]
        scratch = refs[21:]
    up, down, nm, ct, pre, dact, act, pg, gu, gd, sems = scratch[:11]
    core, mine = ids[1], ids[2]
    hidden = up.shape[1]
    tokens = nm_a.shape[0]
    unit_rows = up.shape[0] // UNITS
    copies = Copies(sems)
    copy = copies.start
    halves = (pl.ds(0, tokens), pl.ds(tokens, tokens))

    def unit_at(step):
        start = jnp.bitwise_xor(mine, step) * unit_rows
        return pl.ds(pl.multiple_of(start, unit_rows), unit_rows)

    at = pl.ds(pl.multiple_of(core * hidden, hidden), hidden)
    if own:
        ups = [copy(up_hbm.at[:, at], up)]
    else:
        ups = [copy(unit.at[pl.ds(0, unit_rows)], up.at[unit_at(i), :]) for i, unit in enumerate(units)]
    nms = [copy(nm_a, nm.at[halves[0]])]
    if own:
        downs = [copy(down_hbm.at[at, :], down)]
    else:
        downs = [copy(unit.at[pl.ds(unit_rows, unit_rows)], down.at[unit_at(i), :]) for i, unit in enumerate(units)]
    cts = [copy(ct_a, ct.at[halves[0]])]
    nms.append(copy(nm_b, nm.at[halves[1]]))
    cts.append(copy(ct_b, ct.at[halves[1]]))
    if not own:
        prev_out, prev_dnm, dnm_own, dnm_sib, out_own, out_sib = scratch[11:17]
        lates = [copy(dnm_prev, prev_dnm), copy(out_prev, prev_out)]
    else:
        dnm, out = scratch[11:13]

    piece = 16

    def half_step(half, total):
        rows = pl.ds(pl.multiple_of(half * tokens, tokens), tokens)
        for i in range(2):
            pl.when(half == i)(lambda: wait(nms[i], *(ups if i == 0 else ())))
        pre[...] = nn(nm[rows, :], up[...])
        for i in range(2):
            pl.when(half == i)(lambda: wait(cts[i], *(downs if i == 0 else ())))
        dact[...] = nt(ct[rows, :], down[...])

        def elementwise(step, total):
            at = pl.ds(pl.multiple_of(step * piece, piece), piece)
            to = pl.ds(pl.multiple_of(half * tokens + step * piece, piece), piece)
            value, slope = gelu_parts(pre[at, :] + bias[...])
            act[to, :] = value.astype(BF16)
            back = (dact[at, :] * slope).astype(BF16)
            pg[to, :] = back
            return total + jnp.sum(back.astype(F32), axis=0, keepdims=True)

        return lax.fori_loop(0, tokens // piece, elementwise, total, unroll=2)

    bias_sum = lax.fori_loop(0, 2, half_step, jnp.zeros((1, hidden), F32))
    bias_g[...] = bias_sum
    writes = []
    if own:
        dnm[...] = nt(pg[...], up[...]).astype(BF16)
        writes.append(copy(dnm, dnm_hbm))
        out[...] = nn(act[...], down[...]).astype(BF16)
        writes.append(copy(out, out_hbm))
    else:
        wait(*lates)
        total = nt(pg[...], up[...])
        dnm_own[...] = total[:tokens] + prev_dnm[:tokens, :].astype(F32)
        dnm_sib[...] = (total[tokens:] + prev_dnm[tokens:, :].astype(F32)).astype(BF16)
        writes += [copy(dnm_own, dnm_own_hbm), copy(dnm_sib, dnm_sib_hbm)]
        total = nn(act[...], down[...])
        out_own[...] = total[:tokens] + prev_out[:tokens, :].astype(F32)
        out_sib[...] = (total[tokens:] + prev_out[tokens:, :].astype(F32)).astype(BF16)
        writes += [copy(out_own, out_own_hbm), copy(out_sib, out_sib_hbm)]
    for source, grad, order, targets in (
        (gd, lambda: tn(act[...], ct[...]), NEAR_FIRST, (keep_b, send_b)),
        (gu, lambda: tn(nm[...], pg[...]), NEAR_FIRST, (keep_a, send_a)),
    ):
        source[...] = grad().astype(BF16)
        for place, step in enumerate(order):
            to = targets[place // 2].at[pl.ds((place % 2) * unit_rows, unit_rows)]
            writes.append(copy(source.at[unit_at(step), :], to))
    wait(*writes)


def attend_back(lens, ids, qkv, datt, dqkv):
    width = datt.shape[1]
    rows = datt.shape[0] // SEQ
    low = low_lanes()

    @pl.loop(0, rows)
    def _(row):
        allowed2, valid = row_mask(lens, ids[0] * rows + row)
        at = pl.ds(pl.multiple_of(row * SEQ, SEQ), SEQ)
        for first in range(0, width, 2 * HEAD):
            q_cols = slice(first, first + 2 * HEAD)
            k_cols = slice(width + first, width + first + 2 * HEAD)
            v_cols = slice(2 * width + first, 2 * width + first + 2 * HEAD)
            k = qkv[at, k_cols]
            q_stack = stack_pair(qkv[at, q_cols], low)
            grad = (datt[at, q_cols].astype(F32) * valid).astype(BF16)
            g_stack = stack_pair(grad, low)
            probs = pair_probs(q_stack, k, allowed2)
            dqkv[at, v_cols] = nn(probs.astype(BF16), g_stack).astype(BF16)
            prob_grad = nt(qkv[at, v_cols], g_stack)
            inner = jnp.sum(probs * prob_grad, axis=0, keepdims=True)
            score_grad = (probs * (prob_grad - inner)).astype(BF16)
            both = tn(score_grad, k)
            dqkv[at, q_cols] = (jnp.where(low, both[:SEQ], both[SEQ:]) * SCALE).astype(BF16)
            dqkv[at, k_cols] = (nn(score_grad, q_stack) * SCALE).astype(BF16)


def weight_grads(copies, ids, nrm, dqkv, dw, dwo, order, keep, send):
    core, mine = ids[1], ids[2]
    width = dw.shape[2]
    part_rows = dw.shape[1] // (2 * UNITS)
    made = []
    for part in (3, 2, 1, 0):
        if part < 3:
            dw[part] = tn(nrm[...], dqkv[:, part * width : (part + 1) * width]).astype(BF16)
        for place in range(UNITS):
            unit = jnp.bitwise_xor(mine, order[place])
            for side, target in ((1 - core, send), (core, keep)):
                at_w = pl.ds(pl.multiple_of((side * UNITS + unit) * part_rows, part_rows), part_rows)
                at_o = pl.ds(pl.multiple_of(unit * part_rows, part_rows), part_rows)
                cols = pl.ds(pl.multiple_of(side * width, width), width)
                source = dw.at[part, at_w, :] if part < 3 else dwo.at[at_o, cols]
                made.append(copies.start(source, target.at[unit_block(part, part_rows, width, 2 * place * part_rows)]))
    return made


def bias_sums(dqkv):
    width = dqkv.shape[1] // 3
    ones = jnp.ones((8, dqkv.shape[0]), BF16)
    return [nn(ones, dqkv[:, first : first + width])[0:1] for first in (0, 2 * width)]


def normed_grad(dqkv, w):
    width = w.shape[2]
    total = nt(dqkv[:, :width], w[0])
    for part in range(1, 3):
        total = total + nt(dqkv[:, part * width : (part + 1) * width], w[part])
    return total


def other_back_kernel(lens, ids, dnm_own_hbm, dnm_sib_hbm, ct_hbm, mid_hbm, vecs, qkv_hbm, att_hbm, nrm_hbm, *refs):
    mine_parts, sib_parts = refs[:4], refs[4:8]
    mg_hbm, dqkv_hbm, keep, send, sums = refs[8:13]
    dnm_own, dnm_sib, ct, mid, qkv, att, nrm, wo, mg, ml, datt, dqkv, dw, dwo, sems = refs[13:]
    copies = Copies(sems)
    first_in = [
        copies.start(dnm_own_hbm, dnm_own), copies.start(dnm_sib_hbm, dnm_sib),
        copies.start(ct_hbm, ct), copies.start(mid_hbm, mid),
    ]
    to_wo = fetch_output_weight(copies, ids, mine_parts, sib_parts, wo)
    qkv_in, att_in, nrm_in = copies.start(qkv_hbm, qkv), copies.start(att_hbm, att), copies.start(nrm_hbm, nrm)
    wait(*first_in)

    def back_rows(at, totals):
        grad = dnm_own[at, :] + dnm_sib[at, :].astype(F32)
        part, gain_sum, shift_sum = norm_back(mid[at, :], grad, vecs[3:4, :])
        out_grad = ct[at, :].astype(F32)
        value = out_grad + part
        mg[at, :] = value
        ml[at, :] = value.astype(BF16)
        adds = (gain_sum, shift_sum, jnp.sum(value, axis=0, keepdims=True), jnp.sum(out_grad, axis=0, keepdims=True))
        return tuple(total + add for total, add in zip(totals, adds))

    totals = over_rows(mid.shape[0], back_rows, (jnp.zeros((1, mid.shape[1]), F32),) * 4)
    sums[...] = jnp.concatenate(list(totals) + [jnp.zeros((4, mid.shape[1]), F32)])
    mg_out = copies.start(mg, mg_hbm)
    wait(*to_wo, qkv_in, att_in)
    datt[...] = nt(ml[...], wo[...]).astype(BF16)
    dwo[...] = tn(att[...], ml[...]).astype(BF16)
    attend_back(lens, ids, qkv, datt, dqkv)
    wait(nrm_in)
    dqkv_out = copies.start(dqkv, dqkv_hbm)
    outs = weight_grads(copies, ids, nrm, dqkv, dw, dwo, NEAR_FIRST, keep, send)
    wait(mg_out, dqkv_out, *outs)


def own_back_kernel(
    lens, ids, mg_hbm, wo_hbm, qkv_hbm, att_hbm, nrm_hbm, dqkv_hbm, keep, send,
    mg, wo, qkv, att, nrm, ml, datt, dqkv, dw, dwo, sems,
):
    copies = Copies(sems)
    mg_in, wo_in = copies.start(mg_hbm, mg), copies.start(wo_hbm, wo)
    att_in, qkv_in, nrm_in = copies.start(att_hbm, att), copies.start(qkv_hbm, qkv), copies.start(nrm_hbm, nrm)
    wait(mg_in)
    ml[...] = mg[...].astype(BF16)
    wait(wo_in, att_in, qkv_in)
    datt[...] = nt(ml[...], wo[...]).astype(BF16)
    dwo[...] = tn(att[...], ml[...]).astype(BF16)
    attend_back(lens, ids, qkv, datt, dqkv)
    dqkv_out = copies.start(dqkv, dqkv_hbm)
    wait(nrm_in)
    outs = weight_grads(copies, ids, nrm, dqkv, dw, dwo, NEAR_FIRST, keep, send)
    wait(dqkv_out, *outs)


def input_grad_kernel(ids, dqkv_a_hbm, dqkv_b_hbm, mg_hbm, x_hbm, vecs, w_hbm, sums, ub_own, ub_other, *refs):
    mine_parts, sib_parts = refs[:4], refs[4:8]
    in_grad, vec = refs[8:10]
    dqkv_a, dqkv_b, mg, x, w_own, w_other, dn, sems = refs[10:]
    half, core = ids[0], ids[1]
    copies = Copies(sems)
    own_in = [copies.start(dqkv_a_hbm, dqkv_a), copies.start(w_hbm, w_own)]
    other_in, _ = fetch_weights(copies, ids, mine_parts, sib_parts, w_other, None)
    other_in.append(copies.start(dqkv_b_hbm, dqkv_b))
    late = [copies.start(mg_hbm, mg), copies.start(x_hbm, x)]
    width = w_own.shape[2]
    wait(*own_in)
    dn[...] = normed_grad(dqkv_a, w_own)
    wait(*other_in)
    dn[...] += normed_grad(dqkv_b, w_other)
    wait(*late)

    def back_rows(at, totals):
        part, gain_sum, shift_sum = norm_back(x[at, :].astype(F32), dn[at, :], vecs[0:1, :])
        in_grad[at, :] = (mg[at, :] + part).astype(BF16)
        return totals[0] + gain_sum, totals[1] + shift_sum

    totals = over_rows(x.shape[0], back_rows, (jnp.zeros((1, x.shape[1]), F32),) * 2)
    vec[...] = jnp.zeros_like(vec)
    for i in range(2):
        vec[i : i + 1, :] = totals[i]
    vec[2:6, :] = sums[0:4, :]
    for dqkv, side in ((dqkv_a, half), (dqkv_b, 1 - half)):
        for i, value in enumerate(bias_sums(dqkv)):
            vec[6 + i : 7 + i, pl.ds(pl.multiple_of(side * width, width), width)] = value
    vec[pl.ds(8 + 2 * half + core, 1), :] = ub_own[...]
    vec[pl.ds(8 + 2 * (1 - half) + core, 1), :] = ub_other[...]


def layer_out_kernel(mid_hbm, own_hbm, sib_hbm, bias, out, mid, own, sib, sems):
    copies = Copies(sems)
    wait(copies.start(mid_hbm, mid), copies.start(own_hbm, own), copies.start(sib_hbm, sib))

    def rows(at, carry):
        out[at, :] = (mid[at, :] + own[at, :] + sib[at, :].astype(F32) + bias[...]).astype(BF16)
        return carry

    over_rows(out.shape[0], rows, 0)


class Placing:
    def __init__(self, ids, copies):
        self.core, self.mine = ids[1], ids[2]
        self.copies = copies
        self.work, self.outs = [], []

    def take(self, refs, narrow, wide, targets):
        for i, ref in enumerate(refs):
            side = self.core if i < UNITS else 1 - self.core
            unit = jnp.bitwise_xor(self.mine, i % UNITS)
            self.work.append((self.copies.start(ref, narrow.at[i]), narrow, wide, i, targets(side, unit)))

    def finish(self):
        for arrived, narrow, wide, i, targets in self.work:
            arrived.wait()
            wide[i] = narrow[i].astype(F32)
            for block, target in targets:
                self.outs.append(self.copies.start(wide.at[i, block[0], block[1]], target))
        wait(*self.outs)


def mlp_targets(out, down_first, rows, width):
    def targets(side, unit):
        base, start = pl.multiple_of(side * width, width), pl.multiple_of(unit * rows, rows)
        if down_first:
            target = out.at[pl.ds(pl.multiple_of(base + start, rows), rows), :]
        else:
            target = out.at[pl.ds(start, rows), pl.ds(base, width)]
        return [((pl.ds(0, rows), pl.ds(0, width)), target)]

    return targets


def attn_targets(w, wo):
    width = w.shape[2]
    rows = w.shape[1] // (2 * UNITS)

    def targets(side, unit):
        at_w = pl.ds(pl.multiple_of((side * UNITS + unit) * rows, rows), rows)
        at_o = pl.ds(pl.multiple_of(unit * rows, rows), rows)
        cols = pl.ds(pl.multiple_of(side * width, width), width)
        places = [w.at[part, at_w, :] for part in range(3)] + [wo.at[at_o, cols]]
        return [(unit_block(part, rows, width), place) for part, place in enumerate(places)]

    return targets


def place_mlp_kernel(down_first, ids, *refs):
    units, (out, narrow, wide, sems) = refs[:8], refs[8:]
    placing = Placing(ids, Copies(sems))
    placing.take(units, narrow, wide, mlp_targets(out, down_first, *units[0].shape))
    placing.finish()


def place_down_kernel(*refs):
    place_mlp_kernel(True, *refs)


def place_two_kernel(ids, *refs):
    up_units, attn_units = refs[:8], refs[8:16]
    up, w, wo, narrow_u, wide_u, narrow_a, wide_a, sems = refs[16:]
    placing = Placing(ids, Copies(sems))
    placing.take(up_units, narrow_u, wide_u, mlp_targets(up, False, *up_units[0].shape))
    placing.take(attn_units, narrow_a, wide_a, attn_targets(w, wo))
    placing.finish()


def vmem(*buffers, sems):
    return [pltpu.VMEM(shape, dtype) for shape, dtype in buffers] + [pltpu.SemaphoreType.DMA((sems,))]


def call(kernel, outs, in_specs, name, scratch=(), out_specs=None, limit=60, gflop=1.0):
    return pl.pallas_call(
        kernel,
        out_shape=tuple(jax.ShapeDtypeStruct(shape, dtype) for shape, dtype in outs),
        in_specs=in_specs,
        out_specs=tuple(VM for _ in outs) if out_specs is None else tuple(out_specs),
        scratch_shapes=list(scratch),
        name=name,
        cost_estimate=pl.CostEstimate(flops=int(gflop * 1e9), bytes_accessed=8 << 20, transcendentals=0),
        compiler_params=pltpu.CompilerParams(vmem_limit_bytes=limit * 1024 * 1024),
    )


def build(mesh):
    devices = mesh.shape["dp"] * mesh.shape["tp"]
    bits = devices.bit_length() - 1

    def swap(value, mask):
        return lax.ppermute(value, ("dp", "tp"), [(i, i ^ mask) for i in range(devices)])

    def after(value, *deps):
        return lax.optimization_barrier((value, deps))[0]

    def share(unit):
        return [unit] + [swap(unit, mask) for mask in (NEAR, FAR, NEAR | FAR)]

    def add(*terms):
        total = terms[0].astype(F32)
        for term in terms[1:]:
            total = total + term.astype(F32)
        return total

    last = []

    def turn(*values):
        return lax.optimization_barrier((values, last[-1]))[0]

    def note(value):
        last.append(value)
        return value

    def due(*values):
        values = turn(*values)
        note(values[-1])
        return values

    def total(parts, *terms):
        cut = lambda v, part: v if part is None else v[v.shape[0] * part[0] // 4 : v.shape[0] * part[1] // 4]
        return note(add(*[cut(term, part) for term, part in zip(turn(*terms), parts)]).astype(BF16))

    def on_device(
        layer_in, lengths, attn_gain, attn_shift, qkv_weight, qv_bias, out_weight, out_bias,
        mlp_gain, mlp_shift, up_weight, up_bias, down_weight, down_bias, cotangent,
    ):
        tokens, wide = layer_in.shape
        width = qkv_weight.shape[2]
        hidden = up_weight.shape[1] // 2
        flat = lax.axis_index("dp") * 2 + lax.axis_index("tp")
        half = lax.axis_index("tp")
        core = (flat >> CORE_BIT) & 1
        mine = ((flat >> FAR_BIT) & 1) * 2 + ((flat >> NEAR_BIT) & 1)
        ids = jnp.stack([half, core, mine]).astype(jnp.int32)
        row = lambda v: v.reshape(1, -1)
        none = jnp.zeros_like(out_bias)
        vecs = jnp.stack([attn_gain, attn_shift, out_bias, mlp_gain, mlp_shift, none, none, none])
        w_own = jnp.transpose(qkv_weight, (1, 0, 2))

        part_rows = wide // (2 * UNITS)
        unit_w = lax.dynamic_slice(w_own, (0, (core * UNITS + mine) * part_rows, 0), (3, part_rows, width))
        unit_o = lax.dynamic_slice(out_weight, (mine * part_rows, core * width), (part_rows, width))
        attn_unit = jnp.concatenate(
            [jnp.concatenate([unit_w[0], unit_w[1]], axis=1), jnp.concatenate([unit_w[2], unit_o], axis=1)]
        )
        attn_unit = swap(attn_unit, TP)

        acts = (tokens, 3 * width)
        one = (tokens, wide)
        head = (tokens, width)
        w_shape, wo_shape = (3, wide, width), (width, wide)
        nrm, qkv_own, att_own = call(
            own_fwd_kernel,
            [(one, BF16), (acts, BF16), (head, BF16)],
            [SM, SM, HB, VM, HB, VM],
            "attn_own_fwd",
            gflop=0.5,
            scratch=vmem((one, BF16), (w_shape, BF16), (one, BF16), (acts, BF16), sems=4),
            out_specs=[HB, HB, VM],
        )(lengths, ids, layer_in, vecs, w_own, qv_bias)
        attn_parts = share(after(attn_unit, att_own))
        unit_rows = hidden // UNITS
        up_late, down_late, bias_late, up_bias_late = after((up_weight, down_weight, qv_bias, up_bias), att_own)
        mlp_unit = jnp.concatenate(
            [
                lax.dynamic_slice(up_late, (mine * unit_rows, core * hidden), (unit_rows, hidden)),
                lax.dynamic_slice(down_late, (core * hidden + mine * unit_rows, 0), (unit_rows, wide)),
            ]
        )
        mlp_unit = swap(mlp_unit, TP)
        small = jnp.concatenate([bias_late.reshape(-1), up_bias_late])
        small_other = swap(small.reshape(-1, 128), TP).reshape(-1)
        ct_sib = swap(cotangent, CORE)
        bias_other = small_other[: 2 * width].reshape(2, width)
        up_bias_own = lax.dynamic_slice(up_bias, (core * hidden,), (hidden,))
        up_bias_other = lax.dynamic_slice(small_other, (2 * width + core * hidden,), (hidden,))
        attn_sib = [swap(part, CORE) for part in attn_parts]
        qkv_other, att_other, mid, nm = call(
            other_fwd_kernel,
            [(acts, BF16), (head, BF16), (one, F32), (one, BF16)],
            [SM, SM, HB, HB, VM, HB, HB, VM] + [HB] * 8,
            "attn_other_fwd",
            gflop=6,
            scratch=vmem(
                (one, BF16), (one, BF16), (head, BF16), (wo_shape, BF16), (w_shape, BF16), (wo_shape, BF16),
                (acts, BF16), (head, BF16), (one, F32), sems=40,
            ),
            out_specs=[HB, HB, HB, VM],
        )(
            lengths, ids, layer_in, after(nrm, mlp_unit), bias_other, att_own, out_weight, vecs,
            *attn_parts, *attn_sib,
        )
        mlp_near, mlp_far = swap(mlp_unit, NEAR), swap(mlp_unit, FAR)

        mlp_near, mlp_far, nm = after((mlp_near, mlp_far, nm))
        mlp_parts = [mlp_unit, mlp_near, mlp_far, swap(mlp_unit, NEAR | FAR)]
        nm_sib = swap(nm, CORE)
        tall, square = (2 * tokens, wide), (wide, hidden)
        scratch = [
            (square, BF16), (square, BF16), (tall, BF16), (tall, BF16), ((tokens, hidden), F32), ((tokens, hidden), F32),
            ((2 * tokens, hidden), BF16), ((2 * tokens, hidden), BF16), (square, BF16), (square, BF16),
        ]

        def mlp_scratch(*more):
            buffers = vmem(*scratch, *more, sems=40)
            return buffers[:10] + buffers[-1:] + buffers[10:-1]

        both = (2 * tokens, wide)
        pair = (2 * unit_rows, hidden)
        out_a, dnm_a, keep_own, send_own, b_own_lo, b_own_hi, ub_own = call(
            lambda *r: mlp_kernel(True, *r),
            [(both, BF16), (both, BF16), *[(pair, BF16)] * 4, ((1, hidden), F32)],
            [SM] + [HB] * 4 + [VM] + [HB] * 2,
            "mlp_own",
            gflop=1,
            scratch=mlp_scratch((tall, BF16), (tall, BF16)),
            out_specs=[HB] * 6 + [VM],
        )(ids, nm, nm_sib, cotangent, ct_sib, row(up_bias_own), up_weight, down_weight)
        out_own, out_sib, dnm_own, dnm_sib, keep_other, send_other, b_other_lo, b_other_hi, ub_other = call(
            lambda *r: mlp_kernel(False, *r),
            [
                (one, F32), (one, BF16), (one, F32), (one, BF16), *[(pair, BF16)] * 4,
                ((1, hidden), F32),
            ],
            [SM] + [HB] * 4 + [VM] + [HB] * 6,
            "mlp_other",
            gflop=12,
            scratch=mlp_scratch((tall, BF16), (tall, BF16), (one, F32), (one, BF16), (one, F32), (one, BF16)),
            out_specs=[HB] * 8 + [VM],
        )(ids, nm, nm_sib, cotangent, ct_sib, row(up_bias_other), *mlp_parts, out_a, dnm_a)
        grad_units = (2 * UNITS * part_rows, 2 * width)
        whole, low_half, high_half, first, second = None, (0, 2), (2, 4), (0, 1), (1, 2)
        a_own = swap(send_own, NEAR)
        note(ub_other)
        a_own, dnm_sib, out_sib, send_other, b_other_hi, b_other_lo = turn(
            a_own, dnm_sib, out_sib, send_other, b_other_hi, b_other_lo
        )
        dnm_got = swap(dnm_sib, CORE)
        a_own2 = swap(total((high_half, high_half), keep_own, a_own), FAR)
        a_other = swap(send_other, NEAR)
        b_hi = swap(b_other_hi, TP)
        mg, dqkv_other, keep_o, send_o, sums_mid = call(
            other_back_kernel,
            [(one, F32), (acts, BF16), (grad_units, BF16), (grad_units, BF16), ((8, wide), F32)],
            [SM, SM, HB, HB, HB, HB, VM, HB, HB, HB] + [HB] * 8,
            "attn_other_back",
            gflop=10,
            scratch=vmem(
                (one, F32), (one, BF16), (one, BF16), (one, F32), (acts, BF16), (head, BF16), (one, BF16),
                (wo_shape, BF16), (one, F32), (one, BF16), (head, BF16), (acts, BF16),
                (w_shape, BF16), (wo_shape, BF16), sems=60,
            ),
            out_specs=[HB] * 4 + [VM],
        )(
            lengths, ids, dnm_own, dnm_got, cotangent, mid, vecs, qkv_other, att_other, nrm,
            *attn_parts, *attn_sib,
        )
        note(sums_mid)
        out_got = swap(turn(out_sib)[0], CORE)
        a_other, a_own2, b_hi, send_o = turn(a_other, a_own2, b_hi, send_o)
        o_sib = swap(send_o, CORE)
        a_other2 = swap(total((high_half, high_half), keep_other, a_other), FAR)
        o1 = swap(total((high_half, high_half), keep_o, o_sib), NEAR)
        b_lo = swap(b_other_lo, TP)
        mg_now, = turn(mg)
        dqkv_own, keep_s, send_s = call(
            own_back_kernel,
            [(acts, BF16), (grad_units, BF16), (grad_units, BF16)],
            [SM, SM] + [HB] * 5,
            "attn_own_back",
            gflop=10,
            scratch=vmem(
                (one, F32), (wo_shape, BF16), (acts, BF16), (head, BF16), (one, BF16),
                (one, BF16), (head, BF16), (acts, BF16), (w_shape, BF16), (wo_shape, BF16), sems=48,
            ),
            out_specs=[HB] * 3,
        )(lengths, ids, mg_now, out_weight, qkv_own, att_own, nrm)
        note(dqkv_own)
        a_other2, o1, b_lo, send_s = turn(a_other2, o1, b_lo, send_s)
        s_sib = swap(send_s, CORE)
        a_back = swap(total((low_half, low_half, whole), keep_other, a_other, a_other2), TP)
        s1 = swap(total((high_half, high_half), keep_s, s_sib), NEAR)
        o2 = swap(total((second, second, high_half), keep_o, o_sib, o1), FAR)
        b1 = swap(total((whole, whole), b_own_hi, b_hi), NEAR)
        a_unit = total((low_half, low_half, whole, whole), keep_own, a_own, a_own2, a_back)
        a_more = swap(a_unit, 1 << FIRST_REST)
        in_grad, vec = call(
            input_grad_kernel,
            [(one, BF16), ((16, wide), F32)],
            [SM, HB, HB, HB, HB, VM, HB, VM, VM, VM] + [HB] * 8,
            "input_grad",
            gflop=0.01,
            scratch=vmem(
                (acts, BF16), (acts, BF16), (one, F32), (one, BF16), (w_shape, BF16), (w_shape, BF16), (one, F32),
                sems=32,
            ),
        )(
            ids, dqkv_own, dqkv_other, *turn(mg), layer_in, vecs, w_own, sums_mid, ub_own, ub_other,
            *attn_parts, *attn_sib,
        )
        note(vec)

        def step(value, bit):
            mine, got = turn(value, swap(value, 1 << bit))
            return note(mine + got)

        def rest(unit, got):
            unit = total((whole, whole), unit, got)
            for bit in range(FIRST_REST + 1, bits):
                unit = total((whole, whole), unit, swap(unit, 1 << bit))
            return unit

        def step_with(value, got):
            mine, got = turn(value, got)
            return note(mine + got)

        s2 = swap(total((second, second, high_half), keep_s, s_sib, s1), FAR)
        o_back = swap(total((first, first, low_half, whole), keep_o, o_sib, o1, o2), TP)
        vec = step(vec, CORE_BIT)
        a_unit = rest(a_unit, a_more)
        a_near, a_far = swap(a_unit, NEAR), swap(a_unit, FAR)
        for bit in range(FIRST_REST, bits):
            vec = step(vec, bit)
        s_unit = total((first, first, low_half, whole, whole), keep_s, s_sib, s1, s2, o_back)
        s_more = swap(s_unit, 1 << FIRST_REST)
        vec_tp = swap(vec, TP)
        b2 = swap(total((high_half, high_half, high_half), b_own_lo, b_lo, b1), FAR)
        layer_out, = call(
            layer_out_kernel,
            [(one, BF16)],
            [HB, HB, HB, VM],
            "layer_out",
            gflop=0.01,
            scratch=vmem((one, F32), (one, F32), (one, BF16), sems=3),
        )(mid, out_own, *turn(out_got), row(down_bias))
        note(layer_out)
        a_near, a_far, vec_tp, b2, s_more = due(a_near, a_far, vec_tp, b2, s_more)
        s_unit = rest(s_unit, s_more)
        s_units = share(s_unit)
        b_unit = total((low_half, low_half, low_half, whole), b_own_lo, b_lo, b1, b2)
        b_more = swap(b_unit, 1 << FIRST_REST)
        a_corner = swap(a_far, NEAR)
        vec = note(vec + vec_tp)
        *s_units, a_corner, b_more = due(*s_units, a_corner, b_more)
        b_unit = rest(b_unit, b_more)
        b_units = share(b_unit)
        vec_near = swap(vec, NEAR)
        a_units = [a_unit, a_near, a_far, a_corner]
        a_sib = [swap(value, CORE) for value in turn(*a_units)]
        s_sib = [swap(value, CORE) for value in turn(*s_units)]
        up_grad, qkv_grad, out_grad = call(
            place_two_kernel,
            [((wide, 2 * hidden), F32), ((3, wide, width), F32), ((width, wide), F32)],
            [SM] + [HB] * 16,
            "place_two",
            gflop=0.01,
            scratch=vmem(
                ((8, unit_rows, hidden), BF16), ((8, unit_rows, hidden), F32),
                ((8, 2 * part_rows, 2 * width), BF16), ((8, 2 * part_rows, 2 * width), F32), sems=56,
            ),
            out_specs=[HB] * 3,
            limit=32,
        )(ids, *turn(*a_units, *a_sib, *s_units, *s_sib))
        note(out_grad)
        vec = step_with(vec, vec_near)
        vec_far = swap(vec, FAR)
        *b_units, vec_far = due(*b_units, vec_far)
        b_sib = [swap(value, CORE) for value in b_units]
        vec = vec + vec_far
        down_grad, = call(
            place_down_kernel,
            [((2 * hidden, wide), F32)],
            [SM] + [HB] * 8,
            "place_down",
            scratch=vmem(((8, unit_rows, wide), BF16), ((8, unit_rows, wide), F32), sems=16),
            out_specs=[HB],
            limit=24,
        )(ids, *b_units, *b_sib)
        one_of = lambda i: vec[i]
        qvb = lax.dynamic_slice(vec, (6, half * width), (2, width))
        ub = lax.dynamic_slice(vec, (8 + 2 * half, 0), (2, hidden)).reshape(2 * hidden)
        return (
            layer_out, in_grad, one_of(0), one_of(1), jnp.transpose(qkv_grad, (1, 0, 2)), qvb,
            out_grad, one_of(4), one_of(2), one_of(3), up_grad, ub, down_grad, one_of(5),
        )

    return on_device


def solution(mesh):
    tokens, vector = P(("dp", "tp"), None), P()
    in_specs = (
        tokens, P("dp", None), vector, vector, P(None, None, "tp"), P(None, "tp"), P("tp", None), vector,
        vector, vector, P(None, "tp"), P("tp"), P("tp", None), vector, tokens,
    )
    out_specs = (
        tokens, tokens, vector, vector, P(None, None, "tp"), P(None, "tp"), P("tp", None), vector,
        vector, vector, P(None, "tp"), P("tp"), P("tp", None), vector,
    )
    return jax.shard_map(build(mesh), mesh=mesh, in_specs=in_specs, out_specs=out_specs, check_vma=False)
```

```python
import math

import jax
import jax.numpy as jnp
from jax import lax
from jax.experimental import pallas as pl
from jax.experimental.pallas import tpu as pltpu
from jax.sharding import PartitionSpec as P

HEAD = 64
SEQ = 128
UNITS = 4
EPS = 1e-05
SCALE = 1.0 / math.sqrt(HEAD)
F32 = jnp.float32
BF16 = jnp.bfloat16

VM = pl.BlockSpec(memory_space=pltpu.VMEM)
SM = pl.BlockSpec(memory_space=pltpu.SMEM)
HB = pl.BlockSpec(memory_space=pl.ANY)

NEAR_FIRST, FAR_FIRST = (0, 2, 1, 3), (0, 1, 2, 3)
TP_BIT, CORE_BIT, NEAR_BIT, FAR_BIT, FIRST_REST = 0, 1, 2, 3, 4
TP, CORE, NEAR, FAR = (1 << bit for bit in (TP_BIT, CORE_BIT, NEAR_BIT, FAR_BIT))


def nn(a, b):
    return lax.dot_general(a, b, (((1,), (0,)), ((), ())), preferred_element_type=F32)


def nt(a, b):
    return lax.dot_general(a, b, (((1,), (1,)), ((), ())), preferred_element_type=F32)


def tn(a, b):
    return lax.dot_general(a, b, (((0,), (0,)), ((), ())), preferred_element_type=F32)


def normalize(values):
    center = values - jnp.mean(values, axis=-1, keepdims=True)
    inv = lax.rsqrt(jnp.mean(center * center, axis=-1, keepdims=True) + EPS)
    return center * inv, inv


def norm_back(values, grad, gain):
    normed, inv = normalize(values)
    scaled = grad * gain
    mean_g = jnp.mean(scaled, axis=-1, keepdims=True)
    mean_gn = jnp.mean(scaled * normed, axis=-1, keepdims=True)
    part = inv * (scaled - mean_g - normed * mean_gn)
    gain_sum = jnp.sum(grad * normed, axis=0, keepdims=True)
    shift_sum = jnp.sum(grad, axis=0, keepdims=True)
    return part, gain_sum, shift_sum


def row_mask(lens, row):
    at_k = lax.broadcasted_iota(jnp.int32, (SEQ, 1), 0)
    at_q = lax.broadcasted_iota(jnp.int32, (1, SEQ), 1)
    total = jnp.int32(0)
    seg_q = jnp.zeros((1, SEQ), jnp.int32)
    seg_k = jnp.zeros((SEQ, 1), jnp.int32)
    for entry in range(lens.shape[1]):
        total = total + lens[row, entry]
        seg_q = seg_q + jnp.where(at_q >= total, 1, 0)
        seg_k = seg_k + jnp.where(at_k >= total, 1, 0)
    allowed = (seg_q == seg_k) & (at_k <= at_q) & ((at_k < total) | (at_k == at_q))
    valid = jnp.where(at_k < total, 1.0, 0.0).astype(F32)
    return jnp.concatenate([allowed, allowed], axis=1), valid


def low_lanes():
    return lax.broadcasted_iota(jnp.int32, (SEQ, 2 * HEAD), 1) < HEAD


def stack_pair(pair, low):
    zero = jnp.zeros_like(pair)
    return jnp.concatenate([jnp.where(low, pair, zero), jnp.where(low, zero, pair)], axis=0)


def pair_probs(q_stack, keys, allowed2):
    scores = jnp.where(allowed2, nt(keys, q_stack) * SCALE, -1e30)
    weights = jnp.exp(scores - jnp.max(scores, axis=0, keepdims=True))
    return weights * (1.0 / jnp.sum(weights, axis=0, keepdims=True))


class Copies:
    def __init__(self, sems):
        self.sems = sems
        self.count = 0

    def start(self, src, dst):
        made = pltpu.make_async_copy(src, dst, self.sems.at[self.count])
        self.count += 1
        made.start()
        return made


def wait(*copies):
    for made in copies:
        made.wait()


def blocks(count, size=SEQ):
    return [slice(i * size, (i + 1) * size) for i in range(count)]


def over_rows(tokens, body, start):
    at = lambda i: pl.ds(pl.multiple_of(i * SEQ, SEQ), SEQ)
    return lax.fori_loop(0, tokens // SEQ, lambda i, carry: body(at(i), carry), start)


def project(nrm, w, bias, qkv):
    width = w.shape[2]
    for part in range(3):
        value = nn(nrm[...], w[part])
        if part != 1:
            value = value + bias[part // 2]
        qkv[:, part * width : (part + 1) * width] = value.astype(BF16)


def attend(lens, ids, qkv, att):
    width = att.shape[1]
    rows = att.shape[0] // SEQ
    low = low_lanes()
    @pl.loop(0, rows, unroll=2)
    def _(row):
        at = pl.ds(pl.multiple_of(row * SEQ, SEQ), SEQ)
        allowed2, valid = row_mask(lens, ids[0] * rows + row)
        for first in range(0, width, 2 * HEAD):
            q = qkv[at, first : first + 2 * HEAD]
            k = qkv[at, width + first : width + first + 2 * HEAD]
            v = qkv[at, 2 * width + first : 2 * width + first + 2 * HEAD]
            probs = pair_probs(stack_pair(q, low), k, allowed2)
            both = tn(probs.astype(BF16), v)
            out = jnp.where(low, both[:SEQ], both[SEQ:]) * valid
            att[at, first : first + 2 * HEAD] = out.astype(BF16)


def own_fwd_kernel(lens, ids, x_hbm, vecs, w_hbm, bias, nrm_hbm, qkv_hbm, att, x, w, nrm, qkv, sems):
    copies = Copies(sems)
    x_in = copies.start(x_hbm, x)
    w_in = copies.start(w_hbm, w)
    wait(x_in)

    def norm_rows(at, carry):
        normed, _ = normalize(x[at, :].astype(F32))
        nrm[at, :] = (normed * vecs[0:1, :] + vecs[1:2, :]).astype(BF16)
        return carry

    over_rows(x.shape[0], norm_rows, 0)
    nrm_out = copies.start(nrm, nrm_hbm)
    wait(w_in)
    project(nrm, w, [bias[0:1, :], bias[1:2, :]], qkv)
    qkv_out = copies.start(qkv, qkv_hbm)
    attend(lens, ids, qkv, att)
    wait(nrm_out, qkv_out)


def unit_block(part, rows, width, first=0):
    return pl.ds(first + (part // 2) * rows, rows), pl.ds((part % 2) * width, width)


def fetch_weights(copies, ids, mine_parts, sib_parts, w, wo):
    core, mine = ids[1], ids[2]
    width = w.shape[2]
    part_rows = w.shape[1] // (2 * UNITS)
    to_w, to_wo = [], []
    for side, parts in ((core, mine_parts), (1 - core, sib_parts)):
        for step, unit_ref in enumerate(parts):
            unit = jnp.bitwise_xor(mine, step)
            at_w = pl.ds(pl.multiple_of((side * UNITS + unit) * part_rows, part_rows), part_rows)
            at_o = pl.ds(pl.multiple_of(unit * part_rows, part_rows), part_rows)
            cols = pl.ds(pl.multiple_of(side * width, width), width)
            for part in range(3):
                to_w.append(copies.start(unit_ref.at[unit_block(part, part_rows, width)], w.at[part, at_w, :]))
            if wo is not None:
                to_wo.append(copies.start(unit_ref.at[unit_block(3, part_rows, width)], wo.at[at_o, cols]))
    return to_w, to_wo


def fetch_output_weight(copies, ids, mine_parts, sib_parts, wo):
    core, mine = ids[1], ids[2]
    width = wo.shape[0]
    part_rows = width // UNITS
    made = []
    for side, parts in ((core, mine_parts), (1 - core, sib_parts)):
        for step, unit_ref in enumerate(parts):
            at_o = pl.ds(pl.multiple_of(jnp.bitwise_xor(mine, step) * part_rows, part_rows), part_rows)
            cols = pl.ds(pl.multiple_of(side * width, width), width)
            made.append(copies.start(unit_ref.at[unit_block(3, part_rows, width)], wo.at[at_o, cols]))
    return made


def other_fwd_kernel(lens, ids, x_hbm, nrm_hbm, bias, att_own_hbm, wo_own_hbm, vecs, *refs):
    mine_parts, sib_parts = refs[:4], refs[4:8]
    qkv_hbm, att_hbm, mid_hbm, nm = refs[8:12]
    x, nrm, att_own, wo_own, w, wo, qkv, att, mid, sems = refs[12:]
    copies = Copies(sems)
    nrm_in = copies.start(nrm_hbm, nrm)
    to_w, to_wo = fetch_weights(copies, ids, mine_parts, sib_parts, w, wo)
    late = [copies.start(x_hbm, x), copies.start(att_own_hbm, att_own), copies.start(wo_own_hbm, wo_own)]
    wait(nrm_in, *to_w)
    half = w.shape[2]
    project(nrm, w, [bias[0:1, :half], bias[0:1, half:]], qkv)
    qkv_out = copies.start(qkv, qkv_hbm)
    attend(lens, ids, qkv, att)
    att_out = copies.start(att, att_hbm)
    wait(*to_wo, *late)
    mid[...] = nn(att_own[...], wo_own[...]) + nn(att[...], wo[...])

    def norm_rows(at, carry):
        value = x[at, :].astype(F32) + mid[at, :] + vecs[2:3, :]
        mid[at, :] = value
        normed, _ = normalize(value)
        nm[at, :] = (normed * vecs[3:4, :] + vecs[4:5, :]).astype(BF16)
        return carry

    over_rows(x.shape[0], norm_rows, 0)
    mid_out = copies.start(mid, mid_hbm)
    wait(qkv_out, att_out, mid_out)


def gelu_parts(pre):
    bell = jnp.exp(-0.5 * pre * pre)
    t = 1.0 / (1.0 + (0.3275911 * math.sqrt(0.5)) * jnp.abs(pre))
    poly = 0.5307027145 * t - 0.7265760135
    poly = poly * t + 0.7107068705
    poly = poly * t - 0.142248368
    poly = poly * t + 0.127414796
    tail = poly * t * bell
    cdf = jnp.where(pre >= 0, 1.0 - tail, tail)
    return pre * cdf, cdf + pre * bell * (1.0 / math.sqrt(2.0 * math.pi))


def mlp_kernel(own, *refs):
    ids, nm_a, nm_b, ct_a, ct_b, biases = refs[:6]
    if own:
        up_hbm, down_hbm = refs[6:8]
        out_hbm, dnm_hbm, keep_a, send_a, keep_b, send_b, bias_g = refs[8:15]
        scratch = refs[15:]
    else:
        units, (out_prev, dnm_prev) = refs[6:10], refs[10:12]
        out_own_hbm, out_sib_hbm, dnm_own_hbm, dnm_sib_hbm, keep_a, send_a, keep_b, send_b, bias_g = refs[12:21]
        scratch = refs[21:]
    up, down, nm, ct, pre, dact, act, pg, gu, gd, sems = scratch[:11]
    core, mine = ids[1], ids[2]
    hidden = up.shape[1]
    tokens = nm_a.shape[0]
    unit_rows = up.shape[0] // UNITS
    copies = Copies(sems)
    copy = copies.start
    halves = (pl.ds(0, tokens), pl.ds(tokens, tokens))

    def unit_at(step):
        start = jnp.bitwise_xor(mine, step) * unit_rows
        return pl.ds(pl.multiple_of(start, unit_rows), unit_rows)

    at = pl.ds(pl.multiple_of(core * hidden, hidden), hidden)
    if own:
        ups = [copy(up_hbm.at[:, at], up)]
    else:
        ups = [copy(unit.at[pl.ds(0, unit_rows)], up.at[unit_at(i), :]) for i, unit in enumerate(units)]
    nms = [copy(nm_a, nm.at[halves[0]])]
    if own:
        downs = [copy(down_hbm.at[at, :], down)]
    else:
        downs = [copy(unit.at[pl.ds(unit_rows, unit_rows)], down.at[unit_at(i), :]) for i, unit in enumerate(units)]
    cts = [copy(ct_a, ct.at[halves[0]])]
    nms.append(copy(nm_b, nm.at[halves[1]]))
    cts.append(copy(ct_b, ct.at[halves[1]]))
    if not own:
        prev_out, prev_dnm, dnm_own, dnm_sib, out_own, out_sib = scratch[11:17]
        lates = [copy(dnm_prev, prev_dnm), copy(out_prev, prev_out)]
    else:
        dnm, out = scratch[11:13]

    piece = 32

    def half_step(half, total):
        rows = pl.ds(pl.multiple_of(half * tokens, tokens), tokens)
        for i in range(2):
            pl.when(half == i)(lambda: wait(nms[i], *(ups if i == 0 else ())))
        pre[...] = nn(nm[rows, :], up[...])
        for i in range(2):
            pl.when(half == i)(lambda: wait(cts[i], *(downs if i == 0 else ())))
        dact[...] = nt(ct[rows, :], down[...])

        def elementwise(step, total):
            at = pl.ds(pl.multiple_of(step * piece, piece), piece)
            to = pl.ds(pl.multiple_of(half * tokens + step * piece, piece), piece)
            value, slope = gelu_parts(pre[at, :] + bias)
            act[to, :] = value.astype(BF16)
            back = (dact[at, :] * slope).astype(BF16)
            pg[to, :] = back
            return total + jnp.sum(back.astype(F32), axis=0, keepdims=True)

        return lax.fori_loop(0, tokens // piece, elementwise, total)

    bias = biases[pl.ds((6 if own else 1 + core), 1), :]
    bias_sum = lax.fori_loop(0, 2, half_step, jnp.zeros((1, hidden), F32))
    bias_g[...] = bias_sum
    writes = []
    if own:
        dnm[...] = nt(pg[...], up[...]).astype(BF16)
        writes.append(copy(dnm, dnm_hbm))
        out[...] = nn(act[...], down[...]).astype(BF16)
        writes.append(copy(out, out_hbm))
    else:
        wait(*lates)
        total = nt(pg[...], up[...])
        dnm_own[...] = total[:tokens] + prev_dnm[:tokens, :].astype(F32)
        dnm_sib[...] = (total[tokens:] + prev_dnm[tokens:, :].astype(F32)).astype(BF16)
        writes += [copy(dnm_own, dnm_own_hbm), copy(dnm_sib, dnm_sib_hbm)]
        total = nn(act[...], down[...])
        out_own[...] = total[:tokens] + prev_out[:tokens, :].astype(F32)
        out_sib[...] = (total[tokens:] + prev_out[tokens:, :].astype(F32)).astype(BF16)
        writes += [copy(out_own, out_own_hbm), copy(out_sib, out_sib_hbm)]
    for source, grad, order, targets in (
        (gd, lambda: tn(act[...], ct[...]), NEAR_FIRST, (keep_b, send_b)),
        (gu, lambda: tn(nm[...], pg[...]), NEAR_FIRST, (keep_a, send_a)),
    ):
        source[...] = grad().astype(BF16)
        for place, step in enumerate(order):
            to = targets[place // 2].at[pl.ds((place % 2) * unit_rows, unit_rows)]
            writes.append(copy(source.at[unit_at(step), :], to))
    wait(*writes)


def attend_back(lens, ids, qkv, datt, dqkv):
    width = datt.shape[1]
    rows = datt.shape[0] // SEQ
    low = low_lanes()

    @pl.loop(0, rows)
    def _(row):
        allowed2, valid = row_mask(lens, ids[0] * rows + row)
        at = pl.ds(pl.multiple_of(row * SEQ, SEQ), SEQ)
        for first in range(0, width, 2 * HEAD):
            q_cols = slice(first, first + 2 * HEAD)
            k_cols = slice(width + first, width + first + 2 * HEAD)
            v_cols = slice(2 * width + first, 2 * width + first + 2 * HEAD)
            k = qkv[at, k_cols]
            q_stack = stack_pair(qkv[at, q_cols], low)
            grad = (datt[at, q_cols].astype(F32) * valid).astype(BF16)
            g_stack = stack_pair(grad, low)
            probs = pair_probs(q_stack, k, allowed2)
            dqkv[at, v_cols] = nn(probs.astype(BF16), g_stack).astype(BF16)
            prob_grad = nt(qkv[at, v_cols], g_stack)
            inner = jnp.sum(probs * prob_grad, axis=0, keepdims=True)
            score_grad = (probs * (prob_grad - inner)).astype(BF16)
            both = tn(score_grad, k)
            dqkv[at, q_cols] = (jnp.where(low, both[:SEQ], both[SEQ:]) * SCALE).astype(BF16)
            dqkv[at, k_cols] = (nn(score_grad, q_stack) * SCALE).astype(BF16)


def weight_grads(copies, ids, nrm, dqkv, dw, dwo, order, keep, send):
    core, mine = ids[1], ids[2]
    width = dw.shape[2]
    part_rows = dw.shape[1] // (2 * UNITS)
    made = []
    for part in (3, 2, 1, 0):
        if part < 3:
            dw[part] = tn(nrm[...], dqkv[:, part * width : (part + 1) * width]).astype(BF16)
        for place in range(UNITS):
            unit = jnp.bitwise_xor(mine, order[place])
            for side, target in ((1 - core, send), (core, keep)):
                at_w = pl.ds(pl.multiple_of((side * UNITS + unit) * part_rows, part_rows), part_rows)
                at_o = pl.ds(pl.multiple_of(unit * part_rows, part_rows), part_rows)
                cols = pl.ds(pl.multiple_of(side * width, width), width)
                source = dw.at[part, at_w, :] if part < 3 else dwo.at[at_o, cols]
                made.append(copies.start(source, target.at[unit_block(part, part_rows, width, 2 * place * part_rows)]))
    return made


def bias_sums(dqkv):
    width = dqkv.shape[1] // 3
    ones = jnp.ones((8, dqkv.shape[0]), BF16)
    return [nn(ones, dqkv[:, first : first + width])[0:1] for first in (0, 2 * width)]


def normed_grad(dqkv, w):
    width = w.shape[2]
    total = nt(dqkv[:, :width], w[0])
    for part in range(1, 3):
        total = total + nt(dqkv[:, part * width : (part + 1) * width], w[part])
    return total


def other_back_kernel(lens, ids, dnm_own_hbm, dnm_sib_hbm, ct_hbm, mid_hbm, vecs, qkv_hbm, att_hbm, nrm_hbm, *refs):
    mine_parts, sib_parts = refs[:4], refs[4:8]
    mg_hbm, dqkv_hbm, keep, send, sums = refs[8:13]
    dnm_own, dnm_sib, ct, mid, qkv, att, nrm, wo, mg, ml, datt, dqkv, dw, dwo, sems = refs[13:]
    copies = Copies(sems)
    first_in = [
        copies.start(dnm_own_hbm, dnm_own), copies.start(dnm_sib_hbm, dnm_sib),
        copies.start(ct_hbm, ct), copies.start(mid_hbm, mid),
    ]
    to_wo = fetch_output_weight(copies, ids, mine_parts, sib_parts, wo)
    qkv_in, att_in, nrm_in = copies.start(qkv_hbm, qkv), copies.start(att_hbm, att), copies.start(nrm_hbm, nrm)
    wait(*first_in)

    def back_rows(at, totals):
        grad = dnm_own[at, :] + dnm_sib[at, :].astype(F32)
        part, gain_sum, shift_sum = norm_back(mid[at, :], grad, vecs[3:4, :])
        out_grad = ct[at, :].astype(F32)
        value = out_grad + part
        mg[at, :] = value
        ml[at, :] = value.astype(BF16)
        adds = (gain_sum, shift_sum, jnp.sum(value, axis=0, keepdims=True), jnp.sum(out_grad, axis=0, keepdims=True))
        return tuple(total + add for total, add in zip(totals, adds))

    totals = over_rows(mid.shape[0], back_rows, (jnp.zeros((1, mid.shape[1]), F32),) * 4)
    sums[...] = jnp.concatenate(list(totals) + [jnp.zeros((4, mid.shape[1]), F32)])
    mg_out = copies.start(mg, mg_hbm)
    wait(*to_wo, qkv_in, att_in)
    datt[...] = nt(ml[...], wo[...]).astype(BF16)
    dwo[...] = tn(att[...], ml[...]).astype(BF16)
    attend_back(lens, ids, qkv, datt, dqkv)
    wait(nrm_in)
    dqkv_out = copies.start(dqkv, dqkv_hbm)
    outs = weight_grads(copies, ids, nrm, dqkv, dw, dwo, NEAR_FIRST, keep, send)
    wait(mg_out, dqkv_out, *outs)


def own_back_kernel(
    lens, ids, mg_hbm, wo_hbm, qkv_hbm, att_hbm, nrm_hbm, dqkv_hbm, keep, send,
    mg, wo, qkv, att, nrm, ml, datt, dqkv, dw, dwo, sems,
):
    copies = Copies(sems)
    mg_in, wo_in = copies.start(mg_hbm, mg), copies.start(wo_hbm, wo)
    att_in, qkv_in, nrm_in = copies.start(att_hbm, att), copies.start(qkv_hbm, qkv), copies.start(nrm_hbm, nrm)
    wait(mg_in)
    ml[...] = mg[...].astype(BF16)
    wait(wo_in, att_in, qkv_in)
    datt[...] = nt(ml[...], wo[...]).astype(BF16)
    dwo[...] = tn(att[...], ml[...]).astype(BF16)
    attend_back(lens, ids, qkv, datt, dqkv)
    dqkv_out = copies.start(dqkv, dqkv_hbm)
    wait(nrm_in)
    outs = weight_grads(copies, ids, nrm, dqkv, dw, dwo, NEAR_FIRST, keep, send)
    wait(dqkv_out, *outs)


def input_grad_kernel(ids, dqkv_a_hbm, dqkv_b_hbm, mg_hbm, x_hbm, vecs, w_hbm, sums, ub_own, ub_other, *refs):
    mine_parts, sib_parts = refs[:4], refs[4:8]
    in_grad, vec = refs[8:10]
    dqkv_a, dqkv_b, mg, x, w_own, w_other, dn, sems = refs[10:]
    half, core = ids[0], ids[1]
    copies = Copies(sems)
    own_in = [copies.start(dqkv_a_hbm, dqkv_a), copies.start(w_hbm, w_own)]
    other_in, _ = fetch_weights(copies, ids, mine_parts, sib_parts, w_other, None)
    other_in.append(copies.start(dqkv_b_hbm, dqkv_b))
    late = [copies.start(mg_hbm, mg), copies.start(x_hbm, x)]
    width = w_own.shape[2]
    wait(*own_in)
    dn[...] = normed_grad(dqkv_a, w_own)
    wait(*other_in)
    dn[...] += normed_grad(dqkv_b, w_other)
    wait(*late)

    def back_rows(at, totals):
        part, gain_sum, shift_sum = norm_back(x[at, :].astype(F32), dn[at, :], vecs[0:1, :])
        in_grad[at, :] = (mg[at, :] + part).astype(BF16)
        return totals[0] + gain_sum, totals[1] + shift_sum

    totals = over_rows(x.shape[0], back_rows, (jnp.zeros((1, x.shape[1]), F32),) * 2)
    vec[...] = jnp.zeros_like(vec)
    for i in range(2):
        vec[i : i + 1, :] = totals[i]
    vec[2:6, :] = sums[0:4, :]
    for dqkv, side in ((dqkv_a, half), (dqkv_b, 1 - half)):
        for i, value in enumerate(bias_sums(dqkv)):
            vec[6 + i : 7 + i, pl.ds(pl.multiple_of(side * width, width), width)] = value
    vec[pl.ds(8 + 2 * half + core, 1), :] = ub_own[...]
    vec[pl.ds(8 + 2 * (1 - half) + core, 1), :] = ub_other[...]


def layer_out_kernel(mid_hbm, own_hbm, sib_hbm, vecs, out, mid, own, sib, sems):
    copies = Copies(sems)
    wait(copies.start(mid_hbm, mid), copies.start(own_hbm, own), copies.start(sib_hbm, sib))

    def rows(at, carry):
        out[at, :] = (mid[at, :] + own[at, :] + sib[at, :].astype(F32) + vecs[5:6, :]).astype(BF16)
        return carry

    over_rows(out.shape[0], rows, 0)


class Placing:
    def __init__(self, ids, copies):
        self.core, self.mine = ids[1], ids[2]
        self.copies = copies
        self.work, self.outs = [], []

    def take(self, refs, narrow, wide, targets):
        for i, ref in enumerate(refs):
            side = self.core if i < UNITS else 1 - self.core
            unit = jnp.bitwise_xor(self.mine, i % UNITS)
            self.work.append((self.copies.start(ref, narrow.at[i]), narrow, wide, i, targets(side, unit)))

    def finish(self):
        for arrived, narrow, wide, i, targets in self.work:
            arrived.wait()
            wide[i] = narrow[i].astype(F32)
            for block, target in targets:
                self.outs.append(self.copies.start(wide.at[i, block[0], block[1]], target))
        wait(*self.outs)


def mlp_targets(out, down_first, rows, width):
    def targets(side, unit):
        base, start = pl.multiple_of(side * width, width), pl.multiple_of(unit * rows, rows)
        if down_first:
            target = out.at[pl.ds(pl.multiple_of(base + start, rows), rows), :]
        else:
            target = out.at[pl.ds(start, rows), pl.ds(base, width)]
        return [((pl.ds(0, rows), pl.ds(0, width)), target)]

    return targets


def attn_targets(w, wo):
    width = w.shape[2]
    rows = w.shape[1] // (2 * UNITS)

    def targets(side, unit):
        at_w = pl.ds(pl.multiple_of((side * UNITS + unit) * rows, rows), rows)
        at_o = pl.ds(pl.multiple_of(unit * rows, rows), rows)
        cols = pl.ds(pl.multiple_of(side * width, width), width)
        places = [w.at[part, at_w, :] for part in range(3)] + [wo.at[at_o, cols]]
        return [(unit_block(part, rows, width), place) for part, place in enumerate(places)]

    return targets


def place_mlp_kernel(down_first, ids, *refs):
    units, (out, narrow, wide, sems) = refs[:8], refs[8:]
    placing = Placing(ids, Copies(sems))
    placing.take(units, narrow, wide, mlp_targets(out, down_first, *units[0].shape))
    placing.finish()


def place_down_kernel(*refs):
    place_mlp_kernel(True, *refs)


def place_two_kernel(ids, *refs):
    up_units, attn_units = refs[:8], refs[8:16]
    up, w, wo, narrow_u, wide_u, narrow_a, wide_a, sems = refs[16:]
    placing = Placing(ids, Copies(sems))
    placing.take(up_units, narrow_u, wide_u, mlp_targets(up, False, *up_units[0].shape))
    placing.take(attn_units, narrow_a, wide_a, attn_targets(w, wo))
    placing.finish()


def vmem(*buffers, sems):
    return [pltpu.VMEM(shape, dtype) for shape, dtype in buffers] + [pltpu.SemaphoreType.DMA((sems,))]


def call(kernel, outs, in_specs, name, scratch=(), out_specs=None, limit=60, gflop=1.0):
    return pl.pallas_call(
        kernel,
        out_shape=tuple(jax.ShapeDtypeStruct(shape, dtype) for shape, dtype in outs),
        in_specs=in_specs,
        out_specs=tuple(VM for _ in outs) if out_specs is None else tuple(out_specs),
        scratch_shapes=list(scratch),
        name=name,
        cost_estimate=pl.CostEstimate(flops=int(gflop * 1e9), bytes_accessed=8 << 20, transcendentals=0),
        compiler_params=pltpu.CompilerParams(vmem_limit_bytes=limit * 1024 * 1024),
    )


def build(mesh):
    devices = mesh.shape["dp"] * mesh.shape["tp"]
    bits = devices.bit_length() - 1

    def swap(value, mask):
        return lax.ppermute(value, ("dp", "tp"), [(i, i ^ mask) for i in range(devices)])

    def after(value, *deps):
        return lax.optimization_barrier((value, deps))[0]

    def share(unit):
        return [unit] + [swap(unit, mask) for mask in (NEAR, FAR, NEAR | FAR)]

    def add(*terms):
        total = terms[0].astype(F32)
        for term in terms[1:]:
            total = total + term.astype(F32)
        return total

    last = []

    def turn(*values):
        return lax.optimization_barrier((values, last[-1]))[0]

    def note(value):
        last.append(value)
        return value

    def due(*values):
        values = turn(*values)
        note(values[-1])
        return values

    def total(parts, *terms):
        cut = lambda v, part: v if part is None else v[v.shape[0] * part[0] // 4 : v.shape[0] * part[1] // 4]
        return note(add(*[cut(term, part) for term, part in zip(turn(*terms), parts)]).astype(BF16))

    def on_device(
        layer_in, lengths, attn_gain, attn_shift, qkv_weight, qv_bias, out_weight, out_bias,
        mlp_gain, mlp_shift, up_weight, up_bias, down_weight, down_bias, cotangent,
    ):
        tokens, wide = layer_in.shape
        width = qkv_weight.shape[2]
        hidden = up_weight.shape[1] // 2
        flat = lax.axis_index("dp") * 2 + lax.axis_index("tp")
        half = lax.axis_index("tp")
        core = (flat >> CORE_BIT) & 1
        mine = ((flat >> FAR_BIT) & 1) * 2 + ((flat >> NEAR_BIT) & 1)
        ids = jnp.stack([half, core, mine]).astype(jnp.int32)
        up_bias_own = lax.dynamic_slice(up_bias, (core * hidden,), (hidden,))
        vecs = jnp.stack([attn_gain, attn_shift, out_bias, mlp_gain, mlp_shift, down_bias, up_bias_own, up_bias_own])
        w_own = jnp.transpose(qkv_weight, (1, 0, 2))

        part_rows = wide // (2 * UNITS)
        unit_w = lax.dynamic_slice(w_own, (0, (core * UNITS + mine) * part_rows, 0), (3, part_rows, width))
        unit_o = lax.dynamic_slice(out_weight, (mine * part_rows, core * width), (part_rows, width))
        attn_unit = jnp.concatenate(
            [jnp.concatenate([unit_w[0], unit_w[1]], axis=1), jnp.concatenate([unit_w[2], unit_o], axis=1)]
        )
        attn_unit = swap(attn_unit, TP)

        acts = (tokens, 3 * width)
        one = (tokens, wide)
        head = (tokens, width)
        w_shape, wo_shape = (3, wide, width), (width, wide)
        nrm, qkv_own, att_own = call(
            own_fwd_kernel,
            [(one, BF16), (acts, BF16), (head, BF16)],
            [SM, SM, HB, VM, HB, VM],
            "attn_own_fwd",
            gflop=0.5,
            scratch=vmem((one, BF16), (w_shape, BF16), (one, BF16), (acts, BF16), sems=4),
            out_specs=[HB, HB, VM],
        )(lengths, ids, layer_in, vecs, w_own, qv_bias)
        attn_parts = share(after(attn_unit, att_own))
        unit_rows = hidden // UNITS
        up_late, down_late, bias_late, up_bias_late = after((up_weight, down_weight, qv_bias, up_bias), att_own)
        mlp_unit = jnp.concatenate(
            [
                lax.dynamic_slice(up_late, (mine * unit_rows, core * hidden), (unit_rows, hidden)),
                lax.dynamic_slice(down_late, (core * hidden + mine * unit_rows, 0), (unit_rows, wide)),
            ]
        )
        mlp_unit = swap(mlp_unit, TP)
        small = jnp.concatenate([bias_late.reshape(-1), up_bias_late])
        small_other = swap(small.reshape(3, wide), TP)
        ct_sib = swap(cotangent, CORE)
        attn_sib = [swap(part, CORE) for part in attn_parts]
        qkv_other, att_other, mid, nm = call(
            other_fwd_kernel,
            [(acts, BF16), (head, BF16), (one, F32), (one, BF16)],
            [SM, SM, HB, HB, VM, HB, HB, VM] + [HB] * 8,
            "attn_other_fwd",
            gflop=6,
            scratch=vmem(
                (one, BF16), (one, BF16), (head, BF16), (wo_shape, BF16), (w_shape, BF16), (wo_shape, BF16),
                (acts, BF16), (head, BF16), (one, F32), sems=40,
            ),
            out_specs=[HB, HB, HB, VM],
        )(
            lengths, ids, layer_in, after(nrm, mlp_unit), small_other, att_own, out_weight, vecs,
            *attn_parts, *attn_sib,
        )
        mlp_near, mlp_far = swap(mlp_unit, NEAR), swap(mlp_unit, FAR)

        mlp_near, mlp_far, nm = after((mlp_near, mlp_far, nm))
        mlp_parts = [mlp_unit, mlp_near, mlp_far, swap(mlp_unit, NEAR | FAR)]
        nm_sib = swap(nm, CORE)
        tall, square = (2 * tokens, wide), (wide, hidden)
        scratch = [
            (square, BF16), (square, BF16), (tall, BF16), (tall, BF16), ((tokens, hidden), F32), ((tokens, hidden), F32),
            ((2 * tokens, hidden), BF16), ((2 * tokens, hidden), BF16), (square, BF16), (square, BF16),
        ]

        def mlp_scratch(*more):
            buffers = vmem(*scratch, *more, sems=40)
            return buffers[:10] + buffers[-1:] + buffers[10:-1]

        both = (2 * tokens, wide)
        pair = (2 * unit_rows, hidden)
        out_a, dnm_a, keep_own, send_own, b_own_lo, b_own_hi, ub_own = call(
            lambda *r: mlp_kernel(True, *r),
            [(both, BF16), (both, BF16), *[(pair, BF16)] * 4, ((1, hidden), F32)],
            [SM] + [HB] * 4 + [VM] + [HB] * 2,
            "mlp_own",
            gflop=1,
            scratch=mlp_scratch((tall, BF16), (tall, BF16)),
            out_specs=[HB] * 6 + [VM],
        )(ids, nm, nm_sib, cotangent, ct_sib, vecs, up_weight, down_weight)
        out_own, out_sib, dnm_own, dnm_sib, keep_other, send_other, b_other_lo, b_other_hi, ub_other = call(
            lambda *r: mlp_kernel(False, *r),
            [
                (one, F32), (one, BF16), (one, F32), (one, BF16), *[(pair, BF16)] * 4,
                ((1, hidden), F32),
            ],
            [SM] + [HB] * 4 + [VM] + [HB] * 6,
            "mlp_other",
            gflop=12,
            scratch=mlp_scratch((tall, BF16), (tall, BF16), (one, F32), (one, BF16), (one, F32), (one, BF16)),
            out_specs=[HB] * 8 + [VM],
        )(ids, nm, nm_sib, cotangent, ct_sib, small_other, *mlp_parts, out_a, dnm_a)
        grad_units = (2 * UNITS * part_rows, 2 * width)
        whole, low_half, high_half, first, second = None, (0, 2), (2, 4), (0, 1), (1, 2)
        a_own = swap(send_own, NEAR)
        note(ub_other)
        a_own, dnm_sib, out_sib, send_other, b_other_hi, b_other_lo = turn(
            a_own, dnm_sib, out_sib, send_other, b_other_hi, b_other_lo
        )
        dnm_got = swap(dnm_sib, CORE)
        a_own2 = swap(total((high_half, high_half), keep_own, a_own), FAR)
        a_other = swap(send_other, NEAR)
        b_hi = swap(b_other_hi, TP)
        mg, dqkv_other, keep_o, send_o, sums_mid = call(
            other_back_kernel,
            [(one, F32), (acts, BF16), (grad_units, BF16), (grad_units, BF16), ((8, wide), F32)],
            [SM, SM, HB, HB, HB, HB, VM, HB, HB, HB] + [HB] * 8,
            "attn_other_back",
            gflop=10,
            scratch=vmem(
                (one, F32), (one, BF16), (one, BF16), (one, F32), (acts, BF16), (head, BF16), (one, BF16),
                (wo_shape, BF16), (one, F32), (one, BF16), (head, BF16), (acts, BF16),
                (w_shape, BF16), (wo_shape, BF16), sems=60,
            ),
            out_specs=[HB] * 4 + [VM],
        )(
            lengths, ids, dnm_own, dnm_got, cotangent, mid, vecs, qkv_other, att_other, nrm,
            *attn_parts, *attn_sib,
        )
        note(sums_mid)
        out_got = swap(turn(out_sib)[0], CORE)
        a_other, a_own2, b_hi, send_o = turn(a_other, a_own2, b_hi, send_o)
        o_sib = swap(send_o, CORE)
        a_other2 = swap(total((high_half, high_half), keep_other, a_other), FAR)
        o1 = swap(total((high_half, high_half), keep_o, o_sib), NEAR)
        b_lo = swap(b_other_lo, TP)
        mg_now, = turn(mg)
        dqkv_own, keep_s, send_s = call(
            own_back_kernel,
            [(acts, BF16), (grad_units, BF16), (grad_units, BF16)],
            [SM, SM] + [HB] * 5,
            "attn_own_back",
            gflop=10,
            scratch=vmem(
                (one, F32), (wo_shape, BF16), (acts, BF16), (head, BF16), (one, BF16),
                (one, BF16), (head, BF16), (acts, BF16), (w_shape, BF16), (wo_shape, BF16), sems=48,
            ),
            out_specs=[HB] * 3,
        )(lengths, ids, mg_now, out_weight, qkv_own, att_own, nrm)
        note(dqkv_own)
        a_other2, o1, b_lo, send_s = turn(a_other2, o1, b_lo, send_s)
        s_sib = swap(send_s, CORE)
        a_back = swap(total((low_half, low_half, whole), keep_other, a_other, a_other2), TP)
        s1 = swap(total((high_half, high_half), keep_s, s_sib), NEAR)
        o2 = swap(total((second, second, high_half), keep_o, o_sib, o1), FAR)
        b1 = swap(total((whole, whole), b_own_hi, b_hi), NEAR)
        a_unit = total((low_half, low_half, whole, whole), keep_own, a_own, a_own2, a_back)
        a_more = swap(a_unit, 1 << FIRST_REST)
        in_grad, vec = call(
            input_grad_kernel,
            [(one, BF16), ((16, wide), F32)],
            [SM, HB, HB, HB, HB, VM, HB, VM, VM, VM] + [HB] * 8,
            "input_grad",
            gflop=0.01,
            scratch=vmem(
                (acts, BF16), (acts, BF16), (one, F32), (one, BF16), (w_shape, BF16), (w_shape, BF16), (one, F32),
                sems=32,
            ),
        )(
            ids, dqkv_own, dqkv_other, *turn(mg), layer_in, vecs, w_own, sums_mid, ub_own, ub_other,
            *attn_parts, *attn_sib,
        )
        note(vec)

        def step(value, bit):
            mine, got = turn(value, swap(value, 1 << bit))
            return note(mine + got)

        def rest(unit, got):
            unit = total((whole, whole), unit, got)
            for bit in range(FIRST_REST + 1, bits):
                unit = total((whole, whole), unit, swap(unit, 1 << bit))
            return unit

        def step_with(value, got):
            mine, got = turn(value, got)
            return note(mine + got)

        s2 = swap(total((second, second, high_half), keep_s, s_sib, s1), FAR)
        o_back = swap(total((first, first, low_half, whole), keep_o, o_sib, o1, o2), TP)
        vec = step(vec, CORE_BIT)
        a_unit = rest(a_unit, a_more)
        a_near, a_far = swap(a_unit, NEAR), swap(a_unit, FAR)
        for bit in range(FIRST_REST, bits):
            vec = step(vec, bit)
        s_unit = total((first, first, low_half, whole, whole), keep_s, s_sib, s1, s2, o_back)
        s_more = swap(s_unit, 1 << FIRST_REST)
        vec_tp = swap(vec, TP)
        b2 = swap(total((high_half, high_half, high_half), b_own_lo, b_lo, b1), FAR)
        layer_out, = call(
            layer_out_kernel,
            [(one, BF16)],
            [HB, HB, HB, VM],
            "layer_out",
            gflop=0.01,
            scratch=vmem((one, F32), (one, F32), (one, BF16), sems=3),
        )(mid, out_own, *turn(out_got), vecs)
        note(layer_out)
        a_near, a_far, vec_tp, b2, s_more = due(a_near, a_far, vec_tp, b2, s_more)
        s_unit = rest(s_unit, s_more)
        s_units = share(s_unit)
        b_unit = total((low_half, low_half, low_half, whole), b_own_lo, b_lo, b1, b2)
        b_more = swap(b_unit, 1 << FIRST_REST)
        a_corner = swap(a_far, NEAR)
        vec = note(vec + vec_tp)
        *s_units, a_corner, b_more = due(*s_units, a_corner, b_more)
        b_unit = rest(b_unit, b_more)
        b_units = share(b_unit)
        vec_near = swap(vec, NEAR)
        a_units = [a_unit, a_near, a_far, a_corner]
        a_sib = [swap(value, CORE) for value in turn(*a_units)]
        s_sib = [swap(value, CORE) for value in turn(*s_units)]
        up_grad, qkv_grad, out_grad = call(
            place_two_kernel,
            [((wide, 2 * hidden), F32), ((3, wide, width), F32), ((width, wide), F32)],
            [SM] + [HB] * 16,
            "place_two",
            gflop=0.01,
            scratch=vmem(
                ((8, unit_rows, hidden), BF16), ((8, unit_rows, hidden), F32),
                ((8, 2 * part_rows, 2 * width), BF16), ((8, 2 * part_rows, 2 * width), F32), sems=56,
            ),
            out_specs=[HB] * 3,
            limit=32,
        )(ids, *turn(*a_units, *a_sib, *s_units, *s_sib))
        note(out_grad)
        vec = step_with(vec, vec_near)
        vec_far = swap(vec, FAR)
        *b_three, b_corner = b_units
        b_three = due(*b_three)
        b_sib = [swap(value, CORE) for value in b_three]
        *b_sib, vec_far, b_corner = due(*b_sib, vec_far, b_corner)
        b_sib.append(swap(b_corner, CORE))
        b_units = [*b_three, b_corner]
        vec = vec + vec_far
        down_grad, = call(
            place_down_kernel,
            [((2 * hidden, wide), F32)],
            [SM] + [HB] * 8,
            "place_down",
            scratch=vmem(((8, unit_rows, wide), BF16), ((8, unit_rows, wide), F32), sems=16),
            out_specs=[HB],
            limit=24,
        )(ids, *b_units, *b_sib)
        one_of = lambda i: vec[i]
        qvb = lax.dynamic_slice(vec, (6, half * width), (2, width))
        ub = lax.dynamic_slice(vec, (8 + 2 * half, 0), (2, hidden)).reshape(2 * hidden)
        return (
            layer_out, in_grad, one_of(0), one_of(1), jnp.transpose(qkv_grad, (1, 0, 2)), qvb,
            out_grad, one_of(4), one_of(2), one_of(3), up_grad, ub, down_grad, one_of(5),
        )

    return on_device


def solution(mesh):
    tokens, vector = P(("dp", "tp"), None), P()
    in_specs = (
        tokens, P("dp", None), vector, vector, P(None, None, "tp"), P(None, "tp"), P("tp", None), vector,
        vector, vector, P(None, "tp"), P("tp"), P("tp", None), vector, tokens,
    )
    out_specs = (
        tokens, tokens, vector, vector, P(None, None, "tp"), P(None, "tp"), P("tp", None), vector,
        vector, vector, P(None, "tp"), P("tp"), P("tp", None), vector,
    )
    return jax.shard_map(build(mesh), mesh=mesh, in_specs=in_specs, out_specs=out_specs, check_vma=False)
```

```python
import math

import jax
import jax.numpy as jnp
from jax import lax
from jax.experimental import pallas as pl
from jax.experimental.pallas import tpu as pltpu
from jax.sharding import PartitionSpec as P

HEAD = 64
SEQ = 128
UNITS = 4
EPS = 1e-05
SCALE = 1.0 / math.sqrt(HEAD)
F32 = jnp.float32
BF16 = jnp.bfloat16

VM = pl.BlockSpec(memory_space=pltpu.VMEM)
SM = pl.BlockSpec(memory_space=pltpu.SMEM)
HB = pl.BlockSpec(memory_space=pl.ANY)

NEAR_FIRST, FAR_FIRST = (0, 2, 1, 3), (0, 1, 2, 3)
TP_BIT, CORE_BIT, NEAR_BIT, FAR_BIT, FIRST_REST = 0, 1, 2, 3, 4
TP, CORE, NEAR, FAR = (1 << bit for bit in (TP_BIT, CORE_BIT, NEAR_BIT, FAR_BIT))


def nn(a, b):
    return lax.dot_general(a, b, (((1,), (0,)), ((), ())), preferred_element_type=F32)


def nt(a, b):
    return lax.dot_general(a, b, (((1,), (1,)), ((), ())), preferred_element_type=F32)


def tn(a, b):
    return lax.dot_general(a, b, (((0,), (0,)), ((), ())), preferred_element_type=F32)


def normalize(values):
    center = values - jnp.mean(values, axis=-1, keepdims=True)
    inv = lax.rsqrt(jnp.mean(center * center, axis=-1, keepdims=True) + EPS)
    return center * inv, inv


def norm_back(values, grad, gain):
    normed, inv = normalize(values)
    scaled = grad * gain
    mean_g = jnp.mean(scaled, axis=-1, keepdims=True)
    mean_gn = jnp.mean(scaled * normed, axis=-1, keepdims=True)
    part = inv * (scaled - mean_g - normed * mean_gn)
    gain_sum = jnp.sum(grad * normed, axis=0, keepdims=True)
    shift_sum = jnp.sum(grad, axis=0, keepdims=True)
    return part, gain_sum, shift_sum


def row_mask(lens, row):
    at_k = lax.broadcasted_iota(jnp.int32, (SEQ, 1), 0)
    at_q = lax.broadcasted_iota(jnp.int32, (1, SEQ), 1)
    total = jnp.int32(0)
    seg_q = jnp.zeros((1, SEQ), jnp.int32)
    seg_k = jnp.zeros((SEQ, 1), jnp.int32)
    for entry in range(lens.shape[1]):
        total = total + lens[row, entry]
        seg_q = seg_q + jnp.where(at_q >= total, 1, 0)
        seg_k = seg_k + jnp.where(at_k >= total, 1, 0)
    allowed = (seg_q == seg_k) & (at_k <= at_q) & ((at_k < total) | (at_k == at_q))
    valid = jnp.where(at_k < total, 1.0, 0.0).astype(F32)
    return jnp.concatenate([allowed, allowed], axis=1), valid


def low_lanes():
    return lax.broadcasted_iota(jnp.int32, (SEQ, 2 * HEAD), 1) < HEAD


def stack_pair(pair, low):
    zero = jnp.zeros_like(pair)
    return jnp.concatenate([jnp.where(low, pair, zero), jnp.where(low, zero, pair)], axis=0)


def pair_probs(q_stack, keys, allowed2):
    scores = jnp.where(allowed2, nt(keys, q_stack) * SCALE, -1e30)
    weights = jnp.exp(scores - jnp.max(scores, axis=0, keepdims=True))
    return weights * (1.0 / jnp.sum(weights, axis=0, keepdims=True))


class Copies:
    def __init__(self, sems):
        self.sems = sems
        self.count = 0

    def start(self, src, dst):
        made = pltpu.make_async_copy(src, dst, self.sems.at[self.count])
        self.count += 1
        made.start()
        return made


def wait(*copies):
    for made in copies:
        made.wait()


def blocks(count, size=SEQ):
    return [slice(i * size, (i + 1) * size) for i in range(count)]


def over_rows(tokens, body, start):
    at = lambda i: pl.ds(pl.multiple_of(i * SEQ, SEQ), SEQ)
    return lax.fori_loop(0, tokens // SEQ, lambda i, carry: body(at(i), carry), start)


def project(nrm, w, bias, qkv):
    width = w.shape[2]
    for part in range(3):
        value = nn(nrm[...], w[part])
        if part != 1:
            value = value + bias[part // 2]
        qkv[:, part * width : (part + 1) * width] = value.astype(BF16)


def attend(lens, ids, qkv, att):
    width = att.shape[1]
    rows = att.shape[0] // SEQ
    low = low_lanes()
    @pl.loop(0, rows, unroll=2)
    def _(row):
        at = pl.ds(pl.multiple_of(row * SEQ, SEQ), SEQ)
        allowed2, valid = row_mask(lens, ids[0] * rows + row)
        for first in range(0, width, 2 * HEAD):
            q = qkv[at, first : first + 2 * HEAD]
            k = qkv[at, width + first : width + first + 2 * HEAD]
            v = qkv[at, 2 * width + first : 2 * width + first + 2 * HEAD]
            probs = pair_probs(stack_pair(q, low), k, allowed2)
            both = tn(probs.astype(BF16), v)
            out = jnp.where(low, both[:SEQ], both[SEQ:]) * valid
            att[at, first : first + 2 * HEAD] = out.astype(BF16)


def own_fwd_kernel(lens, ids, x_hbm, vecs, w_hbm, bias, nrm_hbm, qkv_hbm, att, x, w, nrm, qkv, sems):
    copies = Copies(sems)
    x_in = copies.start(x_hbm, x)
    w_in = copies.start(w_hbm, w)
    wait(x_in)

    def norm_rows(at, carry):
        normed, _ = normalize(x[at, :].astype(F32))
        nrm[at, :] = (normed * vecs[0:1, :] + vecs[1:2, :]).astype(BF16)
        return carry

    over_rows(x.shape[0], norm_rows, 0)
    nrm_out = copies.start(nrm, nrm_hbm)
    wait(w_in)
    project(nrm, w, [bias[0:1, :], bias[1:2, :]], qkv)
    qkv_out = copies.start(qkv, qkv_hbm)
    attend(lens, ids, qkv, att)
    wait(nrm_out, qkv_out)


def unit_block(part, rows, width, first=0):
    return pl.ds(first + (part // 2) * rows, rows), pl.ds((part % 2) * width, width)


def fetch_weights(copies, ids, mine_parts, sib_parts, w, wo):
    core, mine = ids[1], ids[2]
    width = w.shape[2]
    part_rows = w.shape[1] // (2 * UNITS)
    to_w, to_wo = [], []
    for side, parts in ((core, mine_parts), (1 - core, sib_parts)):
        for step, unit_ref in enumerate(parts):
            unit = jnp.bitwise_xor(mine, step)
            at_w = pl.ds(pl.multiple_of((side * UNITS + unit) * part_rows, part_rows), part_rows)
            at_o = pl.ds(pl.multiple_of(unit * part_rows, part_rows), part_rows)
            cols = pl.ds(pl.multiple_of(side * width, width), width)
            for part in range(3):
                to_w.append(copies.start(unit_ref.at[unit_block(part, part_rows, width)], w.at[part, at_w, :]))
            if wo is not None:
                to_wo.append(copies.start(unit_ref.at[unit_block(3, part_rows, width)], wo.at[at_o, cols]))
    return to_w, to_wo


def fetch_output_weight(copies, ids, mine_parts, sib_parts, wo):
    core, mine = ids[1], ids[2]
    width = wo.shape[0]
    part_rows = width // UNITS
    made = []
    for side, parts in ((core, mine_parts), (1 - core, sib_parts)):
        for step, unit_ref in enumerate(parts):
            at_o = pl.ds(pl.multiple_of(jnp.bitwise_xor(mine, step) * part_rows, part_rows), part_rows)
            cols = pl.ds(pl.multiple_of(side * width, width), width)
            made.append(copies.start(unit_ref.at[unit_block(3, part_rows, width)], wo.at[at_o, cols]))
    return made


def other_fwd_kernel(lens, ids, x_hbm, nrm_hbm, bias, att_own_hbm, wo_own_hbm, vecs, *refs):
    mine_parts, sib_parts = refs[:4], refs[4:8]
    qkv_hbm, att_hbm, mid_hbm, nm = refs[8:12]
    x, nrm, att_own, wo_own, w, wo, qkv, att, mid, sems = refs[12:]
    copies = Copies(sems)
    nrm_in = copies.start(nrm_hbm, nrm)
    to_w, to_wo = fetch_weights(copies, ids, mine_parts, sib_parts, w, wo)
    late = [copies.start(x_hbm, x), copies.start(att_own_hbm, att_own), copies.start(wo_own_hbm, wo_own)]
    wait(nrm_in, *to_w)
    half = w.shape[2]
    project(nrm, w, [bias[0:1, :half], bias[0:1, half:]], qkv)
    qkv_out = copies.start(qkv, qkv_hbm)
    attend(lens, ids, qkv, att)
    att_out = copies.start(att, att_hbm)
    wait(*to_wo, *late)
    mid[...] = nn(att_own[...], wo_own[...]) + nn(att[...], wo[...])

    def norm_rows(at, carry):
        value = x[at, :].astype(F32) + mid[at, :] + vecs[2:3, :]
        mid[at, :] = value
        normed, _ = normalize(value)
        nm[at, :] = (normed * vecs[3:4, :] + vecs[4:5, :]).astype(BF16)
        return carry

    over_rows(x.shape[0], norm_rows, 0)
    mid_out = copies.start(mid, mid_hbm)
    wait(qkv_out, att_out, mid_out)


def gelu_parts(pre):
    bell = jnp.exp(-0.5 * pre * pre)
    t = 1.0 / (1.0 + (0.3275911 * math.sqrt(0.5)) * jnp.abs(pre))
    poly = 0.5307027145 * t - 0.7265760135
    poly = poly * t + 0.7107068705
    poly = poly * t - 0.142248368
    poly = poly * t + 0.127414796
    tail = poly * t * bell
    cdf = jnp.where(pre >= 0, 1.0 - tail, tail)
    return pre * cdf, cdf + pre * bell * (1.0 / math.sqrt(2.0 * math.pi))


def mlp_kernel(own, *refs):
    ids, nm_a, nm_b, ct_a, ct_b, biases = refs[:6]
    if own:
        up_hbm, down_hbm = refs[6:8]
        out_hbm, dnm_hbm, keep_a, send_a, keep_b, send_b, bias_g = refs[8:15]
        scratch = refs[15:]
    else:
        units, (out_prev, dnm_prev) = refs[6:10], refs[10:12]
        out_own_hbm, out_sib_hbm, dnm_own_hbm, dnm_sib_hbm, keep_a, send_a, keep_b, send_b, bias_g = refs[12:21]
        scratch = refs[21:]
    up, down, nm, ct, pre, dact, act, pg, gu, gd, sems = scratch[:11]
    core, mine = ids[1], ids[2]
    hidden = up.shape[1]
    tokens = nm_a.shape[0]
    unit_rows = up.shape[0] // UNITS
    copies = Copies(sems)
    copy = copies.start
    halves = (pl.ds(0, tokens), pl.ds(tokens, tokens))

    def unit_at(step):
        start = jnp.bitwise_xor(mine, step) * unit_rows
        return pl.ds(pl.multiple_of(start, unit_rows), unit_rows)

    at = pl.ds(pl.multiple_of(core * hidden, hidden), hidden)
    if own:
        ups = [copy(up_hbm.at[:, at], up)]
    else:
        ups = [copy(unit.at[pl.ds(0, unit_rows)], up.at[unit_at(i), :]) for i, unit in enumerate(units)]
    nms = [copy(nm_a, nm.at[halves[0]])]
    if own:
        downs = [copy(down_hbm.at[at, :], down)]
    else:
        downs = [copy(unit.at[pl.ds(unit_rows, unit_rows)], down.at[unit_at(i), :]) for i, unit in enumerate(units)]
    cts = [copy(ct_a, ct.at[halves[0]])]
    nms.append(copy(nm_b, nm.at[halves[1]]))
    cts.append(copy(ct_b, ct.at[halves[1]]))
    if not own:
        prev_out, prev_dnm, dnm_own, dnm_sib, out_own, out_sib = scratch[11:17]
        lates = [copy(dnm_prev, prev_dnm), copy(out_prev, prev_out)]
    else:
        dnm, out = scratch[11:13]

    piece = 32

    def half_step(half, total):
        rows = pl.ds(pl.multiple_of(half * tokens, tokens), tokens)
        for i in range(2):
            pl.when(half == i)(lambda: wait(nms[i], *(ups if i == 0 else ())))
        pre[...] = nn(nm[rows, :], up[...])
        for i in range(2):
            pl.when(half == i)(lambda: wait(cts[i], *(downs if i == 0 else ())))
        dact[...] = nt(ct[rows, :], down[...])

        def elementwise(step, total):
            at = pl.ds(pl.multiple_of(step * piece, piece), piece)
            to = pl.ds(pl.multiple_of(half * tokens + step * piece, piece), piece)
            value, slope = gelu_parts(pre[at, :] + bias)
            act[to, :] = value.astype(BF16)
            back = dact[at, :] * slope
            pg[to, :] = back.astype(BF16)
            return total + jnp.sum(back.reshape(piece // 8, 8, hidden), axis=0)

        return lax.fori_loop(0, tokens // piece, elementwise, total)

    bias = biases[pl.ds((6 if own else 1 + core), 1), :]
    bias_sum = lax.fori_loop(0, 2, half_step, jnp.zeros((8, hidden), F32))
    bias_g[...] = jnp.sum(bias_sum, axis=0, keepdims=True)
    writes = []
    if own:
        dnm[...] = nt(pg[...], up[...]).astype(BF16)
        writes.append(copy(dnm, dnm_hbm))
        out[...] = nn(act[...], down[...]).astype(BF16)
        writes.append(copy(out, out_hbm))
    else:
        wait(*lates)
        total = nt(pg[...], up[...])
        dnm_own[...] = total[:tokens] + prev_dnm[:tokens, :].astype(F32)
        dnm_sib[...] = (total[tokens:] + prev_dnm[tokens:, :].astype(F32)).astype(BF16)
        writes += [copy(dnm_own, dnm_own_hbm), copy(dnm_sib, dnm_sib_hbm)]
        total = nn(act[...], down[...])
        out_own[...] = total[:tokens] + prev_out[:tokens, :].astype(F32)
        out_sib[...] = (total[tokens:] + prev_out[tokens:, :].astype(F32)).astype(BF16)
        writes += [copy(out_own, out_own_hbm), copy(out_sib, out_sib_hbm)]
    for source, grad, order, targets in (
        (gd, lambda: tn(act[...], ct[...]), NEAR_FIRST, (keep_b, send_b)),
        (gu, lambda: tn(nm[...], pg[...]), NEAR_FIRST, (keep_a, send_a)),
    ):
        source[...] = grad().astype(BF16)
        for place, step in enumerate(order):
            to = targets[place // 2].at[pl.ds((place % 2) * unit_rows, unit_rows)]
            writes.append(copy(source.at[unit_at(step), :], to))
    wait(*writes)


def attend_back(lens, ids, qkv, datt, dqkv):
    width = datt.shape[1]
    rows = datt.shape[0] // SEQ
    low = low_lanes()

    @pl.loop(0, rows)
    def _(row):
        allowed2, valid = row_mask(lens, ids[0] * rows + row)
        at = pl.ds(pl.multiple_of(row * SEQ, SEQ), SEQ)
        for first in range(0, width, 2 * HEAD):
            q_cols = slice(first, first + 2 * HEAD)
            k_cols = slice(width + first, width + first + 2 * HEAD)
            v_cols = slice(2 * width + first, 2 * width + first + 2 * HEAD)
            k = qkv[at, k_cols]
            q_stack = stack_pair(qkv[at, q_cols], low)
            grad = (datt[at, q_cols].astype(F32) * valid).astype(BF16)
            g_stack = stack_pair(grad, low)
            probs = pair_probs(q_stack, k, allowed2)
            dqkv[at, v_cols] = nn(probs.astype(BF16), g_stack).astype(BF16)
            prob_grad = nt(qkv[at, v_cols], g_stack)
            inner = jnp.sum(probs * prob_grad, axis=0, keepdims=True)
            score_grad = (probs * (prob_grad - inner)).astype(BF16)
            both = tn(score_grad, k)
            dqkv[at, q_cols] = (jnp.where(low, both[:SEQ], both[SEQ:]) * SCALE).astype(BF16)
            dqkv[at, k_cols] = (nn(score_grad, q_stack) * SCALE).astype(BF16)


def weight_grads(copies, ids, nrm, dqkv, dw, dwo, order, keep, send):
    core, mine = ids[1], ids[2]
    width = dw.shape[2]
    part_rows = dw.shape[1] // (2 * UNITS)
    made = []
    for part in (3, 2, 1, 0):
        if part < 3:
            dw[part] = tn(nrm[...], dqkv[:, part * width : (part + 1) * width]).astype(BF16)
        for place in range(UNITS):
            unit = jnp.bitwise_xor(mine, order[place])
            for side, target in ((1 - core, send), (core, keep)):
                at_w = pl.ds(pl.multiple_of((side * UNITS + unit) * part_rows, part_rows), part_rows)
                at_o = pl.ds(pl.multiple_of(unit * part_rows, part_rows), part_rows)
                cols = pl.ds(pl.multiple_of(side * width, width), width)
                source = dw.at[part, at_w, :] if part < 3 else dwo.at[at_o, cols]
                made.append(copies.start(source, target.at[unit_block(part, part_rows, width, 2 * place * part_rows)]))
    return made


def bias_sums(dqkv):
    width = dqkv.shape[1] // 3
    ones = jnp.ones((8, dqkv.shape[0]), BF16)
    return [nn(ones, dqkv[:, first : first + width])[0:1] for first in (0, 2 * width)]


def normed_grad(dqkv, w):
    width = w.shape[2]
    total = nt(dqkv[:, :width], w[0])
    for part in range(1, 3):
        total = total + nt(dqkv[:, part * width : (part + 1) * width], w[part])
    return total


def other_back_kernel(lens, ids, dnm_own_hbm, dnm_sib_hbm, ct_hbm, mid_hbm, vecs, qkv_hbm, att_hbm, nrm_hbm, *refs):
    mine_parts, sib_parts = refs[:4], refs[4:8]
    mg_hbm, dqkv_hbm, keep, send, sums = refs[8:13]
    dnm_own, dnm_sib, ct, mid, qkv, att, nrm, wo, mg, ml, datt, dqkv, dw, dwo, sems = refs[13:]
    copies = Copies(sems)
    first_in = [
        copies.start(dnm_own_hbm, dnm_own), copies.start(dnm_sib_hbm, dnm_sib),
        copies.start(ct_hbm, ct), copies.start(mid_hbm, mid),
    ]
    to_wo = fetch_output_weight(copies, ids, mine_parts, sib_parts, wo)
    qkv_in, att_in, nrm_in = copies.start(qkv_hbm, qkv), copies.start(att_hbm, att), copies.start(nrm_hbm, nrm)
    wait(*first_in)

    def back_rows(at, totals):
        grad = dnm_own[at, :] + dnm_sib[at, :].astype(F32)
        part, gain_sum, shift_sum = norm_back(mid[at, :], grad, vecs[3:4, :])
        out_grad = ct[at, :].astype(F32)
        value = out_grad + part
        mg[at, :] = value
        ml[at, :] = value.astype(BF16)
        adds = (gain_sum, shift_sum, jnp.sum(value, axis=0, keepdims=True), jnp.sum(out_grad, axis=0, keepdims=True))
        return tuple(total + add for total, add in zip(totals, adds))

    totals = over_rows(mid.shape[0], back_rows, (jnp.zeros((1, mid.shape[1]), F32),) * 4)
    sums[...] = jnp.concatenate(list(totals) + [jnp.zeros((4, mid.shape[1]), F32)])
    mg_out = copies.start(mg, mg_hbm)
    wait(*to_wo, qkv_in, att_in)
    datt[...] = nt(ml[...], wo[...]).astype(BF16)
    dwo[...] = tn(att[...], ml[...]).astype(BF16)
    attend_back(lens, ids, qkv, datt, dqkv)
    wait(nrm_in)
    dqkv_out = copies.start(dqkv, dqkv_hbm)
    outs = weight_grads(copies, ids, nrm, dqkv, dw, dwo, NEAR_FIRST, keep, send)
    wait(mg_out, dqkv_out, *outs)


def own_back_kernel(
    lens, ids, mg_hbm, wo_hbm, qkv_hbm, att_hbm, nrm_hbm, dqkv_hbm, keep, send,
    mg, wo, qkv, att, nrm, ml, datt, dqkv, dw, dwo, sems,
):
    copies = Copies(sems)
    mg_in, wo_in = copies.start(mg_hbm, mg), copies.start(wo_hbm, wo)
    att_in, qkv_in, nrm_in = copies.start(att_hbm, att), copies.start(qkv_hbm, qkv), copies.start(nrm_hbm, nrm)
    wait(mg_in)
    ml[...] = mg[...].astype(BF16)
    wait(wo_in, att_in, qkv_in)
    datt[...] = nt(ml[...], wo[...]).astype(BF16)
    dwo[...] = tn(att[...], ml[...]).astype(BF16)
    attend_back(lens, ids, qkv, datt, dqkv)
    dqkv_out = copies.start(dqkv, dqkv_hbm)
    wait(nrm_in)
    outs = weight_grads(copies, ids, nrm, dqkv, dw, dwo, NEAR_FIRST, keep, send)
    wait(dqkv_out, *outs)


def input_grad_kernel(ids, dqkv_a_hbm, dqkv_b_hbm, mg_hbm, x_hbm, vecs, w_hbm, sums, ub_own, ub_other, *refs):
    mine_parts, sib_parts = refs[:4], refs[4:8]
    in_grad, vec = refs[8:10]
    dqkv_a, dqkv_b, mg, x, w_own, w_other, dn, sems = refs[10:]
    half, core = ids[0], ids[1]
    copies = Copies(sems)
    own_in = [copies.start(dqkv_a_hbm, dqkv_a), copies.start(w_hbm, w_own)]
    other_in, _ = fetch_weights(copies, ids, mine_parts, sib_parts, w_other, None)
    other_in.append(copies.start(dqkv_b_hbm, dqkv_b))
    late = [copies.start(mg_hbm, mg), copies.start(x_hbm, x)]
    width = w_own.shape[2]
    wait(*own_in)
    dn[...] = normed_grad(dqkv_a, w_own)
    wait(*other_in)
    dn[...] += normed_grad(dqkv_b, w_other)
    wait(*late)

    def back_rows(at, totals):
        part, gain_sum, shift_sum = norm_back(x[at, :].astype(F32), dn[at, :], vecs[0:1, :])
        in_grad[at, :] = (mg[at, :] + part).astype(BF16)
        return totals[0] + gain_sum, totals[1] + shift_sum

    totals = over_rows(x.shape[0], back_rows, (jnp.zeros((1, x.shape[1]), F32),) * 2)
    vec[...] = jnp.zeros_like(vec)
    for i in range(2):
        vec[i : i + 1, :] = totals[i]
    vec[2:6, :] = sums[0:4, :]
    for dqkv, side in ((dqkv_a, half), (dqkv_b, 1 - half)):
        for i, value in enumerate(bias_sums(dqkv)):
            vec[6 + i : 7 + i, pl.ds(pl.multiple_of(side * width, width), width)] = value
    vec[pl.ds(8 + 2 * half + core, 1), :] = ub_own[...]
    vec[pl.ds(8 + 2 * (1 - half) + core, 1), :] = ub_other[...]


def layer_out_kernel(mid_hbm, own_hbm, sib_hbm, vecs, out, mid, own, sib, sems):
    copies = Copies(sems)
    wait(copies.start(mid_hbm, mid), copies.start(own_hbm, own), copies.start(sib_hbm, sib))

    def rows(at, carry):
        out[at, :] = (mid[at, :] + own[at, :] + sib[at, :].astype(F32) + vecs[5:6, :]).astype(BF16)
        return carry

    over_rows(out.shape[0], rows, 0)


class Placing:
    def __init__(self, ids, copies):
        self.core, self.mine = ids[1], ids[2]
        self.copies = copies
        self.work, self.outs = [], []

    def take(self, refs, narrow, wide, targets):
        for i, ref in enumerate(refs):
            side = self.core if i < UNITS else 1 - self.core
            unit = jnp.bitwise_xor(self.mine, i % UNITS)
            self.work.append((self.copies.start(ref, narrow.at[i]), narrow, wide, i, targets(side, unit)))

    def finish(self):
        for arrived, narrow, wide, i, targets in self.work:
            arrived.wait()
            wide[i] = narrow[i].astype(F32)
            for block, target in targets:
                self.outs.append(self.copies.start(wide.at[i, block[0], block[1]], target))
        wait(*self.outs)


def mlp_targets(out, down_first, rows, width):
    def targets(side, unit):
        base, start = pl.multiple_of(side * width, width), pl.multiple_of(unit * rows, rows)
        if down_first:
            target = out.at[pl.ds(pl.multiple_of(base + start, rows), rows), :]
        else:
            target = out.at[pl.ds(start, rows), pl.ds(base, width)]
        return [((pl.ds(0, rows), pl.ds(0, width)), target)]

    return targets


def attn_targets(w, wo):
    width = w.shape[2]
    rows = w.shape[1] // (2 * UNITS)

    def targets(side, unit):
        at_w = pl.ds(pl.multiple_of((side * UNITS + unit) * rows, rows), rows)
        at_o = pl.ds(pl.multiple_of(unit * rows, rows), rows)
        cols = pl.ds(pl.multiple_of(side * width, width), width)
        places = [w.at[part, at_w, :] for part in range(3)] + [wo.at[at_o, cols]]
        return [(unit_block(part, rows, width), place) for part, place in enumerate(places)]

    return targets


def place_mlp_kernel(down_first, ids, *refs):
    units, (out, narrow, wide, sems) = refs[:8], refs[8:]
    placing = Placing(ids, Copies(sems))
    placing.take(units, narrow, wide, mlp_targets(out, down_first, *units[0].shape))
    placing.finish()


def place_down_kernel(*refs):
    place_mlp_kernel(True, *refs)


def place_two_kernel(ids, *refs):
    up_units, attn_units = refs[:8], refs[8:16]
    up, w, wo, narrow_u, wide_u, narrow_a, wide_a, sems = refs[16:]
    placing = Placing(ids, Copies(sems))
    placing.take(up_units, narrow_u, wide_u, mlp_targets(up, False, *up_units[0].shape))
    placing.take(attn_units, narrow_a, wide_a, attn_targets(w, wo))
    placing.finish()


def vmem(*buffers, sems):
    return [pltpu.VMEM(shape, dtype) for shape, dtype in buffers] + [pltpu.SemaphoreType.DMA((sems,))]


def call(kernel, outs, in_specs, name, scratch=(), out_specs=None, limit=60, gflop=1.0):
    return pl.pallas_call(
        kernel,
        out_shape=tuple(jax.ShapeDtypeStruct(shape, dtype) for shape, dtype in outs),
        in_specs=in_specs,
        out_specs=tuple(VM for _ in outs) if out_specs is None else tuple(out_specs),
        scratch_shapes=list(scratch),
        name=name,
        cost_estimate=pl.CostEstimate(flops=int(gflop * 1e9), bytes_accessed=8 << 20, transcendentals=0),
        compiler_params=pltpu.CompilerParams(vmem_limit_bytes=limit * 1024 * 1024),
    )


def build(mesh):
    devices = mesh.shape["dp"] * mesh.shape["tp"]
    bits = devices.bit_length() - 1

    def swap(value, mask):
        return lax.ppermute(value, ("dp", "tp"), [(i, i ^ mask) for i in range(devices)])

    def after(value, *deps):
        return lax.optimization_barrier((value, deps))[0]

    def share(unit):
        return [unit] + [swap(unit, mask) for mask in (NEAR, FAR, NEAR | FAR)]

    def add(*terms):
        total = terms[0].astype(F32)
        for term in terms[1:]:
            total = total + term.astype(F32)
        return total

    last = []

    def turn(*values):
        return lax.optimization_barrier((values, last[-1]))[0]

    def note(value):
        last.append(value)
        return value

    def due(*values):
        values = turn(*values)
        note(values[-1])
        return values

    def total(parts, *terms):
        cut = lambda v, part: v if part is None else v[v.shape[0] * part[0] // 4 : v.shape[0] * part[1] // 4]
        return note(add(*[cut(term, part) for term, part in zip(turn(*terms), parts)]).astype(BF16))

    def on_device(
        layer_in, lengths, attn_gain, attn_shift, qkv_weight, qv_bias, out_weight, out_bias,
        mlp_gain, mlp_shift, up_weight, up_bias, down_weight, down_bias, cotangent,
    ):
        tokens, wide = layer_in.shape
        width = qkv_weight.shape[2]
        hidden = up_weight.shape[1] // 2
        flat = lax.axis_index("dp") * 2 + lax.axis_index("tp")
        half = lax.axis_index("tp")
        core = (flat >> CORE_BIT) & 1
        mine = ((flat >> FAR_BIT) & 1) * 2 + ((flat >> NEAR_BIT) & 1)
        ids = jnp.stack([half, core, mine]).astype(jnp.int32)
        up_bias_own = lax.dynamic_slice(up_bias, (core * hidden,), (hidden,))
        vecs = jnp.stack([attn_gain, attn_shift, out_bias, mlp_gain, mlp_shift, down_bias, up_bias_own, up_bias_own])
        w_own = jnp.transpose(qkv_weight, (1, 0, 2))

        part_rows = wide // (2 * UNITS)
        unit_w = lax.dynamic_slice(w_own, (0, (core * UNITS + mine) * part_rows, 0), (3, part_rows, width))
        unit_o = lax.dynamic_slice(out_weight, (mine * part_rows, core * width), (part_rows, width))
        attn_unit = jnp.concatenate(
            [jnp.concatenate([unit_w[0], unit_w[1]], axis=1), jnp.concatenate([unit_w[2], unit_o], axis=1)]
        )
        attn_unit = swap(attn_unit, TP)

        acts = (tokens, 3 * width)
        one = (tokens, wide)
        head = (tokens, width)
        w_shape, wo_shape = (3, wide, width), (width, wide)
        nrm, qkv_own, att_own = call(
            own_fwd_kernel,
            [(one, BF16), (acts, BF16), (head, BF16)],
            [SM, SM, HB, VM, HB, VM],
            "attn_own_fwd",
            gflop=0.5,
            scratch=vmem((one, BF16), (w_shape, BF16), (one, BF16), (acts, BF16), sems=4),
            out_specs=[HB, HB, VM],
        )(lengths, ids, layer_in, vecs, w_own, qv_bias)
        attn_parts = share(after(attn_unit, att_own))
        unit_rows = hidden // UNITS
        up_late, down_late, bias_late, up_bias_late = after((up_weight, down_weight, qv_bias, up_bias), att_own)
        mlp_unit = jnp.concatenate(
            [
                lax.dynamic_slice(up_late, (mine * unit_rows, core * hidden), (unit_rows, hidden)),
                lax.dynamic_slice(down_late, (core * hidden + mine * unit_rows, 0), (unit_rows, wide)),
            ]
        )
        mlp_unit = swap(mlp_unit, TP)
        small = jnp.concatenate([bias_late.reshape(-1), up_bias_late])
        small_other = swap(small.reshape(3, wide), TP)
        ct_sib = swap(cotangent, CORE)
        attn_sib = [swap(part, CORE) for part in attn_parts]
        qkv_other, att_other, mid, nm = call(
            other_fwd_kernel,
            [(acts, BF16), (head, BF16), (one, F32), (one, BF16)],
            [SM, SM, HB, HB, VM, HB, HB, VM] + [HB] * 8,
            "attn_other_fwd",
            gflop=6,
            scratch=vmem(
                (one, BF16), (one, BF16), (head, BF16), (wo_shape, BF16), (w_shape, BF16), (wo_shape, BF16),
                (acts, BF16), (head, BF16), (one, F32), sems=40,
            ),
            out_specs=[HB, HB, HB, VM],
        )(
            lengths, ids, layer_in, after(nrm, mlp_unit), small_other, att_own, out_weight, vecs,
            *attn_parts, *attn_sib,
        )
        mlp_near, mlp_far = swap(mlp_unit, NEAR), swap(mlp_unit, FAR)

        mlp_near, mlp_far, nm = after((mlp_near, mlp_far, nm))
        mlp_parts = [mlp_unit, mlp_near, mlp_far, swap(mlp_unit, NEAR | FAR)]
        nm_sib = swap(nm, CORE)
        tall, square = (2 * tokens, wide), (wide, hidden)
        scratch = [
            (square, BF16), (square, BF16), (tall, BF16), (tall, BF16), ((tokens, hidden), F32), ((tokens, hidden), F32),
            ((2 * tokens, hidden), BF16), ((2 * tokens, hidden), BF16), (square, BF16), (square, BF16),
        ]

        def mlp_scratch(*more):
            buffers = vmem(*scratch, *more, sems=40)
            return buffers[:10] + buffers[-1:] + buffers[10:-1]

        both = (2 * tokens, wide)
        pair = (2 * unit_rows, hidden)
        out_a, dnm_a, keep_own, send_own, b_own_lo, b_own_hi, ub_own = call(
            lambda *r: mlp_kernel(True, *r),
            [(both, BF16), (both, BF16), *[(pair, BF16)] * 4, ((1, hidden), F32)],
            [SM] + [HB] * 4 + [VM] + [HB] * 2,
            "mlp_own",
            gflop=1,
            scratch=mlp_scratch((tall, BF16), (tall, BF16)),
            out_specs=[HB] * 6 + [VM],
        )(ids, nm, nm_sib, cotangent, ct_sib, vecs, up_weight, down_weight)
        out_own, out_sib, dnm_own, dnm_sib, keep_other, send_other, b_other_lo, b_other_hi, ub_other = call(
            lambda *r: mlp_kernel(False, *r),
            [
                (one, F32), (one, BF16), (one, F32), (one, BF16), *[(pair, BF16)] * 4,
                ((1, hidden), F32),
            ],
            [SM] + [HB] * 4 + [VM] + [HB] * 6,
            "mlp_other",
            gflop=12,
            scratch=mlp_scratch((tall, BF16), (tall, BF16), (one, F32), (one, BF16), (one, F32), (one, BF16)),
            out_specs=[HB] * 8 + [VM],
        )(ids, nm, nm_sib, cotangent, ct_sib, small_other, *mlp_parts, out_a, dnm_a)
        grad_units = (2 * UNITS * part_rows, 2 * width)
        whole, low_half, high_half, first, second = None, (0, 2), (2, 4), (0, 1), (1, 2)
        a_own = swap(send_own, NEAR)
        note(ub_other)
        a_own, dnm_sib, out_sib, send_other, b_other_hi, b_other_lo = turn(
            a_own, dnm_sib, out_sib, send_other, b_other_hi, b_other_lo
        )
        dnm_got = swap(dnm_sib, CORE)
        a_own2 = swap(total((high_half, high_half), keep_own, a_own), FAR)
        a_other = swap(send_other, NEAR)
        b_hi = swap(b_other_hi, TP)
        mg, dqkv_other, keep_o, send_o, sums_mid = call(
            other_back_kernel,
            [(one, F32), (acts, BF16), (grad_units, BF16), (grad_units, BF16), ((8, wide), F32)],
            [SM, SM, HB, HB, HB, HB, VM, HB, HB, HB] + [HB] * 8,
            "attn_other_back",
            gflop=10,
            scratch=vmem(
                (one, F32), (one, BF16), (one, BF16), (one, F32), (acts, BF16), (head, BF16), (one, BF16),
                (wo_shape, BF16), (one, F32), (one, BF16), (head, BF16), (acts, BF16),
                (w_shape, BF16), (wo_shape, BF16), sems=60,
            ),
            out_specs=[HB] * 4 + [VM],
        )(
            lengths, ids, dnm_own, dnm_got, cotangent, mid, vecs, qkv_other, att_other, nrm,
            *attn_parts, *attn_sib,
        )
        note(sums_mid)
        out_got = swap(turn(out_sib)[0], CORE)
        a_other, a_own2, b_hi, send_o = turn(a_other, a_own2, b_hi, send_o)
        o_sib = swap(send_o, CORE)
        a_other2 = swap(total((high_half, high_half), keep_other, a_other), FAR)
        o1 = swap(total((high_half, high_half), keep_o, o_sib), NEAR)
        b_lo = swap(b_other_lo, TP)
        mg_now, = turn(mg)
        dqkv_own, keep_s, send_s = call(
            own_back_kernel,
            [(acts, BF16), (grad_units, BF16), (grad_units, BF16)],
            [SM, SM] + [HB] * 5,
            "attn_own_back",
            gflop=10,
            scratch=vmem(
                (one, F32), (wo_shape, BF16), (acts, BF16), (head, BF16), (one, BF16),
                (one, BF16), (head, BF16), (acts, BF16), (w_shape, BF16), (wo_shape, BF16), sems=48,
            ),
            out_specs=[HB] * 3,
        )(lengths, ids, mg_now, out_weight, qkv_own, att_own, nrm)
        note(dqkv_own)
        a_other2, o1, b_lo, send_s = turn(a_other2, o1, b_lo, send_s)
        s_sib = swap(send_s, CORE)
        a_back = swap(total((low_half, low_half, whole), keep_other, a_other, a_other2), TP)
        s1 = swap(total((high_half, high_half), keep_s, s_sib), NEAR)
        o2 = swap(total((second, second, high_half), keep_o, o_sib, o1), FAR)
        b1 = swap(total((whole, whole), b_own_hi, b_hi), NEAR)
        a_unit = total((low_half, low_half, whole, whole), keep_own, a_own, a_own2, a_back)
        a_more = swap(a_unit, 1 << FIRST_REST)
        in_grad, vec = call(
            input_grad_kernel,
            [(one, BF16), ((16, wide), F32)],
            [SM, HB, HB, HB, HB, VM, HB, VM, VM, VM] + [HB] * 8,
            "input_grad",
            gflop=0.01,
            scratch=vmem(
                (acts, BF16), (acts, BF16), (one, F32), (one, BF16), (w_shape, BF16), (w_shape, BF16), (one, F32),
                sems=32,
            ),
        )(
            ids, dqkv_own, dqkv_other, *turn(mg), layer_in, vecs, w_own, sums_mid, ub_own, ub_other,
            *attn_parts, *attn_sib,
        )
        note(vec)

        def step(value, bit):
            mine, got = turn(value, swap(value, 1 << bit))
            return note(mine + got)

        def rest(unit, got):
            unit = total((whole, whole), unit, got)
            for bit in range(FIRST_REST + 1, bits):
                unit = total((whole, whole), unit, swap(unit, 1 << bit))
            return unit

        def step_with(value, got):
            mine, got = turn(value, got)
            return note(mine + got)

        s2 = swap(total((second, second, high_half), keep_s, s_sib, s1), FAR)
        o_back = swap(total((first, first, low_half, whole), keep_o, o_sib, o1, o2), TP)
        vec = step(vec, CORE_BIT)
        a_unit = rest(a_unit, a_more)
        a_near, a_far = swap(a_unit, NEAR), swap(a_unit, FAR)
        for bit in range(FIRST_REST, bits):
            vec = step(vec, bit)
        s_unit = total((first, first, low_half, whole, whole), keep_s, s_sib, s1, s2, o_back)
        s_more = swap(s_unit, 1 << FIRST_REST)
        vec_tp = swap(vec, TP)
        b2 = swap(total((high_half, high_half, high_half), b_own_lo, b_lo, b1), FAR)
        layer_out, = call(
            layer_out_kernel,
            [(one, BF16)],
            [HB, HB, HB, VM],
            "layer_out",
            gflop=0.01,
            scratch=vmem((one, F32), (one, F32), (one, BF16), sems=3),
        )(mid, out_own, *turn(out_got), vecs)
        note(layer_out)
        a_near, a_far, vec_tp, b2, s_more = due(a_near, a_far, vec_tp, b2, s_more)
        s_unit = rest(s_unit, s_more)
        s_units = share(s_unit)
        b_unit = total((low_half, low_half, low_half, whole), b_own_lo, b_lo, b1, b2)
        b_more = swap(b_unit, 1 << FIRST_REST)
        a_corner = swap(a_far, NEAR)
        vec = note(vec + vec_tp)
        *s_units, a_corner, b_more = due(*s_units, a_corner, b_more)
        b_unit = rest(b_unit, b_more)
        b_units = share(b_unit)
        vec_near = swap(vec, NEAR)
        a_units = [a_unit, a_near, a_far, a_corner]
        a_sib = [swap(value, CORE) for value in turn(*a_units)]
        s_sib = [swap(value, CORE) for value in turn(*s_units)]
        up_grad, qkv_grad, out_grad = call(
            place_two_kernel,
            [((wide, 2 * hidden), F32), ((3, wide, width), F32), ((width, wide), F32)],
            [SM] + [HB] * 16,
            "place_two",
            gflop=0.01,
            scratch=vmem(
                ((8, unit_rows, hidden), BF16), ((8, unit_rows, hidden), F32),
                ((8, 2 * part_rows, 2 * width), BF16), ((8, 2 * part_rows, 2 * width), F32), sems=56,
            ),
            out_specs=[HB] * 3,
            limit=32,
        )(ids, *turn(*a_units, *a_sib, *s_units, *s_sib))
        note(out_grad)
        vec = step_with(vec, vec_near)
        vec_far = swap(vec, FAR)
        *b_three, b_corner = b_units
        b_three = due(*b_three)
        b_sib = [swap(value, CORE) for value in b_three]
        *b_sib, vec_far, b_corner = due(*b_sib, vec_far, b_corner)
        b_sib.append(swap(b_corner, CORE))
        b_units = [*b_three, b_corner]
        vec = vec + vec_far
        down_grad, = call(
            place_down_kernel,
            [((2 * hidden, wide), F32)],
            [SM] + [HB] * 8,
            "place_down",
            scratch=vmem(((8, unit_rows, wide), BF16), ((8, unit_rows, wide), F32), sems=16),
            out_specs=[HB],
            limit=24,
        )(ids, *b_units, *b_sib)
        one_of = lambda i: vec[i]
        qvb = lax.dynamic_slice(vec, (6, half * width), (2, width))
        ub = lax.dynamic_slice(vec, (8 + 2 * half, 0), (2, hidden)).reshape(2 * hidden)
        return (
            layer_out, in_grad, one_of(0), one_of(1), jnp.transpose(qkv_grad, (1, 0, 2)), qvb,
            out_grad, one_of(4), one_of(2), one_of(3), up_grad, ub, down_grad, one_of(5),
        )

    return on_device


def solution(mesh):
    tokens, vector = P(("dp", "tp"), None), P()
    in_specs = (
        tokens, P("dp", None), vector, vector, P(None, None, "tp"), P(None, "tp"), P("tp", None), vector,
        vector, vector, P(None, "tp"), P("tp"), P("tp", None), vector, tokens,
    )
    out_specs = (
        tokens, tokens, vector, vector, P(None, None, "tp"), P(None, "tp"), P("tp", None), vector,
        vector, vector, P(None, "tp"), P("tp"), P("tp", None), vector,
    )
    return jax.shard_map(build(mesh), mesh=mesh, in_specs=in_specs, out_specs=out_specs, check_vma=False)
```

```python
import math

import jax
import jax.numpy as jnp
from jax import lax
from jax.experimental import pallas as pl
from jax.experimental.pallas import tpu as pltpu
from jax.sharding import PartitionSpec as P

HEAD = 64
SEQ = 128
UNITS = 4
EPS = 1e-05
SCALE = 1.0 / math.sqrt(HEAD)
F32 = jnp.float32
BF16 = jnp.bfloat16

VM = pl.BlockSpec(memory_space=pltpu.VMEM)
SM = pl.BlockSpec(memory_space=pltpu.SMEM)
HB = pl.BlockSpec(memory_space=pl.ANY)

NEAR_FIRST, FAR_FIRST = (0, 2, 1, 3), (0, 1, 2, 3)
TP_BIT, CORE_BIT, NEAR_BIT, FAR_BIT, FIRST_REST = 0, 1, 2, 3, 4
TP, CORE, NEAR, FAR = (1 << bit for bit in (TP_BIT, CORE_BIT, NEAR_BIT, FAR_BIT))


def nn(a, b):
    return lax.dot_general(a, b, (((1,), (0,)), ((), ())), preferred_element_type=F32)


def nt(a, b):
    return lax.dot_general(a, b, (((1,), (1,)), ((), ())), preferred_element_type=F32)


def tn(a, b):
    return lax.dot_general(a, b, (((0,), (0,)), ((), ())), preferred_element_type=F32)


def normalize(values):
    center = values - jnp.mean(values, axis=-1, keepdims=True)
    inv = lax.rsqrt(jnp.mean(center * center, axis=-1, keepdims=True) + EPS)
    return center * inv, inv


def norm_back(values, grad, gain):
    normed, inv = normalize(values)
    scaled = grad * gain
    mean_g = jnp.mean(scaled, axis=-1, keepdims=True)
    mean_gn = jnp.mean(scaled * normed, axis=-1, keepdims=True)
    part = inv * (scaled - mean_g - normed * mean_gn)
    gain_sum = jnp.sum(grad * normed, axis=0, keepdims=True)
    shift_sum = jnp.sum(grad, axis=0, keepdims=True)
    return part, gain_sum, shift_sum


def row_mask(lens, row):
    at_k = lax.broadcasted_iota(jnp.int32, (SEQ, 1), 0)
    at_q = lax.broadcasted_iota(jnp.int32, (1, SEQ), 1)
    total = jnp.int32(0)
    seg_q = jnp.zeros((1, SEQ), jnp.int32)
    seg_k = jnp.zeros((SEQ, 1), jnp.int32)
    for entry in range(lens.shape[1]):
        total = total + lens[row, entry]
        seg_q = seg_q + jnp.where(at_q >= total, 1, 0)
        seg_k = seg_k + jnp.where(at_k >= total, 1, 0)
    allowed = (seg_q == seg_k) & (at_k <= at_q) & ((at_k < total) | (at_k == at_q))
    valid = jnp.where(at_k < total, 1.0, 0.0).astype(F32)
    return jnp.concatenate([allowed, allowed], axis=1), valid


def low_lanes():
    return lax.broadcasted_iota(jnp.int32, (SEQ, 2 * HEAD), 1) < HEAD


def stack_pair(pair, low):
    zero = jnp.zeros_like(pair)
    return jnp.concatenate([jnp.where(low, pair, zero), jnp.where(low, zero, pair)], axis=0)


def pair_probs(q_stack, keys, allowed2):
    scores = jnp.where(allowed2, nt(keys, q_stack) * SCALE, -1e30)
    weights = jnp.exp(scores - jnp.max(scores, axis=0, keepdims=True))
    return weights * (1.0 / jnp.sum(weights, axis=0, keepdims=True))


class Copies:
    def __init__(self, sems):
        self.sems = sems
        self.count = 0

    def start(self, src, dst):
        made = pltpu.make_async_copy(src, dst, self.sems.at[self.count])
        self.count += 1
        made.start()
        return made


def wait(*copies):
    for made in copies:
        made.wait()


def blocks(count, size=SEQ):
    return [slice(i * size, (i + 1) * size) for i in range(count)]


def over_rows(tokens, body, start):
    at = lambda i: pl.ds(pl.multiple_of(i * SEQ, SEQ), SEQ)
    return lax.fori_loop(0, tokens // SEQ, lambda i, carry: body(at(i), carry), start)


def project(nrm, w, bias, qkv):
    width = w.shape[2]
    for part in range(3):
        value = nn(nrm[...], w[part])
        if part != 1:
            value = value + bias[part // 2]
        qkv[:, part * width : (part + 1) * width] = value.astype(BF16)


def attend(lens, ids, qkv, att):
    width = att.shape[1]
    rows = att.shape[0] // SEQ
    low = low_lanes()
    @pl.loop(0, rows, unroll=2)
    def _(row):
        at = pl.ds(pl.multiple_of(row * SEQ, SEQ), SEQ)
        allowed2, valid = row_mask(lens, ids[0] * rows + row)
        for first in range(0, width, 2 * HEAD):
            q = qkv[at, first : first + 2 * HEAD]
            k = qkv[at, width + first : width + first + 2 * HEAD]
            v = qkv[at, 2 * width + first : 2 * width + first + 2 * HEAD]
            probs = pair_probs(stack_pair(q, low), k, allowed2)
            both = tn(probs.astype(BF16), v)
            out = jnp.where(low, both[:SEQ], both[SEQ:]) * valid
            att[at, first : first + 2 * HEAD] = out.astype(BF16)


def own_fwd_kernel(lens, ids, x_hbm, vecs, w_hbm, bias, nrm_hbm, qkv_hbm, att, x, w, nrm, qkv, sems):
    copies = Copies(sems)
    x_in = copies.start(x_hbm, x)
    w_in = copies.start(w_hbm, w)
    wait(x_in)

    def norm_rows(at, carry):
        normed, _ = normalize(x[at, :].astype(F32))
        nrm[at, :] = (normed * vecs[0:1, :] + vecs[1:2, :]).astype(BF16)
        return carry

    over_rows(x.shape[0], norm_rows, 0)
    nrm_out = copies.start(nrm, nrm_hbm)
    wait(w_in)
    project(nrm, w, [bias[0:1, :], bias[1:2, :]], qkv)
    qkv_out = copies.start(qkv, qkv_hbm)
    attend(lens, ids, qkv, att)
    wait(nrm_out, qkv_out)


def unit_block(part, rows, width, first=0):
    return pl.ds(first + (part // 2) * rows, rows), pl.ds((part % 2) * width, width)


def fetch_weights(copies, ids, mine_parts, sib_parts, w, wo):
    core, mine = ids[1], ids[2]
    width = w.shape[2]
    part_rows = w.shape[1] // (2 * UNITS)
    to_w, to_wo = [], []
    for side, parts in ((core, mine_parts), (1 - core, sib_parts)):
        for step, unit_ref in enumerate(parts):
            unit = jnp.bitwise_xor(mine, step)
            at_w = pl.ds(pl.multiple_of((side * UNITS + unit) * part_rows, part_rows), part_rows)
            at_o = pl.ds(pl.multiple_of(unit * part_rows, part_rows), part_rows)
            cols = pl.ds(pl.multiple_of(side * width, width), width)
            for part in range(3):
                to_w.append(copies.start(unit_ref.at[unit_block(part, part_rows, width)], w.at[part, at_w, :]))
            if wo is not None:
                to_wo.append(copies.start(unit_ref.at[unit_block(3, part_rows, width)], wo.at[at_o, cols]))
    return to_w, to_wo


def fetch_output_weight(copies, ids, mine_parts, sib_parts, wo):
    core, mine = ids[1], ids[2]
    width = wo.shape[0]
    part_rows = width // UNITS
    made = []
    for side, parts in ((core, mine_parts), (1 - core, sib_parts)):
        for step, unit_ref in enumerate(parts):
            at_o = pl.ds(pl.multiple_of(jnp.bitwise_xor(mine, step) * part_rows, part_rows), part_rows)
            cols = pl.ds(pl.multiple_of(side * width, width), width)
            made.append(copies.start(unit_ref.at[unit_block(3, part_rows, width)], wo.at[at_o, cols]))
    return made


def other_fwd_kernel(lens, ids, x_hbm, nrm_hbm, bias, att_own_hbm, wo_own_hbm, vecs, *refs):
    mine_parts, sib_parts = refs[:4], refs[4:8]
    qkv_hbm, att_hbm, mid_hbm, nm = refs[8:12]
    x, nrm, att_own, wo_own, w, wo, qkv, att, mid, sems = refs[12:]
    copies = Copies(sems)
    nrm_in = copies.start(nrm_hbm, nrm)
    to_w, to_wo = fetch_weights(copies, ids, mine_parts, sib_parts, w, wo)
    late = [copies.start(x_hbm, x), copies.start(att_own_hbm, att_own), copies.start(wo_own_hbm, wo_own)]
    wait(nrm_in, *to_w)
    half = w.shape[2]
    project(nrm, w, [bias[0:1, :half], bias[0:1, half:]], qkv)
    qkv_out = copies.start(qkv, qkv_hbm)
    attend(lens, ids, qkv, att)
    att_out = copies.start(att, att_hbm)
    wait(*to_wo, *late)
    mid[...] = nn(att_own[...], wo_own[...]) + nn(att[...], wo[...])

    def norm_rows(at, carry):
        value = x[at, :].astype(F32) + mid[at, :] + vecs[2:3, :]
        mid[at, :] = value
        normed, _ = normalize(value)
        nm[at, :] = (normed * vecs[3:4, :] + vecs[4:5, :]).astype(BF16)
        return carry

    over_rows(x.shape[0], norm_rows, 0)
    mid_out = copies.start(mid, mid_hbm)
    wait(qkv_out, att_out, mid_out)


def gelu_parts(pre):
    bell = jnp.exp(-0.5 * pre * pre)
    t = 1.0 / (1.0 + (0.3275911 * math.sqrt(0.5)) * jnp.abs(pre))
    poly = 0.5307027145 * t - 0.7265760135
    poly = poly * t + 0.7107068705
    poly = poly * t - 0.142248368
    poly = poly * t + 0.127414796
    tail = poly * t * bell
    cdf = jnp.where(pre >= 0, 1.0 - tail, tail)
    return pre * cdf, cdf + pre * bell * (1.0 / math.sqrt(2.0 * math.pi))


def mlp_kernel(own, *refs):
    ids, nm_a, nm_b, ct_a, ct_b, biases = refs[:6]
    if own:
        up_hbm, down_hbm = refs[6:8]
        out_hbm, dnm_hbm, keep_a, send_a, keep_b, send_b, bias_g = refs[8:15]
        scratch = refs[15:]
    else:
        units, (out_prev, dnm_prev) = refs[6:10], refs[10:12]
        out_own_hbm, out_sib_hbm, dnm_own_hbm, dnm_sib_hbm, keep_a, send_a, keep_b, send_b, bias_g = refs[12:21]
        scratch = refs[21:]
    up, down, nm, ct, pre, dact, act, pg, gu, gd, sems = scratch[:11]
    core, mine = ids[1], ids[2]
    hidden = up.shape[1]
    tokens = nm_a.shape[0]
    unit_rows = up.shape[0] // UNITS
    copies = Copies(sems)
    copy = copies.start
    halves = (pl.ds(0, tokens), pl.ds(tokens, tokens))

    def unit_at(step):
        start = jnp.bitwise_xor(mine, step) * unit_rows
        return pl.ds(pl.multiple_of(start, unit_rows), unit_rows)

    at = pl.ds(pl.multiple_of(core * hidden, hidden), hidden)
    if own:
        ups = [copy(up_hbm.at[:, at], up)]
    else:
        ups = [copy(unit.at[pl.ds(0, unit_rows)], up.at[unit_at(i), :]) for i, unit in enumerate(units)]
    nms = [copy(nm_a, nm.at[halves[0]])]
    if own:
        downs = [copy(down_hbm.at[at, :], down)]
    else:
        downs = [copy(unit.at[pl.ds(unit_rows, unit_rows)], down.at[unit_at(i), :]) for i, unit in enumerate(units)]
    cts = [copy(ct_a, ct.at[halves[0]])]
    nms.append(copy(nm_b, nm.at[halves[1]]))
    cts.append(copy(ct_b, ct.at[halves[1]]))
    if not own:
        prev_out, prev_dnm, dnm_own, dnm_sib, out_own, out_sib = scratch[11:17]
        lates = [copy(dnm_prev, prev_dnm), copy(out_prev, prev_out)]
    else:
        dnm, out = scratch[11:13]

    piece = 32

    def half_step(half, total):
        rows = pl.ds(pl.multiple_of(half * tokens, tokens), tokens)
        for i in range(2):
            pl.when(half == i)(lambda: wait(nms[i], *(ups if i == 0 else ())))
        pre[...] = nn(nm[rows, :], up[...])
        for i in range(2):
            pl.when(half == i)(lambda: wait(cts[i], *(downs if i == 0 else ())))
        dact[...] = nt(ct[rows, :], down[...])

        def elementwise(step, total):
            at = pl.ds(pl.multiple_of(step * piece, piece), piece)
            to = pl.ds(pl.multiple_of(half * tokens + step * piece, piece), piece)
            value, slope = gelu_parts(pre[at, :] + bias)
            act[to, :] = value.astype(BF16)
            back = dact[at, :] * slope
            pg[to, :] = back.astype(BF16)
            return total + jnp.sum(back.reshape(piece // 8, 8, hidden), axis=0)

        return lax.fori_loop(0, tokens // piece, elementwise, total)

    bias = biases[pl.ds((6 if own else 1 + core), 1), :]
    bias_sum = lax.fori_loop(0, 2, half_step, jnp.zeros((8, hidden), F32))
    bias_g[...] = jnp.sum(bias_sum, axis=0, keepdims=True)
    writes = []
    if own:
        dnm[...] = nt(pg[...], up[...]).astype(BF16)
        writes.append(copy(dnm, dnm_hbm))
        out[...] = nn(act[...], down[...]).astype(BF16)
        writes.append(copy(out, out_hbm))
    else:
        wait(*lates)
        total = nt(pg[...], up[...])
        dnm_own[...] = total[:tokens] + prev_dnm[:tokens, :].astype(F32)
        dnm_sib[...] = (total[tokens:] + prev_dnm[tokens:, :].astype(F32)).astype(BF16)
        writes += [copy(dnm_own, dnm_own_hbm), copy(dnm_sib, dnm_sib_hbm)]
        total = nn(act[...], down[...])
        out_own[...] = total[:tokens] + prev_out[:tokens, :].astype(F32)
        out_sib[...] = (total[tokens:] + prev_out[tokens:, :].astype(F32)).astype(BF16)
        writes += [copy(out_own, out_own_hbm), copy(out_sib, out_sib_hbm)]
    for source, grad, order, targets in (
        (gd, lambda: tn(act[...], ct[...]), NEAR_FIRST, (keep_b, send_b)),
        (gu, lambda: tn(nm[...], pg[...]), NEAR_FIRST, (keep_a, send_a)),
    ):
        source[...] = grad().astype(BF16)
        for place, step in enumerate(order):
            to = targets[place // 2].at[pl.ds((place % 2) * unit_rows, unit_rows)]
            writes.append(copy(source.at[unit_at(step), :], to))
    wait(*writes)


def attend_back(lens, ids, qkv, datt, dqkv):
    width = datt.shape[1]
    rows = datt.shape[0] // SEQ
    low = low_lanes()

    @pl.loop(0, rows)
    def _(row):
        allowed2, valid = row_mask(lens, ids[0] * rows + row)
        at = pl.ds(pl.multiple_of(row * SEQ, SEQ), SEQ)
        for first in range(0, width, 2 * HEAD):
            q_cols = slice(first, first + 2 * HEAD)
            k_cols = slice(width + first, width + first + 2 * HEAD)
            v_cols = slice(2 * width + first, 2 * width + first + 2 * HEAD)
            k = qkv[at, k_cols]
            q_stack = stack_pair(qkv[at, q_cols], low)
            grad = (datt[at, q_cols].astype(F32) * valid).astype(BF16)
            g_stack = stack_pair(grad, low)
            probs = pair_probs(q_stack, k, allowed2)
            dqkv[at, v_cols] = nn(probs.astype(BF16), g_stack).astype(BF16)
            prob_grad = nt(qkv[at, v_cols], g_stack)
            inner = jnp.sum(probs * prob_grad, axis=0, keepdims=True)
            score_grad = (probs * (prob_grad - inner)).astype(BF16)
            both = tn(score_grad, k)
            dqkv[at, q_cols] = (jnp.where(low, both[:SEQ], both[SEQ:]) * SCALE).astype(BF16)
            dqkv[at, k_cols] = (nn(score_grad, q_stack) * SCALE).astype(BF16)


def weight_grads(copies, ids, nrm, dqkv, dw, dwo, order, keep, send):
    core, mine = ids[1], ids[2]
    width = dw.shape[2]
    part_rows = dw.shape[1] // (2 * UNITS)
    made = []
    for part in (3, 2, 1, 0):
        if part < 3:
            dw[part] = tn(nrm[...], dqkv[:, part * width : (part + 1) * width]).astype(BF16)
        for place in range(UNITS):
            unit = jnp.bitwise_xor(mine, order[place])
            for side, target in ((1 - core, send), (core, keep)):
                at_w = pl.ds(pl.multiple_of((side * UNITS + unit) * part_rows, part_rows), part_rows)
                at_o = pl.ds(pl.multiple_of(unit * part_rows, part_rows), part_rows)
                cols = pl.ds(pl.multiple_of(side * width, width), width)
                source = dw.at[part, at_w, :] if part < 3 else dwo.at[at_o, cols]
                made.append(copies.start(source, target.at[unit_block(part, part_rows, width, 2 * place * part_rows)]))
    return made


def bias_sums(dqkv):
    width = dqkv.shape[1] // 3
    ones = jnp.ones((8, dqkv.shape[0]), BF16)
    return [nn(ones, dqkv[:, first : first + width])[0:1] for first in (0, 2 * width)]


def normed_grad(dqkv, w):
    width = w.shape[2]
    total = nt(dqkv[:, :width], w[0])
    for part in range(1, 3):
        total = total + nt(dqkv[:, part * width : (part + 1) * width], w[part])
    return total


def other_back_kernel(lens, ids, dnm_own_hbm, dnm_sib_hbm, ct_hbm, mid_hbm, vecs, qkv_hbm, att_hbm, nrm_hbm, *refs):
    mine_parts, sib_parts = refs[:4], refs[4:8]
    mg_hbm, dqkv_hbm, keep, send, sums = refs[8:13]
    dnm_own, dnm_sib, ct, mid, qkv, att, nrm, wo, mg, ml, datt, dqkv, dw, dwo, sems = refs[13:]
    copies = Copies(sems)
    first_in = [
        copies.start(dnm_own_hbm, dnm_own), copies.start(dnm_sib_hbm, dnm_sib),
        copies.start(ct_hbm, ct), copies.start(mid_hbm, mid),
    ]
    to_wo = fetch_output_weight(copies, ids, mine_parts, sib_parts, wo)
    qkv_in, att_in, nrm_in = copies.start(qkv_hbm, qkv), copies.start(att_hbm, att), copies.start(nrm_hbm, nrm)
    wait(*first_in)

    def back_rows(at, totals):
        grad = dnm_own[at, :] + dnm_sib[at, :].astype(F32)
        part, gain_sum, shift_sum = norm_back(mid[at, :], grad, vecs[3:4, :])
        out_grad = ct[at, :].astype(F32)
        value = out_grad + part
        mg[at, :] = value
        ml[at, :] = value.astype(BF16)
        adds = (gain_sum, shift_sum, jnp.sum(value, axis=0, keepdims=True), jnp.sum(out_grad, axis=0, keepdims=True))
        return tuple(total + add for total, add in zip(totals, adds))

    totals = over_rows(mid.shape[0], back_rows, (jnp.zeros((1, mid.shape[1]), F32),) * 4)
    sums[...] = jnp.concatenate(list(totals) + [jnp.zeros((4, mid.shape[1]), F32)])
    mg_out = copies.start(mg, mg_hbm)
    wait(*to_wo, qkv_in, att_in)
    datt[...] = nt(ml[...], wo[...]).astype(BF16)
    dwo[...] = tn(att[...], ml[...]).astype(BF16)
    attend_back(lens, ids, qkv, datt, dqkv)
    wait(nrm_in)
    dqkv_out = copies.start(dqkv, dqkv_hbm)
    outs = weight_grads(copies, ids, nrm, dqkv, dw, dwo, NEAR_FIRST, keep, send)
    wait(mg_out, dqkv_out, *outs)


def own_back_kernel(
    lens, ids, mg_hbm, wo_hbm, qkv_hbm, att_hbm, nrm_hbm, dqkv_hbm, keep, send,
    mg, wo, qkv, att, nrm, ml, datt, dqkv, dw, dwo, sems,
):
    copies = Copies(sems)
    mg_in, wo_in = copies.start(mg_hbm, mg), copies.start(wo_hbm, wo)
    att_in, qkv_in, nrm_in = copies.start(att_hbm, att), copies.start(qkv_hbm, qkv), copies.start(nrm_hbm, nrm)
    wait(mg_in)
    ml[...] = mg[...].astype(BF16)
    wait(wo_in, att_in, qkv_in)
    datt[...] = nt(ml[...], wo[...]).astype(BF16)
    dwo[...] = tn(att[...], ml[...]).astype(BF16)
    attend_back(lens, ids, qkv, datt, dqkv)
    dqkv_out = copies.start(dqkv, dqkv_hbm)
    wait(nrm_in)
    outs = weight_grads(copies, ids, nrm, dqkv, dw, dwo, NEAR_FIRST, keep, send)
    wait(dqkv_out, *outs)


def input_grad_kernel(ids, dqkv_a_hbm, dqkv_b_hbm, mg_hbm, x_hbm, vecs, w_hbm, sums, ub_own, ub_other, *refs):
    mine_parts, sib_parts = refs[:4], refs[4:8]
    in_grad, vec = refs[8:10]
    dqkv_a, dqkv_b, mg, x, w_own, w_other, dn, sems = refs[10:]
    half, core = ids[0], ids[1]
    copies = Copies(sems)
    own_in = [copies.start(dqkv_a_hbm, dqkv_a), copies.start(w_hbm, w_own)]
    other_in, _ = fetch_weights(copies, ids, mine_parts, sib_parts, w_other, None)
    other_in.append(copies.start(dqkv_b_hbm, dqkv_b))
    late = [copies.start(mg_hbm, mg), copies.start(x_hbm, x)]
    width = w_own.shape[2]
    wait(*own_in)
    dn[...] = normed_grad(dqkv_a, w_own)
    wait(*other_in)
    dn[...] += normed_grad(dqkv_b, w_other)
    wait(*late)

    def back_rows(at, totals):
        part, gain_sum, shift_sum = norm_back(x[at, :].astype(F32), dn[at, :], vecs[0:1, :])
        in_grad[at, :] = (mg[at, :] + part).astype(BF16)
        return totals[0] + gain_sum, totals[1] + shift_sum

    totals = over_rows(x.shape[0], back_rows, (jnp.zeros((1, x.shape[1]), F32),) * 2)
    vec[...] = jnp.zeros_like(vec)
    for i in range(2):
        vec[i : i + 1, :] = totals[i]
    vec[2:6, :] = sums[0:4, :]
    for dqkv, side in ((dqkv_a, half), (dqkv_b, 1 - half)):
        for i, value in enumerate(bias_sums(dqkv)):
            vec[6 + i : 7 + i, pl.ds(pl.multiple_of(side * width, width), width)] = value
    vec[pl.ds(8 + 2 * half + core, 1), :] = ub_own[...]
    vec[pl.ds(8 + 2 * (1 - half) + core, 1), :] = ub_other[...]


def layer_out_kernel(mid_hbm, own_hbm, sib_hbm, vecs, out, mid, own, sib, sems):
    copies = Copies(sems)
    wait(copies.start(mid_hbm, mid), copies.start(own_hbm, own), copies.start(sib_hbm, sib))

    def rows(at, carry):
        out[at, :] = (mid[at, :] + own[at, :] + sib[at, :].astype(F32) + vecs[5:6, :]).astype(BF16)
        return carry

    over_rows(out.shape[0], rows, 0)


class Placing:
    def __init__(self, ids, copies):
        self.core, self.mine = ids[1], ids[2]
        self.copies = copies
        self.work, self.outs = [], []

    def take(self, refs, narrow, wide, targets):
        for i, ref in enumerate(refs):
            side = self.core if i < UNITS else 1 - self.core
            unit = jnp.bitwise_xor(self.mine, i % UNITS)
            self.work.append((self.copies.start(ref, narrow.at[i]), narrow, wide, i, targets(side, unit)))

    def finish(self):
        for arrived, narrow, wide, i, targets in self.work:
            arrived.wait()
            wide[i] = narrow[i].astype(F32)
            for block, target in targets:
                self.outs.append(self.copies.start(wide.at[i, block[0], block[1]], target))
        wait(*self.outs)


def mlp_targets(out, down_first, rows, width):
    def targets(side, unit):
        base, start = pl.multiple_of(side * width, width), pl.multiple_of(unit * rows, rows)
        if down_first:
            target = out.at[pl.ds(pl.multiple_of(base + start, rows), rows), :]
        else:
            target = out.at[pl.ds(start, rows), pl.ds(base, width)]
        return [((pl.ds(0, rows), pl.ds(0, width)), target)]

    return targets


def attn_targets(w, wo):
    width = w.shape[2]
    rows = w.shape[1] // (2 * UNITS)

    def targets(side, unit):
        at_w = pl.ds(pl.multiple_of((side * UNITS + unit) * rows, rows), rows)
        at_o = pl.ds(pl.multiple_of(unit * rows, rows), rows)
        cols = pl.ds(pl.multiple_of(side * width, width), width)
        places = [w.at[part, at_w, :] for part in range(3)] + [wo.at[at_o, cols]]
        return [(unit_block(part, rows, width), place) for part, place in enumerate(places)]

    return targets


def place_mlp_kernel(down_first, ids, *refs):
    units, (out, narrow, wide, sems) = refs[:8], refs[8:]
    placing = Placing(ids, Copies(sems))
    placing.take(units, narrow, wide, mlp_targets(out, down_first, *units[0].shape))
    placing.finish()


def place_down_kernel(*refs):
    place_mlp_kernel(True, *refs)


def place_two_kernel(ids, *refs):
    up_units, attn_units = refs[:8], refs[8:16]
    up, w, wo, narrow_u, wide_u, narrow_a, wide_a, sems = refs[16:]
    placing = Placing(ids, Copies(sems))
    placing.take(up_units, narrow_u, wide_u, mlp_targets(up, False, *up_units[0].shape))
    placing.take(attn_units, narrow_a, wide_a, attn_targets(w, wo))
    placing.finish()


def vmem(*buffers, sems):
    return [pltpu.VMEM(shape, dtype) for shape, dtype in buffers] + [pltpu.SemaphoreType.DMA((sems,))]


def call(kernel, outs, in_specs, name, scratch=(), out_specs=None, limit=61, gflop=1.0):
    return pl.pallas_call(
        kernel,
        out_shape=tuple(jax.ShapeDtypeStruct(shape, dtype) for shape, dtype in outs),
        in_specs=in_specs,
        out_specs=tuple(VM for _ in outs) if out_specs is None else tuple(out_specs),
        scratch_shapes=list(scratch),
        name=name,
        cost_estimate=pl.CostEstimate(flops=int(gflop * 1e9), bytes_accessed=8 << 20, transcendentals=0),
        compiler_params=pltpu.CompilerParams(vmem_limit_bytes=limit * 1024 * 1024),
    )


def build(mesh):
    devices = mesh.shape["dp"] * mesh.shape["tp"]
    bits = devices.bit_length() - 1

    def swap(value, mask):
        return lax.ppermute(value, ("dp", "tp"), [(i, i ^ mask) for i in range(devices)])

    def after(value, *deps):
        return lax.optimization_barrier((value, deps))[0]

    def share(unit):
        return [unit] + [swap(unit, mask) for mask in (NEAR, FAR, NEAR | FAR)]

    def add(*terms):
        total = terms[0].astype(F32)
        for term in terms[1:]:
            total = total + term.astype(F32)
        return total

    last = []

    def turn(*values):
        return lax.optimization_barrier((values, last[-1]))[0]

    def note(value):
        last.append(value)
        return value

    def due(*values):
        values = turn(*values)
        note(values[-1])
        return values

    def total(parts, *terms):
        cut = lambda v, part: v if part is None else v[v.shape[0] * part[0] // 4 : v.shape[0] * part[1] // 4]
        return note(add(*[cut(term, part) for term, part in zip(turn(*terms), parts)]).astype(BF16))

    def on_device(
        layer_in, lengths, attn_gain, attn_shift, qkv_weight, qv_bias, out_weight, out_bias,
        mlp_gain, mlp_shift, up_weight, up_bias, down_weight, down_bias, cotangent,
    ):
        tokens, wide = layer_in.shape
        width = qkv_weight.shape[2]
        hidden = up_weight.shape[1] // 2
        flat = lax.axis_index("dp") * 2 + lax.axis_index("tp")
        half = lax.axis_index("tp")
        core = (flat >> CORE_BIT) & 1
        mine = ((flat >> FAR_BIT) & 1) * 2 + ((flat >> NEAR_BIT) & 1)
        ids = jnp.stack([half, core, mine]).astype(jnp.int32)
        up_bias_own = lax.dynamic_slice(up_bias, (core * hidden,), (hidden,))
        vecs = jnp.stack([attn_gain, attn_shift, out_bias, mlp_gain, mlp_shift, down_bias, up_bias_own, up_bias_own])
        w_own = jnp.transpose(qkv_weight, (1, 0, 2))

        part_rows = wide // (2 * UNITS)
        unit_w = lax.dynamic_slice(w_own, (0, (core * UNITS + mine) * part_rows, 0), (3, part_rows, width))
        unit_o = lax.dynamic_slice(out_weight, (mine * part_rows, core * width), (part_rows, width))
        attn_unit = jnp.concatenate(
            [jnp.concatenate([unit_w[0], unit_w[1]], axis=1), jnp.concatenate([unit_w[2], unit_o], axis=1)]
        )
        attn_unit = swap(attn_unit, TP)

        acts = (tokens, 3 * width)
        one = (tokens, wide)
        head = (tokens, width)
        w_shape, wo_shape = (3, wide, width), (width, wide)
        nrm, qkv_own, att_own = call(
            own_fwd_kernel,
            [(one, BF16), (acts, BF16), (head, BF16)],
            [SM, SM, HB, VM, HB, VM],
            "attn_own_fwd",
            gflop=0.5,
            scratch=vmem((one, BF16), (w_shape, BF16), (one, BF16), (acts, BF16), sems=4),
            out_specs=[HB, HB, VM],
        )(lengths, ids, layer_in, vecs, w_own, qv_bias)
        attn_parts = share(after(attn_unit, att_own))
        unit_rows = hidden // UNITS
        up_late, down_late, bias_late, up_bias_late = after((up_weight, down_weight, qv_bias, up_bias), att_own)
        mlp_unit = jnp.concatenate(
            [
                lax.dynamic_slice(up_late, (mine * unit_rows, core * hidden), (unit_rows, hidden)),
                lax.dynamic_slice(down_late, (core * hidden + mine * unit_rows, 0), (unit_rows, wide)),
            ]
        )
        mlp_unit = swap(mlp_unit, TP)
        small = jnp.concatenate([bias_late.reshape(-1), up_bias_late])
        small_other = swap(small.reshape(3, wide), TP)
        ct_sib = swap(cotangent, CORE)
        attn_sib = [swap(part, CORE) for part in attn_parts]
        qkv_other, att_other, mid, nm = call(
            other_fwd_kernel,
            [(acts, BF16), (head, BF16), (one, F32), (one, BF16)],
            [SM, SM, HB, HB, VM, HB, HB, VM] + [HB] * 8,
            "attn_other_fwd",
            gflop=6,
            scratch=vmem(
                (one, BF16), (one, BF16), (head, BF16), (wo_shape, BF16), (w_shape, BF16), (wo_shape, BF16),
                (acts, BF16), (head, BF16), (one, F32), sems=40,
            ),
            out_specs=[HB, HB, HB, VM],
        )(
            lengths, ids, layer_in, after(nrm, mlp_unit), small_other, att_own, out_weight, vecs,
            *attn_parts, *attn_sib,
        )
        mlp_near, mlp_far = swap(mlp_unit, NEAR), swap(mlp_unit, FAR)

        mlp_near, mlp_far, nm = after((mlp_near, mlp_far, nm))
        mlp_parts = [mlp_unit, mlp_near, mlp_far, swap(mlp_unit, NEAR | FAR)]
        nm_sib = swap(nm, CORE)
        tall, square = (2 * tokens, wide), (wide, hidden)
        scratch = [
            (square, BF16), (square, BF16), (tall, BF16), (tall, BF16), ((tokens, hidden), F32), ((tokens, hidden), F32),
            ((2 * tokens, hidden), BF16), ((2 * tokens, hidden), BF16), (square, BF16), (square, BF16),
        ]

        def mlp_scratch(*more):
            buffers = vmem(*scratch, *more, sems=40)
            return buffers[:10] + buffers[-1:] + buffers[10:-1]

        both = (2 * tokens, wide)
        pair = (2 * unit_rows, hidden)
        out_a, dnm_a, keep_own, send_own, b_own_lo, b_own_hi, ub_own = call(
            lambda *r: mlp_kernel(True, *r),
            [(both, BF16), (both, BF16), *[(pair, BF16)] * 4, ((1, hidden), F32)],
            [SM] + [HB] * 4 + [VM] + [HB] * 2,
            "mlp_own",
            gflop=1,
            scratch=mlp_scratch((tall, BF16), (tall, BF16)),
            out_specs=[HB] * 6 + [VM],
        )(ids, nm, nm_sib, cotangent, ct_sib, vecs, up_weight, down_weight)
        out_own, out_sib, dnm_own, dnm_sib, keep_other, send_other, b_other_lo, b_other_hi, ub_other = call(
            lambda *r: mlp_kernel(False, *r),
            [
                (one, F32), (one, BF16), (one, F32), (one, BF16), *[(pair, BF16)] * 4,
                ((1, hidden), F32),
            ],
            [SM] + [HB] * 4 + [VM] + [HB] * 6,
            "mlp_other",
            gflop=12,
            scratch=mlp_scratch((tall, BF16), (tall, BF16), (one, F32), (one, BF16), (one, F32), (one, BF16)),
            out_specs=[HB] * 8 + [VM],
        )(ids, nm, nm_sib, cotangent, ct_sib, small_other, *mlp_parts, out_a, dnm_a)
        grad_units = (2 * UNITS * part_rows, 2 * width)
        whole, low_half, high_half, first, second = None, (0, 2), (2, 4), (0, 1), (1, 2)
        a_own = swap(send_own, NEAR)
        note(ub_other)
        a_own, dnm_sib, out_sib, send_other, b_other_hi, b_other_lo = turn(
            a_own, dnm_sib, out_sib, send_other, b_other_hi, b_other_lo
        )
        dnm_got = swap(dnm_sib, CORE)
        a_own2 = swap(total((high_half, high_half), keep_own, a_own), FAR)
        a_other = swap(send_other, NEAR)
        b_hi = swap(b_other_hi, TP)
        mg, dqkv_other, keep_o, send_o, sums_mid = call(
            other_back_kernel,
            [(one, F32), (acts, BF16), (grad_units, BF16), (grad_units, BF16), ((8, wide), F32)],
            [SM, SM, HB, HB, HB, HB, VM, HB, HB, HB] + [HB] * 8,
            "attn_other_back",
            gflop=10,
            scratch=vmem(
                (one, F32), (one, BF16), (one, BF16), (one, F32), (acts, BF16), (head, BF16), (one, BF16),
                (wo_shape, BF16), (one, F32), (one, BF16), (head, BF16), (acts, BF16),
                (w_shape, BF16), (wo_shape, BF16), sems=60,
            ),
            out_specs=[HB] * 4 + [VM],
        )(
            lengths, ids, dnm_own, dnm_got, cotangent, mid, vecs, qkv_other, att_other, nrm,
            *attn_parts, *attn_sib,
        )
        note(sums_mid)
        out_got = swap(turn(out_sib)[0], CORE)
        a_other, a_own2, b_hi, send_o = turn(a_other, a_own2, b_hi, send_o)
        o_sib = swap(send_o, CORE)
        a_other2 = swap(total((high_half, high_half), keep_other, a_other), FAR)
        o1 = swap(total((high_half, high_half), keep_o, o_sib), NEAR)
        b_lo = swap(b_other_lo, TP)
        mg_now, = turn(mg)
        dqkv_own, keep_s, send_s = call(
            own_back_kernel,
            [(acts, BF16), (grad_units, BF16), (grad_units, BF16)],
            [SM, SM] + [HB] * 5,
            "attn_own_back",
            gflop=10,
            scratch=vmem(
                (one, F32), (wo_shape, BF16), (acts, BF16), (head, BF16), (one, BF16),
                (one, BF16), (head, BF16), (acts, BF16), (w_shape, BF16), (wo_shape, BF16), sems=48,
            ),
            out_specs=[HB] * 3,
        )(lengths, ids, mg_now, out_weight, qkv_own, att_own, nrm)
        note(dqkv_own)
        a_other2, o1, b_lo, send_s = turn(a_other2, o1, b_lo, send_s)
        s_sib = swap(send_s, CORE)
        a_back = swap(total((low_half, low_half, whole), keep_other, a_other, a_other2), TP)
        s1 = swap(total((high_half, high_half), keep_s, s_sib), NEAR)
        o2 = swap(total((second, second, high_half), keep_o, o_sib, o1), FAR)
        b1 = swap(total((whole, whole), b_own_hi, b_hi), NEAR)
        a_unit = total((low_half, low_half, whole, whole), keep_own, a_own, a_own2, a_back)
        a_more = swap(a_unit, 1 << FIRST_REST)
        in_grad, vec = call(
            input_grad_kernel,
            [(one, BF16), ((16, wide), F32)],
            [SM, HB, HB, HB, HB, VM, HB, VM, VM, VM] + [HB] * 8,
            "input_grad",
            gflop=0.01,
            scratch=vmem(
                (acts, BF16), (acts, BF16), (one, F32), (one, BF16), (w_shape, BF16), (w_shape, BF16), (one, F32),
                sems=32,
            ),
        )(
            ids, dqkv_own, dqkv_other, *turn(mg), layer_in, vecs, w_own, sums_mid, ub_own, ub_other,
            *attn_parts, *attn_sib,
        )
        note(vec)

        def step(value, bit):
            mine, got = turn(value, swap(value, 1 << bit))
            return note(mine + got)

        def rest(unit, got):
            unit = total((whole, whole), unit, got)
            for bit in range(FIRST_REST + 1, bits):
                unit = total((whole, whole), unit, swap(unit, 1 << bit))
            return unit

        def step_with(value, got):
            mine, got = turn(value, got)
            return note(mine + got)

        s2 = swap(total((second, second, high_half), keep_s, s_sib, s1), FAR)
        o_back = swap(total((first, first, low_half, whole), keep_o, o_sib, o1, o2), TP)
        vec = step(vec, CORE_BIT)
        a_unit = rest(a_unit, a_more)
        a_near, a_far = swap(a_unit, NEAR), swap(a_unit, FAR)
        for bit in range(FIRST_REST, bits):
            vec = step(vec, bit)
        s_unit = total((first, first, low_half, whole, whole), keep_s, s_sib, s1, s2, o_back)
        s_more = swap(s_unit, 1 << FIRST_REST)
        vec_tp = swap(vec, TP)
        b2 = swap(total((high_half, high_half, high_half), b_own_lo, b_lo, b1), FAR)
        layer_out, = call(
            layer_out_kernel,
            [(one, BF16)],
            [HB, HB, HB, VM],
            "layer_out",
            gflop=0.01,
            scratch=vmem((one, F32), (one, F32), (one, BF16), sems=3),
        )(mid, out_own, *turn(out_got), vecs)
        note(layer_out)
        a_near, a_far, vec_tp, b2, s_more = due(a_near, a_far, vec_tp, b2, s_more)
        s_unit = rest(s_unit, s_more)
        s_units = share(s_unit)
        b_unit = total((low_half, low_half, low_half, whole), b_own_lo, b_lo, b1, b2)
        b_more = swap(b_unit, 1 << FIRST_REST)
        a_corner = swap(a_far, NEAR)
        vec = note(vec + vec_tp)
        *s_units, a_corner, b_more = due(*s_units, a_corner, b_more)
        b_unit = rest(b_unit, b_more)
        b_units = share(b_unit)
        vec_near = swap(vec, NEAR)
        a_units = [a_unit, a_near, a_far, a_corner]
        a_sib = [swap(value, CORE) for value in turn(*a_units)]
        s_sib = [swap(value, CORE) for value in turn(*s_units)]
        up_grad, qkv_grad, out_grad = call(
            place_two_kernel,
            [((wide, 2 * hidden), F32), ((3, wide, width), F32), ((width, wide), F32)],
            [SM] + [HB] * 16,
            "place_two",
            gflop=0.01,
            scratch=vmem(
                ((8, unit_rows, hidden), BF16), ((8, unit_rows, hidden), F32),
                ((8, 2 * part_rows, 2 * width), BF16), ((8, 2 * part_rows, 2 * width), F32), sems=56,
            ),
            out_specs=[HB] * 3,
            limit=32,
        )(ids, *turn(*a_units, *a_sib, *s_units, *s_sib))
        note(out_grad)
        vec = step_with(vec, vec_near)
        vec_far = swap(vec, FAR)
        *b_three, b_corner = b_units
        b_three = due(*b_three)
        b_sib = [swap(value, CORE) for value in b_three]
        *b_sib, vec_far, b_corner = due(*b_sib, vec_far, b_corner)
        b_sib.append(swap(b_corner, CORE))
        b_units = [*b_three, b_corner]
        vec = vec + vec_far
        down_grad, = call(
            place_down_kernel,
            [((2 * hidden, wide), F32)],
            [SM] + [HB] * 8,
            "place_down",
            scratch=vmem(((8, unit_rows, wide), BF16), ((8, unit_rows, wide), F32), sems=16),
            out_specs=[HB],
            limit=24,
        )(ids, *b_units, *b_sib)
        one_of = lambda i: vec[i]
        qvb = lax.dynamic_slice(vec, (6, half * width), (2, width))
        ub = lax.dynamic_slice(vec, (8 + 2 * half, 0), (2, hidden)).reshape(2 * hidden)
        return (
            layer_out, in_grad, one_of(0), one_of(1), jnp.transpose(qkv_grad, (1, 0, 2)), qvb,
            out_grad, one_of(4), one_of(2), one_of(3), up_grad, ub, down_grad, one_of(5),
        )

    return on_device


def solution(mesh):
    tokens, vector = P(("dp", "tp"), None), P()
    in_specs = (
        tokens, P("dp", None), vector, vector, P(None, None, "tp"), P(None, "tp"), P("tp", None), vector,
        vector, vector, P(None, "tp"), P("tp"), P("tp", None), vector, tokens,
    )
    out_specs = (
        tokens, tokens, vector, vector, P(None, None, "tp"), P(None, "tp"), P("tp", None), vector,
        vector, vector, P(None, "tp"), P("tp"), P("tp", None), vector,
    )
    return jax.shard_map(build(mesh), mesh=mesh, in_specs=in_specs, out_specs=out_specs, check_vma=False)
```

```python
import math

import jax
import jax.numpy as jnp
from jax import lax
from jax.experimental import pallas as pl
from jax.experimental.pallas import tpu as pltpu
from jax.sharding import PartitionSpec as P

HEAD = 64
SEQ = 128
UNITS = 4
EPS = 1e-05
SCALE = 1.0 / math.sqrt(HEAD)
F32 = jnp.float32
BF16 = jnp.bfloat16

VM = pl.BlockSpec(memory_space=pltpu.VMEM)
SM = pl.BlockSpec(memory_space=pltpu.SMEM)
HB = pl.BlockSpec(memory_space=pl.ANY)

NEAR_FIRST, FAR_FIRST = (0, 2, 1, 3), (0, 1, 2, 3)
TP_BIT, CORE_BIT, NEAR_BIT, FAR_BIT, FIRST_REST = 0, 1, 2, 3, 4
TP, CORE, NEAR, FAR = (1 << bit for bit in (TP_BIT, CORE_BIT, NEAR_BIT, FAR_BIT))


def nn(a, b):
    return lax.dot_general(a, b, (((1,), (0,)), ((), ())), preferred_element_type=F32)


def nt(a, b):
    return lax.dot_general(a, b, (((1,), (1,)), ((), ())), preferred_element_type=F32)


def tn(a, b):
    return lax.dot_general(a, b, (((0,), (0,)), ((), ())), preferred_element_type=F32)


def normalize(values):
    center = values - jnp.mean(values, axis=-1, keepdims=True)
    inv = lax.rsqrt(jnp.mean(center * center, axis=-1, keepdims=True) + EPS)
    return center * inv, inv


def norm_back(values, grad, gain):
    normed, inv = normalize(values)
    scaled = grad * gain
    mean_g = jnp.mean(scaled, axis=-1, keepdims=True)
    mean_gn = jnp.mean(scaled * normed, axis=-1, keepdims=True)
    part = inv * (scaled - mean_g - normed * mean_gn)
    gain_sum = jnp.sum(grad * normed, axis=0, keepdims=True)
    shift_sum = jnp.sum(grad, axis=0, keepdims=True)
    return part, gain_sum, shift_sum


def row_mask(lens, row):
    at_k = lax.broadcasted_iota(jnp.int32, (SEQ, 1), 0)
    at_q = lax.broadcasted_iota(jnp.int32, (1, SEQ), 1)
    total = jnp.int32(0)
    seg_q = jnp.zeros((1, SEQ), jnp.int32)
    seg_k = jnp.zeros((SEQ, 1), jnp.int32)
    for entry in range(lens.shape[1]):
        total = total + lens[row, entry]
        seg_q = seg_q + jnp.where(at_q >= total, 1, 0)
        seg_k = seg_k + jnp.where(at_k >= total, 1, 0)
    allowed = (seg_q == seg_k) & (at_k <= at_q) & ((at_k < total) | (at_k == at_q))
    valid = jnp.where(at_k < total, 1.0, 0.0).astype(F32)
    return jnp.concatenate([allowed, allowed], axis=1), valid


def low_lanes():
    return lax.broadcasted_iota(jnp.int32, (SEQ, 2 * HEAD), 1) < HEAD


def stack_pair(pair, low):
    zero = jnp.zeros_like(pair)
    return jnp.concatenate([jnp.where(low, pair, zero), jnp.where(low, zero, pair)], axis=0)


def pair_probs(q_stack, keys, allowed2):
    scores = jnp.where(allowed2, nt(keys, q_stack) * SCALE, -1e30)
    weights = jnp.exp(scores - jnp.max(scores, axis=0, keepdims=True))
    return weights * (1.0 / jnp.sum(weights, axis=0, keepdims=True))


class Copies:
    def __init__(self, sems):
        self.sems = sems
        self.count = 0

    def start(self, src, dst):
        made = pltpu.make_async_copy(src, dst, self.sems.at[self.count])
        self.count += 1
        made.start()
        return made


def wait(*copies):
    for made in copies:
        made.wait()


def blocks(count, size=SEQ):
    return [slice(i * size, (i + 1) * size) for i in range(count)]


def over_rows(tokens, body, start):
    at = lambda i: pl.ds(pl.multiple_of(i * SEQ, SEQ), SEQ)
    return lax.fori_loop(0, tokens // SEQ, lambda i, carry: body(at(i), carry), start)


def project(nrm, w, bias, qkv):
    width = w.shape[2]
    for part in range(3):
        value = nn(nrm[...], w[part])
        if part != 1:
            value = value + bias[part // 2]
        qkv[:, part * width : (part + 1) * width] = value.astype(BF16)


def attend(lens, ids, qkv, att):
    width = att.shape[1]
    rows = att.shape[0] // SEQ
    low = low_lanes()
    @pl.loop(0, rows, unroll=2)
    def _(row):
        at = pl.ds(pl.multiple_of(row * SEQ, SEQ), SEQ)
        allowed2, valid = row_mask(lens, ids[0] * rows + row)
        for first in range(0, width, 2 * HEAD):
            q = qkv[at, first : first + 2 * HEAD]
            k = qkv[at, width + first : width + first + 2 * HEAD]
            v = qkv[at, 2 * width + first : 2 * width + first + 2 * HEAD]
            probs = pair_probs(stack_pair(q, low), k, allowed2)
            both = tn(probs.astype(BF16), v)
            out = jnp.where(low, both[:SEQ], both[SEQ:]) * valid
            att[at, first : first + 2 * HEAD] = out.astype(BF16)


def own_fwd_kernel(lens, ids, x_hbm, vecs, w_hbm, bias, nrm_hbm, qkv_hbm, att, x, w, nrm, qkv, sems):
    copies = Copies(sems)
    x_in = copies.start(x_hbm, x)
    w_in = copies.start(w_hbm, w)
    wait(x_in)

    def norm_rows(at, carry):
        normed, _ = normalize(x[at, :].astype(F32))
        nrm[at, :] = (normed * vecs[0:1, :] + vecs[1:2, :]).astype(BF16)
        return carry

    over_rows(x.shape[0], norm_rows, 0)
    nrm_out = copies.start(nrm, nrm_hbm)
    wait(w_in)
    project(nrm, w, [bias[0:1, :], bias[1:2, :]], qkv)
    qkv_out = copies.start(qkv, qkv_hbm)
    attend(lens, ids, qkv, att)
    wait(nrm_out, qkv_out)


def unit_block(part, rows, width, first=0):
    return pl.ds(first + (part // 2) * rows, rows), pl.ds((part % 2) * width, width)


def fetch_weights(copies, ids, mine_parts, sib_parts, w, wo):
    core, mine = ids[1], ids[2]
    width = w.shape[2]
    part_rows = w.shape[1] // (2 * UNITS)
    to_w, to_wo = [], []
    for side, parts in ((core, mine_parts), (1 - core, sib_parts)):
        for step, unit_ref in enumerate(parts):
            unit = jnp.bitwise_xor(mine, step)
            at_w = pl.ds(pl.multiple_of((side * UNITS + unit) * part_rows, part_rows), part_rows)
            at_o = pl.ds(pl.multiple_of(unit * part_rows, part_rows), part_rows)
            cols = pl.ds(pl.multiple_of(side * width, width), width)
            for part in range(3):
                to_w.append(copies.start(unit_ref.at[unit_block(part, part_rows, width)], w.at[part, at_w, :]))
            if wo is not None:
                to_wo.append(copies.start(unit_ref.at[unit_block(3, part_rows, width)], wo.at[at_o, cols]))
    return to_w, to_wo


def fetch_output_weight(copies, ids, mine_parts, sib_parts, wo):
    core, mine = ids[1], ids[2]
    width = wo.shape[0]
    part_rows = width // UNITS
    made = []
    for side, parts in ((core, mine_parts), (1 - core, sib_parts)):
        for step, unit_ref in enumerate(parts):
            at_o = pl.ds(pl.multiple_of(jnp.bitwise_xor(mine, step) * part_rows, part_rows), part_rows)
            cols = pl.ds(pl.multiple_of(side * width, width), width)
            made.append(copies.start(unit_ref.at[unit_block(3, part_rows, width)], wo.at[at_o, cols]))
    return made


def other_fwd_kernel(lens, ids, x_hbm, nrm_hbm, bias, att_own_hbm, wo_own_hbm, vecs, *refs):
    mine_parts, sib_parts = refs[:4], refs[4:8]
    qkv_hbm, att_hbm, mid_hbm, nm = refs[8:12]
    x, nrm, att_own, wo_own, w, wo, qkv, att, mid, sems = refs[12:]
    copies = Copies(sems)
    nrm_in = copies.start(nrm_hbm, nrm)
    to_w, to_wo = fetch_weights(copies, ids, mine_parts, sib_parts, w, wo)
    late = [copies.start(x_hbm, x), copies.start(att_own_hbm, att_own), copies.start(wo_own_hbm, wo_own)]
    wait(nrm_in, *to_w)
    half = w.shape[2]
    project(nrm, w, [bias[0:1, :half], bias[0:1, half:]], qkv)
    qkv_out = copies.start(qkv, qkv_hbm)
    attend(lens, ids, qkv, att)
    att_out = copies.start(att, att_hbm)
    wait(*to_wo, *late)
    mid[...] = nn(att_own[...], wo_own[...]) + nn(att[...], wo[...])

    def norm_rows(at, carry):
        value = x[at, :].astype(F32) + mid[at, :] + vecs[2:3, :]
        mid[at, :] = value
        normed, _ = normalize(value)
        nm[at, :] = (normed * vecs[3:4, :] + vecs[4:5, :]).astype(BF16)
        return carry

    over_rows(x.shape[0], norm_rows, 0)
    mid_out = copies.start(mid, mid_hbm)
    wait(qkv_out, att_out, mid_out)


def gelu_parts(pre):
    bell = jnp.exp2(pre * pre * (-0.5 * math.log2(math.e)))
    t = 1.0 / (1.0 + (0.3275911 * math.sqrt(0.5)) * jnp.abs(pre))
    poly = 0.5307027145 * t - 0.7265760135
    poly = poly * t + 0.7107068705
    poly = poly * t - 0.142248368
    poly = poly * t + 0.127414796
    tail = poly * t * bell
    cdf = jnp.where(pre >= 0, 1.0 - tail, tail)
    return pre * cdf, cdf + pre * bell * (1.0 / math.sqrt(2.0 * math.pi))


def mlp_kernel(own, *refs):
    ids, nm_a, nm_b, ct_a, ct_b, biases = refs[:6]
    if own:
        up_hbm, down_hbm = refs[6:8]
        out_hbm, dnm_hbm, keep_a, send_a, keep_b, send_b, bias_g = refs[8:15]
        scratch = refs[15:]
    else:
        units, (out_prev, dnm_prev) = refs[6:10], refs[10:12]
        out_own_hbm, out_sib_hbm, dnm_own_hbm, dnm_sib_hbm, keep_a, send_a, keep_b, send_b, bias_g = refs[12:21]
        scratch = refs[21:]
    up, down, nm, ct, pre, dact, act, pg, gu, gd, sems = scratch[:11]
    core, mine = ids[1], ids[2]
    hidden = up.shape[1]
    tokens = nm_a.shape[0]
    unit_rows = up.shape[0] // UNITS
    copies = Copies(sems)
    copy = copies.start
    halves = (pl.ds(0, tokens), pl.ds(tokens, tokens))

    def unit_at(step):
        start = jnp.bitwise_xor(mine, step) * unit_rows
        return pl.ds(pl.multiple_of(start, unit_rows), unit_rows)

    at = pl.ds(pl.multiple_of(core * hidden, hidden), hidden)
    if own:
        ups = [copy(up_hbm.at[:, at], up)]
    else:
        ups = [copy(unit.at[pl.ds(0, unit_rows)], up.at[unit_at(i), :]) for i, unit in enumerate(units)]
    nms = [copy(nm_a, nm.at[halves[0]])]
    if own:
        downs = [copy(down_hbm.at[at, :], down)]
    else:
        downs = [copy(unit.at[pl.ds(unit_rows, unit_rows)], down.at[unit_at(i), :]) for i, unit in enumerate(units)]
    cts = [copy(ct_a, ct.at[halves[0]])]
    nms.append(copy(nm_b, nm.at[halves[1]]))
    cts.append(copy(ct_b, ct.at[halves[1]]))
    if not own:
        prev_out, prev_dnm, dnm_own, dnm_sib, out_own, out_sib = scratch[11:17]
        lates = [copy(dnm_prev, prev_dnm), copy(out_prev, prev_out)]
    else:
        dnm, out = scratch[11:13]

    piece = 32

    def half_step(half, total):
        rows = pl.ds(pl.multiple_of(half * tokens, tokens), tokens)
        for i in range(2):
            pl.when(half == i)(lambda: wait(nms[i], *(ups if i == 0 else ())))
        pre[...] = nn(nm[rows, :], up[...])
        for i in range(2):
            pl.when(half == i)(lambda: wait(cts[i], *(downs if i == 0 else ())))
        dact[...] = nt(ct[rows, :], down[...])

        def elementwise(step, total):
            at = pl.ds(pl.multiple_of(step * piece, piece), piece)
            to = pl.ds(pl.multiple_of(half * tokens + step * piece, piece), piece)
            value, slope = gelu_parts(pre[at, :] + bias)
            act[to, :] = value.astype(BF16)
            back = dact[at, :] * slope
            pg[to, :] = back.astype(BF16)
            return total + jnp.sum(back.reshape(piece // 8, 8, hidden), axis=0)

        return lax.fori_loop(0, tokens // piece, elementwise, total)

    bias = biases[pl.ds((6 if own else 1 + core), 1), :]
    bias_sum = lax.fori_loop(0, 2, half_step, jnp.zeros((8, hidden), F32))
    bias_g[...] = jnp.sum(bias_sum, axis=0, keepdims=True)
    writes = []
    if own:
        dnm[...] = nt(pg[...], up[...]).astype(BF16)
        writes.append(copy(dnm, dnm_hbm))
        out[...] = nn(act[...], down[...]).astype(BF16)
        writes.append(copy(out, out_hbm))
    else:
        wait(*lates)
        total = nt(pg[...], up[...])
        dnm_own[...] = total[:tokens] + prev_dnm[:tokens, :].astype(F32)
        dnm_sib[...] = (total[tokens:] + prev_dnm[tokens:, :].astype(F32)).astype(BF16)
        writes += [copy(dnm_own, dnm_own_hbm), copy(dnm_sib, dnm_sib_hbm)]
        total = nn(act[...], down[...])
        out_own[...] = total[:tokens] + prev_out[:tokens, :].astype(F32)
        out_sib[...] = (total[tokens:] + prev_out[tokens:, :].astype(F32)).astype(BF16)
        writes += [copy(out_own, out_own_hbm), copy(out_sib, out_sib_hbm)]
    for source, grad, order, targets in (
        (gd, lambda: tn(act[...], ct[...]), NEAR_FIRST, (keep_b, send_b)),
        (gu, lambda: tn(nm[...], pg[...]), NEAR_FIRST, (keep_a, send_a)),
    ):
        source[...] = grad().astype(BF16)
        for place, step in enumerate(order):
            to = targets[place // 2].at[pl.ds((place % 2) * unit_rows, unit_rows)]
            writes.append(copy(source.at[unit_at(step), :], to))
    wait(*writes)


def attend_back(lens, ids, qkv, datt, dqkv):
    width = datt.shape[1]
    rows = datt.shape[0] // SEQ
    low = low_lanes()

    @pl.loop(0, rows)
    def _(row):
        allowed2, valid = row_mask(lens, ids[0] * rows + row)
        at = pl.ds(pl.multiple_of(row * SEQ, SEQ), SEQ)
        for first in range(0, width, 2 * HEAD):
            q_cols = slice(first, first + 2 * HEAD)
            k_cols = slice(width + first, width + first + 2 * HEAD)
            v_cols = slice(2 * width + first, 2 * width + first + 2 * HEAD)
            k = qkv[at, k_cols]
            q_stack = stack_pair(qkv[at, q_cols], low)
            grad = (datt[at, q_cols].astype(F32) * valid).astype(BF16)
            g_stack = stack_pair(grad, low)
            probs = pair_probs(q_stack, k, allowed2)
            dqkv[at, v_cols] = nn(probs.astype(BF16), g_stack).astype(BF16)
            prob_grad = nt(qkv[at, v_cols], g_stack)
            inner = jnp.sum(probs * prob_grad, axis=0, keepdims=True)
            score_grad = (probs * (prob_grad - inner)).astype(BF16)
            both = tn(score_grad, k)
            dqkv[at, q_cols] = (jnp.where(low, both[:SEQ], both[SEQ:]) * SCALE).astype(BF16)
            dqkv[at, k_cols] = (nn(score_grad, q_stack) * SCALE).astype(BF16)


def weight_grads(copies, ids, nrm, dqkv, dw, dwo, order, keep, send):
    core, mine = ids[1], ids[2]
    width = dw.shape[2]
    part_rows = dw.shape[1] // (2 * UNITS)
    made = []
    for part in (3, 2, 1, 0):
        if part < 3:
            dw[part] = tn(nrm[...], dqkv[:, part * width : (part + 1) * width]).astype(BF16)
        for place in range(UNITS):
            unit = jnp.bitwise_xor(mine, order[place])
            for side, target in ((1 - core, send), (core, keep)):
                at_w = pl.ds(pl.multiple_of((side * UNITS + unit) * part_rows, part_rows), part_rows)
                at_o = pl.ds(pl.multiple_of(unit * part_rows, part_rows), part_rows)
                cols = pl.ds(pl.multiple_of(side * width, width), width)
                source = dw.at[part, at_w, :] if part < 3 else dwo.at[at_o, cols]
                made.append(copies.start(source, target.at[unit_block(part, part_rows, width, 2 * place * part_rows)]))
    return made


def bias_sums(dqkv):
    width = dqkv.shape[1] // 3
    ones = jnp.ones((8, dqkv.shape[0]), BF16)
    return [nn(ones, dqkv[:, first : first + width])[0:1] for first in (0, 2 * width)]


def normed_grad(dqkv, w):
    width = w.shape[2]
    total = nt(dqkv[:, :width], w[0])
    for part in range(1, 3):
        total = total + nt(dqkv[:, part * width : (part + 1) * width], w[part])
    return total


def other_back_kernel(lens, ids, dnm_own_hbm, dnm_sib_hbm, ct_hbm, mid_hbm, vecs, qkv_hbm, att_hbm, nrm_hbm, *refs):
    mine_parts, sib_parts = refs[:4], refs[4:8]
    mg_hbm, dqkv_hbm, keep, send, sums = refs[8:13]
    dnm_own, dnm_sib, ct, mid, qkv, att, nrm, wo, mg, ml, datt, dqkv, dw, dwo, sems = refs[13:]
    copies = Copies(sems)
    first_in = [
        copies.start(dnm_own_hbm, dnm_own), copies.start(dnm_sib_hbm, dnm_sib),
        copies.start(ct_hbm, ct), copies.start(mid_hbm, mid),
    ]
    to_wo = fetch_output_weight(copies, ids, mine_parts, sib_parts, wo)
    qkv_in, att_in, nrm_in = copies.start(qkv_hbm, qkv), copies.start(att_hbm, att), copies.start(nrm_hbm, nrm)
    wait(*first_in)

    def back_rows(at, totals):
        grad = dnm_own[at, :] + dnm_sib[at, :].astype(F32)
        part, gain_sum, shift_sum = norm_back(mid[at, :], grad, vecs[3:4, :])
        out_grad = ct[at, :].astype(F32)
        value = out_grad + part
        mg[at, :] = value
        ml[at, :] = value.astype(BF16)
        adds = (gain_sum, shift_sum, jnp.sum(value, axis=0, keepdims=True), jnp.sum(out_grad, axis=0, keepdims=True))
        return tuple(total + add for total, add in zip(totals, adds))

    totals = over_rows(mid.shape[0], back_rows, (jnp.zeros((1, mid.shape[1]), F32),) * 4)
    sums[...] = jnp.concatenate(list(totals) + [jnp.zeros((4, mid.shape[1]), F32)])
    mg_out = copies.start(mg, mg_hbm)
    wait(*to_wo, qkv_in, att_in)
    datt[...] = nt(ml[...], wo[...]).astype(BF16)
    dwo[...] = tn(att[...], ml[...]).astype(BF16)
    attend_back(lens, ids, qkv, datt, dqkv)
    wait(nrm_in)
    dqkv_out = copies.start(dqkv, dqkv_hbm)
    outs = weight_grads(copies, ids, nrm, dqkv, dw, dwo, NEAR_FIRST, keep, send)
    wait(mg_out, dqkv_out, *outs)


def own_back_kernel(
    lens, ids, mg_hbm, wo_hbm, qkv_hbm, att_hbm, nrm_hbm, dqkv_hbm, keep, send,
    mg, wo, qkv, att, nrm, ml, datt, dqkv, dw, dwo, sems,
):
    copies = Copies(sems)
    mg_in, wo_in = copies.start(mg_hbm, mg), copies.start(wo_hbm, wo)
    att_in, qkv_in, nrm_in = copies.start(att_hbm, att), copies.start(qkv_hbm, qkv), copies.start(nrm_hbm, nrm)
    wait(mg_in)
    ml[...] = mg[...].astype(BF16)
    wait(wo_in, att_in, qkv_in)
    datt[...] = nt(ml[...], wo[...]).astype(BF16)
    dwo[...] = tn(att[...], ml[...]).astype(BF16)
    attend_back(lens, ids, qkv, datt, dqkv)
    dqkv_out = copies.start(dqkv, dqkv_hbm)
    wait(nrm_in)
    outs = weight_grads(copies, ids, nrm, dqkv, dw, dwo, NEAR_FIRST, keep, send)
    wait(dqkv_out, *outs)


def input_grad_kernel(ids, dqkv_a_hbm, dqkv_b_hbm, mg_hbm, x_hbm, vecs, w_hbm, sums, ub_own, ub_other, *refs):
    mine_parts, sib_parts = refs[:4], refs[4:8]
    in_grad, vec = refs[8:10]
    dqkv_a, dqkv_b, mg, x, w_own, w_other, dn, sems = refs[10:]
    half, core = ids[0], ids[1]
    copies = Copies(sems)
    own_in = [copies.start(dqkv_a_hbm, dqkv_a), copies.start(w_hbm, w_own)]
    other_in, _ = fetch_weights(copies, ids, mine_parts, sib_parts, w_other, None)
    other_in.append(copies.start(dqkv_b_hbm, dqkv_b))
    late = [copies.start(mg_hbm, mg), copies.start(x_hbm, x)]
    width = w_own.shape[2]
    wait(*own_in)
    dn[...] = normed_grad(dqkv_a, w_own)
    wait(*other_in)
    dn[...] += normed_grad(dqkv_b, w_other)
    wait(*late)

    def back_rows(at, totals):
        part, gain_sum, shift_sum = norm_back(x[at, :].astype(F32), dn[at, :], vecs[0:1, :])
        in_grad[at, :] = (mg[at, :] + part).astype(BF16)
        return totals[0] + gain_sum, totals[1] + shift_sum

    totals = over_rows(x.shape[0], back_rows, (jnp.zeros((1, x.shape[1]), F32),) * 2)
    vec[...] = jnp.zeros_like(vec)
    for i in range(2):
        vec[i : i + 1, :] = totals[i]
    vec[2:6, :] = sums[0:4, :]
    for dqkv, side in ((dqkv_a, half), (dqkv_b, 1 - half)):
        for i, value in enumerate(bias_sums(dqkv)):
            vec[6 + i : 7 + i, pl.ds(pl.multiple_of(side * width, width), width)] = value
    vec[pl.ds(8 + 2 * half + core, 1), :] = ub_own[...]
    vec[pl.ds(8 + 2 * (1 - half) + core, 1), :] = ub_other[...]


def layer_out_kernel(mid_hbm, own_hbm, sib_hbm, vecs, out, mid, own, sib, sems):
    copies = Copies(sems)
    wait(copies.start(mid_hbm, mid), copies.start(own_hbm, own), copies.start(sib_hbm, sib))

    def rows(at, carry):
        out[at, :] = (mid[at, :] + own[at, :] + sib[at, :].astype(F32) + vecs[5:6, :]).astype(BF16)
        return carry

    over_rows(out.shape[0], rows, 0)


class Placing:
    def __init__(self, ids, copies):
        self.core, self.mine = ids[1], ids[2]
        self.copies = copies
        self.work, self.outs = [], []

    def take(self, refs, narrow, wide, targets):
        for i, ref in enumerate(refs):
            side = self.core if i < UNITS else 1 - self.core
            unit = jnp.bitwise_xor(self.mine, i % UNITS)
            self.work.append((self.copies.start(ref, narrow.at[i]), narrow, wide, i, targets(side, unit)))

    def finish(self):
        for arrived, narrow, wide, i, targets in self.work:
            arrived.wait()
            wide[i] = narrow[i].astype(F32)
            for block, target in targets:
                self.outs.append(self.copies.start(wide.at[i, block[0], block[1]], target))
        wait(*self.outs)


def mlp_targets(out, down_first, rows, width):
    def targets(side, unit):
        base, start = pl.multiple_of(side * width, width), pl.multiple_of(unit * rows, rows)
        if down_first:
            target = out.at[pl.ds(pl.multiple_of(base + start, rows), rows), :]
        else:
            target = out.at[pl.ds(start, rows), pl.ds(base, width)]
        return [((pl.ds(0, rows), pl.ds(0, width)), target)]

    return targets


def attn_targets(w, wo):
    width = w.shape[2]
    rows = w.shape[1] // (2 * UNITS)

    def targets(side, unit):
        at_w = pl.ds(pl.multiple_of((side * UNITS + unit) * rows, rows), rows)
        at_o = pl.ds(pl.multiple_of(unit * rows, rows), rows)
        cols = pl.ds(pl.multiple_of(side * width, width), width)
        places = [w.at[part, at_w, :] for part in range(3)] + [wo.at[at_o, cols]]
        return [(unit_block(part, rows, width), place) for part, place in enumerate(places)]

    return targets


def place_mlp_kernel(down_first, ids, *refs):
    units, (out, narrow, wide, sems) = refs[:8], refs[8:]
    placing = Placing(ids, Copies(sems))
    placing.take(units, narrow, wide, mlp_targets(out, down_first, *units[0].shape))
    placing.finish()


def place_down_kernel(*refs):
    place_mlp_kernel(True, *refs)


def place_two_kernel(ids, *refs):
    up_units, attn_units = refs[:8], refs[8:16]
    up, w, wo, narrow_u, wide_u, narrow_a, wide_a, sems = refs[16:]
    placing = Placing(ids, Copies(sems))
    placing.take(up_units, narrow_u, wide_u, mlp_targets(up, False, *up_units[0].shape))
    placing.take(attn_units, narrow_a, wide_a, attn_targets(w, wo))
    placing.finish()


def vmem(*buffers, sems):
    return [pltpu.VMEM(shape, dtype) for shape, dtype in buffers] + [pltpu.SemaphoreType.DMA((sems,))]


def call(kernel, outs, in_specs, name, scratch=(), out_specs=None, limit=61, gflop=1.0):
    return pl.pallas_call(
        kernel,
        out_shape=tuple(jax.ShapeDtypeStruct(shape, dtype) for shape, dtype in outs),
        in_specs=in_specs,
        out_specs=tuple(VM for _ in outs) if out_specs is None else tuple(out_specs),
        scratch_shapes=list(scratch),
        name=name,
        cost_estimate=pl.CostEstimate(flops=int(gflop * 1e9), bytes_accessed=8 << 20, transcendentals=0),
        compiler_params=pltpu.CompilerParams(vmem_limit_bytes=limit * 1024 * 1024),
    )


def build(mesh):
    devices = mesh.shape["dp"] * mesh.shape["tp"]
    bits = devices.bit_length() - 1

    def swap(value, mask):
        return lax.ppermute(value, ("dp", "tp"), [(i, i ^ mask) for i in range(devices)])

    def after(value, *deps):
        return lax.optimization_barrier((value, deps))[0]

    def share(unit):
        return [unit] + [swap(unit, mask) for mask in (NEAR, FAR, NEAR | FAR)]

    def add(*terms):
        total = terms[0].astype(F32)
        for term in terms[1:]:
            total = total + term.astype(F32)
        return total

    last = []

    def turn(*values):
        return lax.optimization_barrier((values, last[-1]))[0]

    def note(value):
        last.append(value)
        return value

    def due(*values):
        values = turn(*values)
        note(values[-1])
        return values

    def total(parts, *terms):
        cut = lambda v, part: v if part is None else v[v.shape[0] * part[0] // 4 : v.shape[0] * part[1] // 4]
        return note(add(*[cut(term, part) for term, part in zip(turn(*terms), parts)]).astype(BF16))

    def on_device(
        layer_in, lengths, attn_gain, attn_shift, qkv_weight, qv_bias, out_weight, out_bias,
        mlp_gain, mlp_shift, up_weight, up_bias, down_weight, down_bias, cotangent,
    ):
        tokens, wide = layer_in.shape
        width = qkv_weight.shape[2]
        hidden = up_weight.shape[1] // 2
        flat = lax.axis_index("dp") * 2 + lax.axis_index("tp")
        half = lax.axis_index("tp")
        core = (flat >> CORE_BIT) & 1
        mine = ((flat >> FAR_BIT) & 1) * 2 + ((flat >> NEAR_BIT) & 1)
        ids = jnp.stack([half, core, mine]).astype(jnp.int32)
        up_bias_own = lax.dynamic_slice(up_bias, (core * hidden,), (hidden,))
        vecs = jnp.stack([attn_gain, attn_shift, out_bias, mlp_gain, mlp_shift, down_bias, up_bias_own, up_bias_own])
        w_own = jnp.transpose(qkv_weight, (1, 0, 2))

        part_rows = wide // (2 * UNITS)
        unit_w = lax.dynamic_slice(w_own, (0, (core * UNITS + mine) * part_rows, 0), (3, part_rows, width))
        unit_o = lax.dynamic_slice(out_weight, (mine * part_rows, core * width), (part_rows, width))
        attn_unit = jnp.concatenate(
            [jnp.concatenate([unit_w[0], unit_w[1]], axis=1), jnp.concatenate([unit_w[2], unit_o], axis=1)]
        )
        attn_unit = swap(attn_unit, TP)

        acts = (tokens, 3 * width)
        one = (tokens, wide)
        head = (tokens, width)
        w_shape, wo_shape = (3, wide, width), (width, wide)
        nrm, qkv_own, att_own = call(
            own_fwd_kernel,
            [(one, BF16), (acts, BF16), (head, BF16)],
            [SM, SM, HB, VM, HB, VM],
            "attn_own_fwd",
            gflop=0.5,
            scratch=vmem((one, BF16), (w_shape, BF16), (one, BF16), (acts, BF16), sems=4),
            out_specs=[HB, HB, VM],
        )(lengths, ids, layer_in, vecs, w_own, qv_bias)
        attn_parts = share(after(attn_unit, att_own))
        unit_rows = hidden // UNITS
        up_late, down_late, bias_late, up_bias_late = after((up_weight, down_weight, qv_bias, up_bias), att_own)
        mlp_unit = jnp.concatenate(
            [
                lax.dynamic_slice(up_late, (mine * unit_rows, core * hidden), (unit_rows, hidden)),
                lax.dynamic_slice(down_late, (core * hidden + mine * unit_rows, 0), (unit_rows, wide)),
            ]
        )
        mlp_unit = swap(mlp_unit, TP)
        small = jnp.concatenate([bias_late.reshape(-1), up_bias_late])
        small_other = swap(small.reshape(3, wide), TP)
        ct_sib = swap(cotangent, CORE)
        attn_sib = [swap(part, CORE) for part in attn_parts]
        qkv_other, att_other, mid, nm = call(
            other_fwd_kernel,
            [(acts, BF16), (head, BF16), (one, F32), (one, BF16)],
            [SM, SM, HB, HB, VM, HB, HB, VM] + [HB] * 8,
            "attn_other_fwd",
            gflop=6,
            scratch=vmem(
                (one, BF16), (one, BF16), (head, BF16), (wo_shape, BF16), (w_shape, BF16), (wo_shape, BF16),
                (acts, BF16), (head, BF16), (one, F32), sems=40,
            ),
            out_specs=[HB, HB, HB, VM],
        )(
            lengths, ids, layer_in, after(nrm, mlp_unit), small_other, att_own, out_weight, vecs,
            *attn_parts, *attn_sib,
        )
        mlp_near, mlp_far = swap(mlp_unit, NEAR), swap(mlp_unit, FAR)

        mlp_near, mlp_far, nm = after((mlp_near, mlp_far, nm))
        mlp_parts = [mlp_unit, mlp_near, mlp_far, swap(mlp_unit, NEAR | FAR)]
        nm_sib = swap(nm, CORE)
        tall, square = (2 * tokens, wide), (wide, hidden)
        scratch = [
            (square, BF16), (square, BF16), (tall, BF16), (tall, BF16), ((tokens, hidden), F32), ((tokens, hidden), F32),
            ((2 * tokens, hidden), BF16), ((2 * tokens, hidden), BF16), (square, BF16), (square, BF16),
        ]

        def mlp_scratch(*more):
            buffers = vmem(*scratch, *more, sems=40)
            return buffers[:10] + buffers[-1:] + buffers[10:-1]

        both = (2 * tokens, wide)
        pair = (2 * unit_rows, hidden)
        out_a, dnm_a, keep_own, send_own, b_own_lo, b_own_hi, ub_own = call(
            lambda *r: mlp_kernel(True, *r),
            [(both, BF16), (both, BF16), *[(pair, BF16)] * 4, ((1, hidden), F32)],
            [SM] + [HB] * 4 + [VM] + [HB] * 2,
            "mlp_own",
            gflop=1,
            scratch=mlp_scratch((tall, BF16), (tall, BF16)),
            out_specs=[HB] * 6 + [VM],
        )(ids, nm, nm_sib, cotangent, ct_sib, vecs, up_weight, down_weight)
        out_own, out_sib, dnm_own, dnm_sib, keep_other, send_other, b_other_lo, b_other_hi, ub_other = call(
            lambda *r: mlp_kernel(False, *r),
            [
                (one, F32), (one, BF16), (one, F32), (one, BF16), *[(pair, BF16)] * 4,
                ((1, hidden), F32),
            ],
            [SM] + [HB] * 4 + [VM] + [HB] * 6,
            "mlp_other",
            gflop=12,
            scratch=mlp_scratch((tall, BF16), (tall, BF16), (one, F32), (one, BF16), (one, F32), (one, BF16)),
            out_specs=[HB] * 8 + [VM],
        )(ids, nm, nm_sib, cotangent, ct_sib, small_other, *mlp_parts, out_a, dnm_a)
        grad_units = (2 * UNITS * part_rows, 2 * width)
        whole, low_half, high_half, first, second = None, (0, 2), (2, 4), (0, 1), (1, 2)
        a_own = swap(send_own, NEAR)
        note(ub_other)
        a_own, dnm_sib, out_sib, send_other, b_other_hi, b_other_lo = turn(
            a_own, dnm_sib, out_sib, send_other, b_other_hi, b_other_lo
        )
        dnm_got = swap(dnm_sib, CORE)
        a_own2 = swap(total((high_half, high_half), keep_own, a_own), FAR)
        a_other = swap(send_other, NEAR)
        b_hi = swap(b_other_hi, TP)
        mg, dqkv_other, keep_o, send_o, sums_mid = call(
            other_back_kernel,
            [(one, F32), (acts, BF16), (grad_units, BF16), (grad_units, BF16), ((8, wide), F32)],
            [SM, SM, HB, HB, HB, HB, VM, HB, HB, HB] + [HB] * 8,
            "attn_other_back",
            gflop=10,
            scratch=vmem(
                (one, F32), (one, BF16), (one, BF16), (one, F32), (acts, BF16), (head, BF16), (one, BF16),
                (wo_shape, BF16), (one, F32), (one, BF16), (head, BF16), (acts, BF16),
                (w_shape, BF16), (wo_shape, BF16), sems=60,
            ),
            out_specs=[HB] * 4 + [VM],
        )(
            lengths, ids, dnm_own, dnm_got, cotangent, mid, vecs, qkv_other, att_other, nrm,
            *attn_parts, *attn_sib,
        )
        note(sums_mid)
        out_got = swap(turn(out_sib)[0], CORE)
        a_other, a_own2, b_hi, send_o = turn(a_other, a_own2, b_hi, send_o)
        o_sib = swap(send_o, CORE)
        a_other2 = swap(total((high_half, high_half), keep_other, a_other), FAR)
        o1 = swap(total((high_half, high_half), keep_o, o_sib), NEAR)
        b_lo = swap(b_other_lo, TP)
        mg_now, = turn(mg)
        dqkv_own, keep_s, send_s = call(
            own_back_kernel,
            [(acts, BF16), (grad_units, BF16), (grad_units, BF16)],
            [SM, SM] + [HB] * 5,
            "attn_own_back",
            gflop=10,
            scratch=vmem(
                (one, F32), (wo_shape, BF16), (acts, BF16), (head, BF16), (one, BF16),
                (one, BF16), (head, BF16), (acts, BF16), (w_shape, BF16), (wo_shape, BF16), sems=48,
            ),
            out_specs=[HB] * 3,
        )(lengths, ids, mg_now, out_weight, qkv_own, att_own, nrm)
        note(dqkv_own)
        a_other2, o1, b_lo, send_s = turn(a_other2, o1, b_lo, send_s)
        s_sib = swap(send_s, CORE)
        a_back = swap(total((low_half, low_half, whole), keep_other, a_other, a_other2), TP)
        s1 = swap(total((high_half, high_half), keep_s, s_sib), NEAR)
        o2 = swap(total((second, second, high_half), keep_o, o_sib, o1), FAR)
        b1 = swap(total((whole, whole), b_own_hi, b_hi), NEAR)
        a_unit = total((low_half, low_half, whole, whole), keep_own, a_own, a_own2, a_back)
        a_more = swap(a_unit, 1 << FIRST_REST)
        in_grad, vec = call(
            input_grad_kernel,
            [(one, BF16), ((16, wide), F32)],
            [SM, HB, HB, HB, HB, VM, HB, VM, VM, VM] + [HB] * 8,
            "input_grad",
            gflop=0.01,
            scratch=vmem(
                (acts, BF16), (acts, BF16), (one, F32), (one, BF16), (w_shape, BF16), (w_shape, BF16), (one, F32),
                sems=32,
            ),
        )(
            ids, dqkv_own, dqkv_other, *turn(mg), layer_in, vecs, w_own, sums_mid, ub_own, ub_other,
            *attn_parts, *attn_sib,
        )
        note(vec)

        def step(value, bit):
            mine, got = turn(value, swap(value, 1 << bit))
            return note(mine + got)

        def rest(unit, got):
            unit = total((whole, whole), unit, got)
            for bit in range(FIRST_REST + 1, bits):
                unit = total((whole, whole), unit, swap(unit, 1 << bit))
            return unit

        def step_with(value, got):
            mine, got = turn(value, got)
            return note(mine + got)

        s2 = swap(total((second, second, high_half), keep_s, s_sib, s1), FAR)
        o_back = swap(total((first, first, low_half, whole), keep_o, o_sib, o1, o2), TP)
        vec = step(vec, CORE_BIT)
        a_unit = rest(a_unit, a_more)
        a_near, a_far = swap(a_unit, NEAR), swap(a_unit, FAR)
        for bit in range(FIRST_REST, bits):
            vec = step(vec, bit)
        s_unit = total((first, first, low_half, whole, whole), keep_s, s_sib, s1, s2, o_back)
        s_more = swap(s_unit, 1 << FIRST_REST)
        vec_tp = swap(vec, TP)
        b2 = swap(total((high_half, high_half, high_half), b_own_lo, b_lo, b1), FAR)
        layer_out, = call(
            layer_out_kernel,
            [(one, BF16)],
            [HB, HB, HB, VM],
            "layer_out",
            gflop=0.01,
            scratch=vmem((one, F32), (one, F32), (one, BF16), sems=3),
        )(mid, out_own, *turn(out_got), vecs)
        note(layer_out)
        a_near, a_far, vec_tp, b2, s_more = due(a_near, a_far, vec_tp, b2, s_more)
        s_unit = rest(s_unit, s_more)
        s_units = share(s_unit)
        b_unit = total((low_half, low_half, low_half, whole), b_own_lo, b_lo, b1, b2)
        b_more = swap(b_unit, 1 << FIRST_REST)
        a_corner = swap(a_far, NEAR)
        vec = note(vec + vec_tp)
        *s_units, a_corner, b_more = due(*s_units, a_corner, b_more)
        b_unit = rest(b_unit, b_more)
        b_units = share(b_unit)
        vec_near = swap(vec, NEAR)
        a_units = [a_unit, a_near, a_far, a_corner]
        a_sib = [swap(value, CORE) for value in turn(*a_units)]
        s_sib = [swap(value, CORE) for value in turn(*s_units)]
        up_grad, qkv_grad, out_grad = call(
            place_two_kernel,
            [((wide, 2 * hidden), F32), ((3, wide, width), F32), ((width, wide), F32)],
            [SM] + [HB] * 16,
            "place_two",
            gflop=0.01,
            scratch=vmem(
                ((8, unit_rows, hidden), BF16), ((8, unit_rows, hidden), F32),
                ((8, 2 * part_rows, 2 * width), BF16), ((8, 2 * part_rows, 2 * width), F32), sems=56,
            ),
            out_specs=[HB] * 3,
            limit=32,
        )(ids, *turn(*a_units, *a_sib, *s_units, *s_sib))
        note(out_grad)
        vec = step_with(vec, vec_near)
        vec_far = swap(vec, FAR)
        *b_three, b_corner = b_units
        b_three = due(*b_three)
        b_sib = [swap(value, CORE) for value in b_three]
        *b_sib, vec_far, b_corner = due(*b_sib, vec_far, b_corner)
        b_sib.append(swap(b_corner, CORE))
        b_units = [*b_three, b_corner]
        vec = vec + vec_far
        down_grad, = call(
            place_down_kernel,
            [((2 * hidden, wide), F32)],
            [SM] + [HB] * 8,
            "place_down",
            scratch=vmem(((8, unit_rows, wide), BF16), ((8, unit_rows, wide), F32), sems=16),
            out_specs=[HB],
            limit=24,
        )(ids, *b_units, *b_sib)
        one_of = lambda i: vec[i]
        qvb = lax.dynamic_slice(vec, (6, half * width), (2, width))
        ub = lax.dynamic_slice(vec, (8 + 2 * half, 0), (2, hidden)).reshape(2 * hidden)
        return (
            layer_out, in_grad, one_of(0), one_of(1), jnp.transpose(qkv_grad, (1, 0, 2)), qvb,
            out_grad, one_of(4), one_of(2), one_of(3), up_grad, ub, down_grad, one_of(5),
        )

    return on_device


def solution(mesh):
    tokens, vector = P(("dp", "tp"), None), P()
    in_specs = (
        tokens, P("dp", None), vector, vector, P(None, None, "tp"), P(None, "tp"), P("tp", None), vector,
        vector, vector, P(None, "tp"), P("tp"), P("tp", None), vector, tokens,
    )
    out_specs = (
        tokens, tokens, vector, vector, P(None, None, "tp"), P(None, "tp"), P("tp", None), vector,
        vector, vector, P(None, "tp"), P("tp"), P("tp", None), vector,
    )
    return jax.shard_map(build(mesh), mesh=mesh, in_specs=in_specs, out_specs=out_specs, check_vma=False)
```

```python
import math

import jax
import jax.numpy as jnp
from jax import lax
from jax.experimental import pallas as pl
from jax.experimental.pallas import tpu as pltpu
from jax.sharding import PartitionSpec as P

HEAD = 64
SEQ = 128
UNITS = 4
EPS = 1e-05
SCALE = 1.0 / math.sqrt(HEAD)
F32 = jnp.float32
BF16 = jnp.bfloat16

VM = pl.BlockSpec(memory_space=pltpu.VMEM)
SM = pl.BlockSpec(memory_space=pltpu.SMEM)
HB = pl.BlockSpec(memory_space=pl.ANY)

NEAR_FIRST, FAR_FIRST = (0, 2, 1, 3), (0, 1, 2, 3)
TP_BIT, CORE_BIT, NEAR_BIT, FAR_BIT, FIRST_REST = 0, 1, 2, 3, 4
TP, CORE, NEAR, FAR = (1 << bit for bit in (TP_BIT, CORE_BIT, NEAR_BIT, FAR_BIT))


def nn(a, b):
    return lax.dot_general(a, b, (((1,), (0,)), ((), ())), preferred_element_type=F32)


def nt(a, b):
    return lax.dot_general(a, b, (((1,), (1,)), ((), ())), preferred_element_type=F32)


def tn(a, b):
    return lax.dot_general(a, b, (((0,), (0,)), ((), ())), preferred_element_type=F32)


def normalize(values):
    center = values - jnp.mean(values, axis=-1, keepdims=True)
    inv = lax.rsqrt(jnp.mean(center * center, axis=-1, keepdims=True) + EPS)
    return center * inv, inv


def norm_back(values, grad, gain):
    normed, inv = normalize(values)
    scaled = grad * gain
    mean_g = jnp.mean(scaled, axis=-1, keepdims=True)
    mean_gn = jnp.mean(scaled * normed, axis=-1, keepdims=True)
    part = inv * (scaled - mean_g - normed * mean_gn)
    gain_sum = jnp.sum(grad * normed, axis=0, keepdims=True)
    shift_sum = jnp.sum(grad, axis=0, keepdims=True)
    return part, gain_sum, shift_sum


def row_mask(lens, row):
    at_k = lax.broadcasted_iota(jnp.int32, (SEQ, 1), 0)
    at_q = lax.broadcasted_iota(jnp.int32, (1, SEQ), 1)
    total = jnp.int32(0)
    seg_q = jnp.zeros((1, SEQ), jnp.int32)
    seg_k = jnp.zeros((SEQ, 1), jnp.int32)
    for entry in range(lens.shape[1]):
        total = total + lens[row, entry]
        seg_q = seg_q + jnp.where(at_q >= total, 1, 0)
        seg_k = seg_k + jnp.where(at_k >= total, 1, 0)
    allowed = (seg_q == seg_k) & (at_k <= at_q) & ((at_k < total) | (at_k == at_q))
    valid = jnp.where(at_k < total, 1.0, 0.0).astype(F32)
    return jnp.concatenate([allowed, allowed], axis=1), valid


def low_lanes():
    return lax.broadcasted_iota(jnp.int32, (SEQ, 2 * HEAD), 1) < HEAD


def stack_pair(pair, low):
    zero = jnp.zeros_like(pair)
    return jnp.concatenate([jnp.where(low, pair, zero), jnp.where(low, zero, pair)], axis=0)


def pair_probs(q_stack, keys, allowed2):
    scores = jnp.where(allowed2, nt(keys, q_stack) * SCALE, -1e30)
    weights = jnp.exp(scores - jnp.max(scores, axis=0, keepdims=True))
    return weights * (1.0 / jnp.sum(weights, axis=0, keepdims=True))


class Copies:
    def __init__(self, sems):
        self.sems = sems
        self.count = 0

    def start(self, src, dst):
        made = pltpu.make_async_copy(src, dst, self.sems.at[self.count])
        self.count += 1
        made.start()
        return made


def wait(*copies):
    for made in copies:
        made.wait()


def blocks(count, size=SEQ):
    return [slice(i * size, (i + 1) * size) for i in range(count)]


def over_rows(tokens, body, start):
    at = lambda i: pl.ds(pl.multiple_of(i * SEQ, SEQ), SEQ)
    return lax.fori_loop(0, tokens // SEQ, lambda i, carry: body(at(i), carry), start)


def project(nrm, w, bias, qkv):
    width = w.shape[2]
    for part in range(3):
        value = nn(nrm[...], w[part])
        if part != 1:
            value = value + bias[part // 2]
        qkv[:, part * width : (part + 1) * width] = value.astype(BF16)


def attend(lens, ids, qkv, att):
    width = att.shape[1]
    rows = att.shape[0] // SEQ
    low = low_lanes()
    @pl.loop(0, rows, unroll=2)
    def _(row):
        at = pl.ds(pl.multiple_of(row * SEQ, SEQ), SEQ)
        allowed2, valid = row_mask(lens, ids[0] * rows + row)
        for first in range(0, width, 2 * HEAD):
            q = qkv[at, first : first + 2 * HEAD]
            k = qkv[at, width + first : width + first + 2 * HEAD]
            v = qkv[at, 2 * width + first : 2 * width + first + 2 * HEAD]
            probs = pair_probs(stack_pair(q, low), k, allowed2)
            both = tn(probs.astype(BF16), v)
            out = jnp.where(low, both[:SEQ], both[SEQ:]) * valid
            att[at, first : first + 2 * HEAD] = out.astype(BF16)


def own_fwd_kernel(lens, ids, x_hbm, vecs, w_hbm, bias, nrm_hbm, qkv_hbm, att, x, w, nrm, qkv, sems):
    copies = Copies(sems)
    x_in = copies.start(x_hbm, x)
    w_in = copies.start(w_hbm, w)
    wait(x_in)

    def norm_rows(at, carry):
        normed, _ = normalize(x[at, :].astype(F32))
        nrm[at, :] = (normed * vecs[0:1, :] + vecs[1:2, :]).astype(BF16)
        return carry

    over_rows(x.shape[0], norm_rows, 0)
    nrm_out = copies.start(nrm, nrm_hbm)
    wait(w_in)
    project(nrm, w, [bias[0:1, :], bias[1:2, :]], qkv)
    qkv_out = copies.start(qkv, qkv_hbm)
    attend(lens, ids, qkv, att)
    wait(nrm_out, qkv_out)


def unit_block(part, rows, width, first=0):
    return pl.ds(first + (part // 2) * rows, rows), pl.ds((part % 2) * width, width)


def fetch_weights(copies, ids, mine_parts, sib_parts, w, wo):
    core, mine = ids[1], ids[2]
    width = w.shape[2]
    part_rows = w.shape[1] // (2 * UNITS)
    to_w, to_wo = [], []
    for side, parts in ((core, mine_parts), (1 - core, sib_parts)):
        for step, unit_ref in enumerate(parts):
            unit = jnp.bitwise_xor(mine, step)
            at_w = pl.ds(pl.multiple_of((side * UNITS + unit) * part_rows, part_rows), part_rows)
            at_o = pl.ds(pl.multiple_of(unit * part_rows, part_rows), part_rows)
            cols = pl.ds(pl.multiple_of(side * width, width), width)
            for part in range(3):
                to_w.append(copies.start(unit_ref.at[unit_block(part, part_rows, width)], w.at[part, at_w, :]))
            if wo is not None:
                to_wo.append(copies.start(unit_ref.at[unit_block(3, part_rows, width)], wo.at[at_o, cols]))
    return to_w, to_wo


def fetch_output_weight(copies, ids, mine_parts, sib_parts, wo):
    core, mine = ids[1], ids[2]
    width = wo.shape[0]
    part_rows = width // UNITS
    made = []
    for side, parts in ((core, mine_parts), (1 - core, sib_parts)):
        for step, unit_ref in enumerate(parts):
            at_o = pl.ds(pl.multiple_of(jnp.bitwise_xor(mine, step) * part_rows, part_rows), part_rows)
            cols = pl.ds(pl.multiple_of(side * width, width), width)
            made.append(copies.start(unit_ref.at[unit_block(3, part_rows, width)], wo.at[at_o, cols]))
    return made


def other_fwd_kernel(lens, ids, x_hbm, nrm_hbm, bias, att_own_hbm, wo_own_hbm, vecs, *refs):
    mine_parts, sib_parts = refs[:4], refs[4:8]
    qkv_hbm, att_hbm, mid_hbm, nm = refs[8:12]
    x, nrm, att_own, wo_own, w, wo, qkv, att, mid, sems = refs[12:]
    copies = Copies(sems)
    nrm_in = copies.start(nrm_hbm, nrm)
    to_w, to_wo = fetch_weights(copies, ids, mine_parts, sib_parts, w, wo)
    late = [copies.start(x_hbm, x), copies.start(att_own_hbm, att_own), copies.start(wo_own_hbm, wo_own)]
    wait(nrm_in, *to_w)
    half = w.shape[2]
    project(nrm, w, [bias[0:1, :half], bias[0:1, half:]], qkv)
    qkv_out = copies.start(qkv, qkv_hbm)
    attend(lens, ids, qkv, att)
    att_out = copies.start(att, att_hbm)
    wait(*to_wo, *late)
    mid[...] = nn(att_own[...], wo_own[...]) + nn(att[...], wo[...])

    def norm_rows(at, carry):
        value = x[at, :].astype(F32) + mid[at, :] + vecs[2:3, :]
        mid[at, :] = value
        normed, _ = normalize(value)
        nm[at, :] = (normed * vecs[3:4, :] + vecs[4:5, :]).astype(BF16)
        return carry

    over_rows(x.shape[0], norm_rows, 0)
    mid_out = copies.start(mid, mid_hbm)
    wait(qkv_out, att_out, mid_out)


def gelu_parts(pre):
    bell = jnp.exp2(pre * pre * (-0.5 * math.log2(math.e)))
    t = 1.0 / (1.0 + (0.3275911 * math.sqrt(0.5)) * jnp.abs(pre))
    poly = 0.5307027145 * t - 0.7265760135
    poly = poly * t + 0.7107068705
    poly = poly * t - 0.142248368
    poly = poly * t + 0.127414796
    tail = poly * t * bell
    cdf = jnp.where(pre >= 0, 1.0 - tail, tail)
    return pre * cdf, cdf + pre * bell * (1.0 / math.sqrt(2.0 * math.pi))


def mlp_kernel(own, *refs):
    ids, nm_a, nm_b, ct_a, ct_b, biases = refs[:6]
    if own:
        up_hbm, down_hbm = refs[6:8]
        out_hbm, dnm_hbm, keep_a, send_a, keep_b, send_b, bias_g = refs[8:15]
        scratch = refs[15:]
    else:
        units, (out_prev, dnm_prev) = refs[6:10], refs[10:12]
        out_own_hbm, out_sib_hbm, dnm_own_hbm, dnm_sib_hbm, keep_a, send_a, keep_b, send_b, bias_g = refs[12:21]
        scratch = refs[21:]
    up, down, nm, ct, pre, dact, act, pg, gu, gd, sems = scratch[:11]
    core, mine = ids[1], ids[2]
    hidden = up.shape[1]
    tokens = nm_a.shape[0]
    unit_rows = up.shape[0] // UNITS
    copies = Copies(sems)
    copy = copies.start
    halves = (pl.ds(0, tokens), pl.ds(tokens, tokens))

    def unit_at(step):
        start = jnp.bitwise_xor(mine, step) * unit_rows
        return pl.ds(pl.multiple_of(start, unit_rows), unit_rows)

    at = pl.ds(pl.multiple_of(core * hidden, hidden), hidden)
    if own:
        ups = [copy(up_hbm.at[:, at], up)]
    else:
        ups = [copy(unit.at[pl.ds(0, unit_rows)], up.at[unit_at(i), :]) for i, unit in enumerate(units)]
    nms = [copy(nm_a, nm.at[halves[0]])]
    if own:
        downs = [copy(down_hbm.at[at, :], down)]
    else:
        downs = [copy(unit.at[pl.ds(unit_rows, unit_rows)], down.at[unit_at(i), :]) for i, unit in enumerate(units)]
    cts = [copy(ct_a, ct.at[halves[0]])]
    nms.append(copy(nm_b, nm.at[halves[1]]))
    cts.append(copy(ct_b, ct.at[halves[1]]))
    if not own:
        prev_out, prev_dnm, dnm_own, dnm_sib, out_own, out_sib = scratch[11:17]
        lates = [copy(dnm_prev, prev_dnm), copy(out_prev, prev_out)]
    else:
        dnm, out = scratch[11:13]

    piece = 32

    def half_step(half, total):
        rows = pl.ds(pl.multiple_of(half * tokens, tokens), tokens)
        for i in range(2):
            pl.when(half == i)(lambda: wait(nms[i], *(ups if i == 0 else ())))
        pre[...] = nn(nm[rows, :], up[...])
        for i in range(2):
            pl.when(half == i)(lambda: wait(cts[i], *(downs if i == 0 else ())))
        dact[...] = nt(ct[rows, :], down[...])

        def elementwise(step, total):
            at = pl.ds(pl.multiple_of(step * piece, piece), piece)
            to = pl.ds(pl.multiple_of(half * tokens + step * piece, piece), piece)
            value, slope = gelu_parts(pre[at, :] + bias)
            act[to, :] = value.astype(BF16)
            back = dact[at, :] * slope
            pg[to, :] = back.astype(BF16)
            return total + jnp.sum(back.reshape(piece // 8, 8, hidden), axis=0)

        return lax.fori_loop(0, tokens // piece, elementwise, total)

    bias = biases[pl.ds((6 if own else 1 + core), 1), :]
    bias_sum = lax.fori_loop(0, 2, half_step, jnp.zeros((8, hidden), F32))
    bias_g[...] = jnp.sum(bias_sum, axis=0, keepdims=True)
    writes = []
    if own:
        dnm[...] = nt(pg[...], up[...]).astype(BF16)
        writes.append(copy(dnm, dnm_hbm))
        out[...] = nn(act[...], down[...]).astype(BF16)
        writes.append(copy(out, out_hbm))
    else:
        wait(*lates)
        total = nt(pg[...], up[...])
        dnm_own[...] = total[:tokens] + prev_dnm[:tokens, :].astype(F32)
        dnm_sib[...] = (total[tokens:] + prev_dnm[tokens:, :].astype(F32)).astype(BF16)
        writes += [copy(dnm_own, dnm_own_hbm), copy(dnm_sib, dnm_sib_hbm)]
        total = nn(act[...], down[...])
        out_own[...] = total[:tokens] + prev_out[:tokens, :].astype(F32)
        out_sib[...] = (total[tokens:] + prev_out[tokens:, :].astype(F32)).astype(BF16)
        writes += [copy(out_own, out_own_hbm), copy(out_sib, out_sib_hbm)]
    for source, grad, order, targets in (
        (gd, lambda: tn(act[...], ct[...]), NEAR_FIRST, (keep_b, send_b)),
        (gu, lambda: tn(nm[...], pg[...]), NEAR_FIRST, (keep_a, send_a)),
    ):
        source[...] = grad().astype(BF16)
        for place, step in enumerate(order):
            to = targets[place // 2].at[pl.ds((place % 2) * unit_rows, unit_rows)]
            writes.append(copy(source.at[unit_at(step), :], to))
    wait(*writes)


def attend_back(lens, ids, qkv, datt, dqkv):
    width = datt.shape[1]
    rows = datt.shape[0] // SEQ
    low = low_lanes()

    @pl.loop(0, rows)
    def _(row):
        allowed2, valid = row_mask(lens, ids[0] * rows + row)
        at = pl.ds(pl.multiple_of(row * SEQ, SEQ), SEQ)
        for first in range(0, width, 2 * HEAD):
            q_cols = slice(first, first + 2 * HEAD)
            k_cols = slice(width + first, width + first + 2 * HEAD)
            v_cols = slice(2 * width + first, 2 * width + first + 2 * HEAD)
            k = qkv[at, k_cols]
            q_stack = stack_pair(qkv[at, q_cols], low)
            grad = (datt[at, q_cols].astype(F32) * valid).astype(BF16)
            g_stack = stack_pair(grad, low)
            probs = pair_probs(q_stack, k, allowed2)
            dqkv[at, v_cols] = nn(probs.astype(BF16), g_stack).astype(BF16)
            prob_grad = nt(qkv[at, v_cols], g_stack)
            inner = jnp.sum(probs * prob_grad, axis=0, keepdims=True)
            score_grad = (probs * (prob_grad - inner)).astype(BF16)
            both = tn(score_grad, k)
            dqkv[at, q_cols] = (jnp.where(low, both[:SEQ], both[SEQ:]) * SCALE).astype(BF16)
            dqkv[at, k_cols] = (nn(score_grad, q_stack) * SCALE).astype(BF16)


def weight_grads(copies, ids, nrm, dqkv, dw, dwo, order, keep, send):
    core, mine = ids[1], ids[2]
    width = dw.shape[2]
    part_rows = dw.shape[1] // (2 * UNITS)
    made = []
    for part in (3, 2, 1, 0):
        if part < 3:
            dw[part] = tn(nrm[...], dqkv[:, part * width : (part + 1) * width]).astype(BF16)
        for place in range(UNITS):
            unit = jnp.bitwise_xor(mine, order[place])
            for side, target in ((1 - core, send), (core, keep)):
                at_w = pl.ds(pl.multiple_of((side * UNITS + unit) * part_rows, part_rows), part_rows)
                at_o = pl.ds(pl.multiple_of(unit * part_rows, part_rows), part_rows)
                cols = pl.ds(pl.multiple_of(side * width, width), width)
                source = dw.at[part, at_w, :] if part < 3 else dwo.at[at_o, cols]
                made.append(copies.start(source, target.at[unit_block(part, part_rows, width, 2 * place * part_rows)]))
    return made


def bias_sums(dqkv):
    width = dqkv.shape[1] // 3
    ones = jnp.ones((8, dqkv.shape[0]), BF16)
    return [nn(ones, dqkv[:, first : first + width])[0:1] for first in (0, 2 * width)]


def normed_grad(dqkv, w):
    width = w.shape[2]
    total = nt(dqkv[:, :width], w[0])
    for part in range(1, 3):
        total = total + nt(dqkv[:, part * width : (part + 1) * width], w[part])
    return total


def other_back_kernel(lens, ids, dnm_own_hbm, dnm_sib_hbm, ct_hbm, mid_hbm, vecs, qkv_hbm, att_hbm, nrm_hbm, *refs):
    mine_parts, sib_parts = refs[:4], refs[4:8]
    mg_hbm, dqkv_hbm, keep, send, sums = refs[8:13]
    dnm_own, dnm_sib, ct, mid, qkv, att, nrm, wo, mg, ml, datt, dqkv, dw, dwo, sems = refs[13:]
    copies = Copies(sems)
    first_in = [
        copies.start(dnm_own_hbm, dnm_own), copies.start(dnm_sib_hbm, dnm_sib),
        copies.start(ct_hbm, ct), copies.start(mid_hbm, mid),
    ]
    to_wo = fetch_output_weight(copies, ids, mine_parts, sib_parts, wo)
    qkv_in, att_in, nrm_in = copies.start(qkv_hbm, qkv), copies.start(att_hbm, att), copies.start(nrm_hbm, nrm)
    wait(*first_in)

    def back_rows(at, totals):
        grad = dnm_own[at, :] + dnm_sib[at, :].astype(F32)
        part, gain_sum, shift_sum = norm_back(mid[at, :], grad, vecs[3:4, :])
        out_grad = ct[at, :].astype(F32)
        value = out_grad + part
        mg[at, :] = value
        ml[at, :] = value.astype(BF16)
        adds = (gain_sum, shift_sum, jnp.sum(value, axis=0, keepdims=True), jnp.sum(out_grad, axis=0, keepdims=True))
        return tuple(total + add for total, add in zip(totals, adds))

    totals = over_rows(mid.shape[0], back_rows, (jnp.zeros((1, mid.shape[1]), F32),) * 4)
    sums[...] = jnp.concatenate(list(totals) + [jnp.zeros((4, mid.shape[1]), F32)])
    mg_out = copies.start(mg, mg_hbm)
    wait(*to_wo, qkv_in, att_in)
    datt[...] = nt(ml[...], wo[...]).astype(BF16)
    dwo[...] = tn(att[...], ml[...]).astype(BF16)
    attend_back(lens, ids, qkv, datt, dqkv)
    wait(nrm_in)
    dqkv_out = copies.start(dqkv, dqkv_hbm)
    outs = weight_grads(copies, ids, nrm, dqkv, dw, dwo, NEAR_FIRST, keep, send)
    wait(mg_out, dqkv_out, *outs)


def own_back_kernel(
    lens, ids, mg_hbm, wo_hbm, qkv_hbm, att_hbm, nrm_hbm, dqkv_hbm, keep, send,
    mg, wo, qkv, att, nrm, ml, datt, dqkv, dw, dwo, sems,
):
    copies = Copies(sems)
    mg_in, wo_in = copies.start(mg_hbm, mg), copies.start(wo_hbm, wo)
    att_in, qkv_in, nrm_in = copies.start(att_hbm, att), copies.start(qkv_hbm, qkv), copies.start(nrm_hbm, nrm)
    wait(mg_in)
    ml[...] = mg[...].astype(BF16)
    wait(wo_in, att_in, qkv_in)
    datt[...] = nt(ml[...], wo[...]).astype(BF16)
    dwo[...] = tn(att[...], ml[...]).astype(BF16)
    attend_back(lens, ids, qkv, datt, dqkv)
    dqkv_out = copies.start(dqkv, dqkv_hbm)
    wait(nrm_in)
    outs = weight_grads(copies, ids, nrm, dqkv, dw, dwo, NEAR_FIRST, keep, send)
    wait(dqkv_out, *outs)


def input_grad_kernel(ids, dqkv_a_hbm, dqkv_b_hbm, mg_hbm, x_hbm, vecs, w_hbm, sums, ub_own, ub_other, *refs):
    mine_parts, sib_parts = refs[:4], refs[4:8]
    in_grad, vec = refs[8:10]
    dqkv_a, dqkv_b, mg, x, w_own, w_other, dn, sems = refs[10:]
    half, core = ids[0], ids[1]
    copies = Copies(sems)
    own_in = [copies.start(dqkv_a_hbm, dqkv_a), copies.start(w_hbm, w_own)]
    other_in, _ = fetch_weights(copies, ids, mine_parts, sib_parts, w_other, None)
    other_in.append(copies.start(dqkv_b_hbm, dqkv_b))
    late = [copies.start(mg_hbm, mg), copies.start(x_hbm, x)]
    width = w_own.shape[2]
    wait(*own_in)
    dn[...] = normed_grad(dqkv_a, w_own)
    wait(*other_in)
    dn[...] += normed_grad(dqkv_b, w_other)
    wait(*late)

    def back_rows(at, totals):
        part, gain_sum, shift_sum = norm_back(x[at, :].astype(F32), dn[at, :], vecs[0:1, :])
        in_grad[at, :] = (mg[at, :] + part).astype(BF16)
        return totals[0] + gain_sum, totals[1] + shift_sum

    totals = over_rows(x.shape[0], back_rows, (jnp.zeros((1, x.shape[1]), F32),) * 2)
    vec[...] = jnp.zeros_like(vec)
    for i in range(2):
        vec[i : i + 1, :] = totals[i]
    vec[2:6, :] = sums[0:4, :]
    for dqkv, side in ((dqkv_a, half), (dqkv_b, 1 - half)):
        for i, value in enumerate(bias_sums(dqkv)):
            vec[6 + i : 7 + i, pl.ds(pl.multiple_of(side * width, width), width)] = value
    vec[pl.ds(8 + 2 * half + core, 1), :] = ub_own[...]
    vec[pl.ds(8 + 2 * (1 - half) + core, 1), :] = ub_other[...]


def layer_out_kernel(mid_hbm, own_hbm, sib_hbm, vecs, out, mid, own, sib, sems):
    copies = Copies(sems)
    wait(copies.start(mid_hbm, mid), copies.start(own_hbm, own), copies.start(sib_hbm, sib))

    def rows(at, carry):
        out[at, :] = (mid[at, :] + own[at, :] + sib[at, :].astype(F32) + vecs[5:6, :]).astype(BF16)
        return carry

    over_rows(out.shape[0], rows, 0)


class Placing:
    def __init__(self, ids, copies):
        self.core, self.mine = ids[1], ids[2]
        self.copies = copies
        self.work, self.outs = [], []

    def take(self, refs, narrow, wide, targets):
        for i, ref in enumerate(refs):
            side = self.core if i < UNITS else 1 - self.core
            unit = jnp.bitwise_xor(self.mine, i % UNITS)
            self.work.append((self.copies.start(ref, narrow.at[i]), narrow, wide, i, targets(side, unit)))

    def finish(self):
        for arrived, narrow, wide, i, targets in self.work:
            arrived.wait()
            wide[i] = narrow[i].astype(F32)
            for block, target in targets:
                self.outs.append(self.copies.start(wide.at[i, block[0], block[1]], target))
        wait(*self.outs)


def mlp_targets(out, down_first, rows, width):
    def targets(side, unit):
        base, start = pl.multiple_of(side * width, width), pl.multiple_of(unit * rows, rows)
        if down_first:
            target = out.at[pl.ds(pl.multiple_of(base + start, rows), rows), :]
        else:
            target = out.at[pl.ds(start, rows), pl.ds(base, width)]
        return [((pl.ds(0, rows), pl.ds(0, width)), target)]

    return targets


def attn_targets(w, wo):
    width = w.shape[2]
    rows = w.shape[1] // (2 * UNITS)

    def targets(side, unit):
        at_w = pl.ds(pl.multiple_of((side * UNITS + unit) * rows, rows), rows)
        at_o = pl.ds(pl.multiple_of(unit * rows, rows), rows)
        cols = pl.ds(pl.multiple_of(side * width, width), width)
        places = [w.at[part, at_w, :] for part in range(3)] + [wo.at[at_o, cols]]
        return [(unit_block(part, rows, width), place) for part, place in enumerate(places)]

    return targets


def place_mlp_kernel(down_first, ids, *refs):
    units, (out, narrow, wide, sems) = refs[:8], refs[8:]
    placing = Placing(ids, Copies(sems))
    placing.take(units, narrow, wide, mlp_targets(out, down_first, *units[0].shape))
    placing.finish()


def place_down_kernel(*refs):
    place_mlp_kernel(True, *refs)


def place_two_kernel(ids, *refs):
    up_units, attn_units = refs[:8], refs[8:16]
    up, w, wo, narrow_u, wide_u, narrow_a, wide_a, sems = refs[16:]
    placing = Placing(ids, Copies(sems))
    placing.take(up_units, narrow_u, wide_u, mlp_targets(up, False, *up_units[0].shape))
    placing.take(attn_units, narrow_a, wide_a, attn_targets(w, wo))
    placing.finish()


def vmem(*buffers, sems):
    return [pltpu.VMEM(shape, dtype) for shape, dtype in buffers] + [pltpu.SemaphoreType.DMA((sems,))]


def call(kernel, outs, in_specs, name, scratch=(), out_specs=None, limit=61, gflop=1.0):
    return pl.pallas_call(
        kernel,
        out_shape=tuple(jax.ShapeDtypeStruct(shape, dtype) for shape, dtype in outs),
        in_specs=in_specs,
        out_specs=tuple(VM for _ in outs) if out_specs is None else tuple(out_specs),
        scratch_shapes=list(scratch),
        name=name,
        cost_estimate=pl.CostEstimate(flops=int(gflop * 1e9), bytes_accessed=8 << 20, transcendentals=0),
        compiler_params=pltpu.CompilerParams(vmem_limit_bytes=limit * 1024 * 1024),
    )


def build(mesh):
    devices = mesh.shape["dp"] * mesh.shape["tp"]
    bits = devices.bit_length() - 1

    def swap(value, mask):
        return lax.ppermute(value, ("dp", "tp"), [(i, i ^ mask) for i in range(devices)])

    def after(value, *deps):
        return lax.optimization_barrier((value, deps))[0]

    def share(unit):
        return [unit] + [swap(unit, mask) for mask in (NEAR, FAR, NEAR | FAR)]

    def add(*terms):
        total = terms[0].astype(F32)
        for term in terms[1:]:
            total = total + term.astype(F32)
        return total

    last = []

    def turn(*values):
        return lax.optimization_barrier((values, last[-1]))[0]

    def note(value):
        last.append(value)
        return value

    def due(*values):
        values = turn(*values)
        note(values[-1])
        return values

    def total(parts, *terms):
        cut = lambda v, part: v if part is None else v[v.shape[0] * part[0] // 4 : v.shape[0] * part[1] // 4]
        return note(add(*[cut(term, part) for term, part in zip(turn(*terms), parts)]).astype(BF16))

    def on_device(
        layer_in, lengths, attn_gain, attn_shift, qkv_weight, qv_bias, out_weight, out_bias,
        mlp_gain, mlp_shift, up_weight, up_bias, down_weight, down_bias, cotangent,
    ):
        tokens, wide = layer_in.shape
        width = qkv_weight.shape[2]
        hidden = up_weight.shape[1] // 2
        flat = lax.axis_index("dp") * 2 + lax.axis_index("tp")
        half = lax.axis_index("tp")
        core = (flat >> CORE_BIT) & 1
        mine = ((flat >> FAR_BIT) & 1) * 2 + ((flat >> NEAR_BIT) & 1)
        ids = jnp.stack([half, core, mine]).astype(jnp.int32)
        up_bias_own = lax.dynamic_slice(up_bias, (core * hidden,), (hidden,))
        vecs = jnp.stack([attn_gain, attn_shift, out_bias, mlp_gain, mlp_shift, down_bias, up_bias_own, up_bias_own])
        w_own = jnp.transpose(qkv_weight, (1, 0, 2))

        part_rows = wide // (2 * UNITS)
        unit_w = lax.dynamic_slice(w_own, (0, (core * UNITS + mine) * part_rows, 0), (3, part_rows, width))
        unit_o = lax.dynamic_slice(out_weight, (mine * part_rows, core * width), (part_rows, width))
        attn_unit = jnp.concatenate(
            [jnp.concatenate([unit_w[0], unit_w[1]], axis=1), jnp.concatenate([unit_w[2], unit_o], axis=1)]
        )
        attn_unit = swap(attn_unit, TP)

        acts = (tokens, 3 * width)
        one = (tokens, wide)
        head = (tokens, width)
        w_shape, wo_shape = (3, wide, width), (width, wide)
        nrm, qkv_own, att_own = call(
            own_fwd_kernel,
            [(one, BF16), (acts, BF16), (head, BF16)],
            [SM, SM, HB, VM, HB, VM],
            "attn_own_fwd",
            gflop=0.5,
            scratch=vmem((one, BF16), (w_shape, BF16), (one, BF16), (acts, BF16), sems=4),
            out_specs=[HB, HB, VM],
        )(lengths, ids, layer_in, vecs, w_own, qv_bias)
        attn_parts = share(after(attn_unit, att_own))
        unit_rows = hidden // UNITS
        up_late, down_late, bias_late, up_bias_late = after((up_weight, down_weight, qv_bias, up_bias), att_own)
        mlp_unit = jnp.concatenate(
            [
                lax.dynamic_slice(up_late, (mine * unit_rows, core * hidden), (unit_rows, hidden)),
                lax.dynamic_slice(down_late, (core * hidden + mine * unit_rows, 0), (unit_rows, wide)),
            ]
        )
        mlp_unit = swap(mlp_unit, TP)
        small = jnp.concatenate([bias_late.reshape(-1), up_bias_late])
        small_other = swap(small.reshape(3, wide), TP)
        ct_sib = swap(cotangent, CORE)
        attn_sib = [swap(part, CORE) for part in attn_parts]
        qkv_other, att_other, mid, nm = call(
            other_fwd_kernel,
            [(acts, BF16), (head, BF16), (one, F32), (one, BF16)],
            [SM, SM, HB, HB, VM, HB, HB, VM] + [HB] * 8,
            "attn_other_fwd",
            gflop=6,
            scratch=vmem(
                (one, BF16), (one, BF16), (head, BF16), (wo_shape, BF16), (w_shape, BF16), (wo_shape, BF16),
                (acts, BF16), (head, BF16), (one, F32), sems=40,
            ),
            out_specs=[HB, HB, HB, VM],
        )(
            lengths, ids, layer_in, after(nrm, mlp_unit), small_other, att_own, out_weight, vecs,
            *attn_parts, *attn_sib,
        )
        mlp_near, mlp_far = swap(mlp_unit, NEAR), swap(mlp_unit, FAR)

        mlp_near, mlp_far, nm = after((mlp_near, mlp_far, nm))
        mlp_parts = [mlp_unit, mlp_near, mlp_far, swap(mlp_unit, NEAR | FAR)]
        nm_sib = swap(nm, CORE)
        tall, square = (2 * tokens, wide), (wide, hidden)
        scratch = [
            (square, BF16), (square, BF16), (tall, BF16), (tall, BF16), ((tokens, hidden), F32), ((tokens, hidden), F32),
            ((2 * tokens, hidden), BF16), ((2 * tokens, hidden), BF16), (square, BF16), (square, BF16),
        ]

        def mlp_scratch(*more):
            buffers = vmem(*scratch, *more, sems=40)
            return buffers[:10] + buffers[-1:] + buffers[10:-1]

        both = (2 * tokens, wide)
        pair = (2 * unit_rows, hidden)
        out_a, dnm_a, keep_own, send_own, b_own_lo, b_own_hi, ub_own = call(
            lambda *r: mlp_kernel(True, *r),
            [(both, BF16), (both, BF16), *[(pair, BF16)] * 4, ((1, hidden), F32)],
            [SM] + [HB] * 4 + [VM] + [HB] * 2,
            "mlp_own",
            gflop=1,
            scratch=mlp_scratch((tall, BF16), (tall, BF16)),
            out_specs=[HB] * 6 + [VM],
        )(ids, nm, nm_sib, cotangent, ct_sib, vecs, up_weight, down_weight)
        out_own, out_sib, dnm_own, dnm_sib, keep_other, send_other, b_other_lo, b_other_hi, ub_other = call(
            lambda *r: mlp_kernel(False, *r),
            [
                (one, F32), (one, BF16), (one, F32), (one, BF16), *[(pair, BF16)] * 4,
                ((1, hidden), F32),
            ],
            [SM] + [HB] * 4 + [VM] + [HB] * 6,
            "mlp_other",
            gflop=12,
            scratch=mlp_scratch((tall, BF16), (tall, BF16), (one, F32), (one, BF16), (one, F32), (one, BF16)),
            out_specs=[HB] * 8 + [VM],
        )(ids, nm, nm_sib, cotangent, ct_sib, small_other, *mlp_parts, out_a, dnm_a)
        grad_units = (2 * UNITS * part_rows, 2 * width)
        whole, low_half, high_half, first, second = None, (0, 2), (2, 4), (0, 1), (1, 2)
        a_own = swap(send_own, NEAR)
        note(ub_other)
        a_own, dnm_sib, out_sib, send_other, b_other_hi, b_other_lo = turn(
            a_own, dnm_sib, out_sib, send_other, b_other_hi, b_other_lo
        )
        dnm_got = swap(dnm_sib, CORE)
        a_own2 = swap(total((high_half, high_half), keep_own, a_own), FAR)
        a_other = swap(send_other, NEAR)
        b_hi = swap(b_other_hi, TP)
        mg, dqkv_other, keep_o, send_o, sums_mid = call(
            other_back_kernel,
            [(one, F32), (acts, BF16), (grad_units, BF16), (grad_units, BF16), ((8, wide), F32)],
            [SM, SM, HB, HB, HB, HB, VM, HB, HB, HB] + [HB] * 8,
            "attn_other_back",
            gflop=10,
            scratch=vmem(
                (one, F32), (one, BF16), (one, BF16), (one, F32), (acts, BF16), (head, BF16), (one, BF16),
                (wo_shape, BF16), (one, F32), (one, BF16), (head, BF16), (acts, BF16),
                (w_shape, BF16), (wo_shape, BF16), sems=60,
            ),
            out_specs=[HB] * 4 + [VM],
        )(
            lengths, ids, dnm_own, dnm_got, cotangent, mid, vecs, qkv_other, att_other, nrm,
            *attn_parts, *attn_sib,
        )
        note(sums_mid)
        out_got = swap(turn(out_sib)[0], CORE)
        a_other, a_own2, b_hi, send_o = turn(a_other, a_own2, b_hi, send_o)
        o_sib = swap(send_o, CORE)
        a_other2 = swap(total((high_half, high_half), keep_other, a_other), FAR)
        o1 = swap(total((high_half, high_half), keep_o, o_sib), NEAR)
        b_lo = swap(b_other_lo, TP)
        mg_now, = turn(mg)
        dqkv_own, keep_s, send_s = call(
            own_back_kernel,
            [(acts, BF16), (grad_units, BF16), (grad_units, BF16)],
            [SM, SM] + [HB] * 5,
            "attn_own_back",
            gflop=10,
            scratch=vmem(
                (one, F32), (wo_shape, BF16), (acts, BF16), (head, BF16), (one, BF16),
                (one, BF16), (head, BF16), (acts, BF16), (w_shape, BF16), (wo_shape, BF16), sems=48,
            ),
            out_specs=[HB] * 3,
        )(lengths, ids, mg_now, out_weight, qkv_own, att_own, nrm)
        note(dqkv_own)
        a_other2, o1, b_lo, send_s = turn(a_other2, o1, b_lo, send_s)
        s_sib = swap(send_s, CORE)
        a_back = swap(total((low_half, low_half, whole), keep_other, a_other, a_other2), TP)
        s1 = swap(total((high_half, high_half), keep_s, s_sib), NEAR)
        o2 = swap(total((second, second, high_half), keep_o, o_sib, o1), FAR)
        b1 = swap(total((whole, whole), b_own_hi, b_hi), NEAR)
        a_unit = total((low_half, low_half, whole, whole), keep_own, a_own, a_own2, a_back)
        a_more = swap(a_unit, 1 << FIRST_REST)
        in_grad, vec = call(
            input_grad_kernel,
            [(one, BF16), ((16, wide), F32)],
            [SM, HB, HB, HB, HB, VM, HB, VM, VM, VM] + [HB] * 8,
            "input_grad",
            gflop=0.01,
            scratch=vmem(
                (acts, BF16), (acts, BF16), (one, F32), (one, BF16), (w_shape, BF16), (w_shape, BF16), (one, F32),
                sems=32,
            ),
        )(
            ids, dqkv_own, dqkv_other, *turn(mg), layer_in, vecs, w_own, sums_mid, ub_own, ub_other,
            *attn_parts, *attn_sib,
        )
        note(vec)

        def step(value, bit):
            mine, got = turn(value, swap(value, 1 << bit))
            return note(mine + got)

        def rest(unit, got):
            unit = total((whole, whole), unit, got)
            for bit in range(FIRST_REST + 1, bits):
                unit = total((whole, whole), unit, swap(unit, 1 << bit))
            return unit

        def step_with(value, got):
            mine, got = turn(value, got)
            return note(mine + got)

        s2 = swap(total((second, second, high_half), keep_s, s_sib, s1), FAR)
        o_back = swap(total((first, first, low_half, whole), keep_o, o_sib, o1, o2), TP)
        vec = step(vec, CORE_BIT)
        for bit in range(FIRST_REST, bits):
            vec = step(vec, bit)
        a_unit = rest(a_unit, a_more)
        a_near, a_far = swap(a_unit, NEAR), swap(a_unit, FAR)
        s_unit = total((first, first, low_half, whole, whole), keep_s, s_sib, s1, s2, o_back)
        s_more = swap(s_unit, 1 << FIRST_REST)
        vec_tp = swap(vec, TP)
        b2 = swap(total((high_half, high_half, high_half), b_own_lo, b_lo, b1), FAR)
        layer_out, = call(
            layer_out_kernel,
            [(one, BF16)],
            [HB, HB, HB, VM],
            "layer_out",
            gflop=0.01,
            scratch=vmem((one, F32), (one, F32), (one, BF16), sems=3),
        )(mid, out_own, *turn(out_got), vecs)
        note(layer_out)
        a_near, a_far, vec_tp, b2, s_more = due(a_near, a_far, vec_tp, b2, s_more)
        s_unit = rest(s_unit, s_more)
        s_units = share(s_unit)
        b_unit = total((low_half, low_half, low_half, whole), b_own_lo, b_lo, b1, b2)
        b_more = swap(b_unit, 1 << FIRST_REST)
        a_corner = swap(a_far, NEAR)
        vec = note(vec + vec_tp)
        *s_units, a_corner, b_more = due(*s_units, a_corner, b_more)
        b_unit = rest(b_unit, b_more)
        b_units = share(b_unit)
        vec_near = swap(vec, NEAR)
        a_units = [a_unit, a_near, a_far, a_corner]
        a_sib = [swap(value, CORE) for value in turn(*a_units)]
        s_sib = [swap(value, CORE) for value in turn(*s_units)]
        up_grad, qkv_grad, out_grad = call(
            place_two_kernel,
            [((wide, 2 * hidden), F32), ((3, wide, width), F32), ((width, wide), F32)],
            [SM] + [HB] * 16,
            "place_two",
            gflop=0.01,
            scratch=vmem(
                ((8, unit_rows, hidden), BF16), ((8, unit_rows, hidden), F32),
                ((8, 2 * part_rows, 2 * width), BF16), ((8, 2 * part_rows, 2 * width), F32), sems=56,
            ),
            out_specs=[HB] * 3,
            limit=32,
        )(ids, *turn(*a_units, *a_sib, *s_units, *s_sib))
        note(out_grad)
        vec = step_with(vec, vec_near)
        vec_far = swap(vec, FAR)
        *b_three, b_corner = b_units
        b_three = due(*b_three)
        b_sib = [swap(value, CORE) for value in b_three]
        *b_sib, vec_far, b_corner = due(*b_sib, vec_far, b_corner)
        b_sib.append(swap(b_corner, CORE))
        b_units = [*b_three, b_corner]
        vec = vec + vec_far
        down_grad, = call(
            place_down_kernel,
            [((2 * hidden, wide), F32)],
            [SM] + [HB] * 8,
            "place_down",
            scratch=vmem(((8, unit_rows, wide), BF16), ((8, unit_rows, wide), F32), sems=16),
            out_specs=[HB],
            limit=24,
        )(ids, *b_units, *b_sib)
        one_of = lambda i: vec[i]
        qvb = lax.dynamic_slice(vec, (6, half * width), (2, width))
        ub = lax.dynamic_slice(vec, (8 + 2 * half, 0), (2, hidden)).reshape(2 * hidden)
        return (
            layer_out, in_grad, one_of(0), one_of(1), jnp.transpose(qkv_grad, (1, 0, 2)), qvb,
            out_grad, one_of(4), one_of(2), one_of(3), up_grad, ub, down_grad, one_of(5),
        )

    return on_device


def solution(mesh):
    tokens, vector = P(("dp", "tp"), None), P()
    in_specs = (
        tokens, P("dp", None), vector, vector, P(None, None, "tp"), P(None, "tp"), P("tp", None), vector,
        vector, vector, P(None, "tp"), P("tp"), P("tp", None), vector, tokens,
    )
    out_specs = (
        tokens, tokens, vector, vector, P(None, None, "tp"), P(None, "tp"), P("tp", None), vector,
        vector, vector, P(None, "tp"), P("tp"), P("tp", None), vector,
    )
    return jax.shard_map(build(mesh), mesh=mesh, in_specs=in_specs, out_specs=out_specs, check_vma=False)
```
